512 devices in a mesh: gx: 4 (over x), gy: 128 (over z, y, core).
Axes of the slice: x: 4, y: 8, z: 8, core: 2. Of those that a mesh axis runs over, the one named last changes fastest.
Arguments:
- velocity: float32 [3, 1536, 32, 512], P(None, 'gy', None, 'gx'), may hold values from -6 to 6
- old_advection: float32 [3, 1536, 32, 512], P(None, 'gy', None, 'gx'), may hold values from -12 to 12
- lower_gap: float32 [1536], P('gy'), may hold values from 0.35 to 1.4
- upper_gap: float32 [1536], P('gy'), may hold values from 0.35 to 1.4, as said below
Outputs:
- new_velocity: float32 [3, 1536, 32, 512], P(None, 'gy', None, 'gx')
- advection: float32 [3, 1536, 32, 512], P(None, 'gy', None, 'gx')
The draws below stay inside these ranges and needn't reach their ends.
Inputs may be any that keep to these rules, and one draw needn't show every extreme that they name: upper_gap of every point equals lower_gap of the next point.
All inputs are finite; a program needn't handle non-finite values.
Results may differ from the reference program's by a relative error of at most 0.0075.
Values sent between devices are 32-bit elements; how exact they have to be, the bound alone decides.
A program may use at most 128 MiB of HBM per device.

```python
import jax
import jax.numpy as jnp
from jax import lax

NY = 1536
NZ = 32
NX = 512
STIFF = 1024


def gap_table(key):
    sub_key = jax.random.fold_in(key, 7)
    points = NY + 1
    position = jnp.arange(points, dtype=jnp.float32)
    profile = jnp.sin(jnp.pi * (position + 0.5) / points)
    roughness = jnp.exp(jax.random.uniform(sub_key, (points,), jnp.float32, jnp.log(0.7), jnp.log(1.4)))
    return (0.5 * jnp.exp(profile * jnp.log(2.0)) * roughness).astype(jnp.float32)


def draw_lower_gap(key, part):
    return gap_table(key)[:NY]


def draw_upper_gap(key, part):
    return gap_table(key)[1:]


def draw_velocity(key, part):
    shape = (3, NY, NZ, NX)
    values = jnp.clip(jax.random.normal(key, shape, jnp.float32), -6.0, 6.0)
    return values.astype(jnp.float32)


def steps_of(key, dims, cuts, least, high):
    def one(dim, blocks):
        draws = jax.random.uniform(jax.random.fold_in(jax.random.fold_in(key, 6), dim), (blocks,), jnp.float32, least / len(cuts), high / len(cuts))
        return jnp.repeat(jnp.exp(draws), dims[dim] // blocks).reshape((-1,) + (1,) * (len(dims) - dim - 1))

    gain = one(*cuts[0])
    for cut in cuts[1:]:
        gain = gain * one(*cut)
    return gain


def noise(key, shape, deviation, bound, cuts=(), kind=jnp.bfloat16):
    loudness = steps_of(key, shape, cuts, -0.22, 0.18) if cuts else 1.0
    result = jax.random.normal(key, shape, jnp.float32) * deviation * loudness
    return jnp.minimum(jnp.maximum(result, -bound), bound).astype(kind)


def setup_inputs(seed: int = 0) -> dict:
    splits = jax.random.split(jax.random.key(seed), 5)
    return {
        "velocity": draw_velocity(jax.random.fold_in(splits[4], 71), 0),
        "old_advection": noise(splits[1], (3, NY, NZ, NX), 2.0, 12.0, ((1, 128), (3, 4)), jnp.float32),
        "lower_gap": draw_lower_gap(jax.random.fold_in(splits[4], 71), 0),
        "upper_gap": draw_upper_gap(jax.random.fold_in(splits[4], 71), 0),
    }


STENCIL = (0.8, -0.2, 4.0 / 105.0, -1.0 / 280.0)
GAMMA = 5.0 / 12.0
ZETA = -17.0 / 60.0

def roll_slope(values, along_axis):
    summed = STENCIL[0] * (jnp.roll(values, -1, along_axis) - jnp.roll(values, 1, along_axis))
    for offset in range(2, 5):
        summed = summed + STENCIL[offset - 1] * (jnp.roll(values, -offset, along_axis) - jnp.roll(values, offset, along_axis))
    return summed

def reference(velocity, old_advection, lower_gap, upper_gap):
    gap_sum = lower_gap + upper_gap

    def advect(component):
        stream = roll_slope(component, 2)
        spanwise = roll_slope(component, 1)
        padded = jnp.pad(component, ((1, 1), (0, 0), (0, 0)))
        normal_slope = (padded[2:] - padded[:-2]) / gap_sum[:, None, None]
        return -(velocity[0] * stream + velocity[1] * normal_slope + velocity[2] * spanwise)
    advection = lax.map(advect, velocity)
    forcing = velocity + GAMMA * advection + ZETA * old_advection
    lower_coef = -2.0 * STIFF / (gap_sum * lower_gap)
    upper_coef = -2.0 * STIFF / (gap_sum * upper_gap)
    diagonal = 1.0 - lower_coef - upper_coef
    below_band = lower_coef.at[0].set(0.0)
    above_band = upper_coef.at[-1].set(0.0)
    stacked = forcing.reshape(3, NY, -1)
    solved = lax.linalg.tridiagonal_solve(jnp.stack([below_band] * 3), jnp.stack([diagonal] * 3), jnp.stack([above_band] * 3), stacked)
    new_velocity = solved.reshape(forcing.shape)
    return (new_velocity, advection)
```

```python
import jax
import jax.numpy as jnp
from jax import lax
from jax.sharding import PartitionSpec as P

STIFF = 1024


STENCIL = (0.8, -0.2, 4.0 / 105.0, -1.0 / 280.0)
GAMMA = 5.0 / 12.0
ZETA = -17.0 / 60.0


def extended(array, sides, width, wrap):
    for axis, dim in sides:
        size, length = (lax.axis_size(axis), array.shape[dim])
        up = [(i, (i + 1) % size) for i in range(size if wrap else size - 1)]
        down = [(j, i) for i, j in up]
        last = lax.slice_in_dim(array, length - width, length, axis=dim)
        first = lax.slice_in_dim(array, 0, width, axis=dim)
        before = lax.ppermute(last, axis, up)
        after = lax.ppermute(first, axis, down)
        array = jnp.concatenate([before, array, after], axis=dim)
    return array


def prefix(value, axis, join, neutral, backward):
    count, mine = (lax.axis_size(axis), lax.axis_index(axis))
    step = -1 if backward else 1
    order = [(i, i + step) for i in range(count) if 0 <= i + step < count]
    total = jax.tree.map(lambda part: lax.ppermute(part, axis, order), value)
    inside = (mine >= 1) if not backward else (mine <= count - 2)
    total = jax.tree.map(
        lambda part, zero: jnp.where(inside, part, jnp.full_like(part, 0) + jnp.asarray(zero, part.dtype)),
        total,
        neutral,
    )
    offset = 1
    while offset < count:
        pairs = [(i, i + step * offset) for i in range(count) if 0 <= i + step * offset < count]
        earlier = jax.tree.map(lambda part: lax.ppermute(part, axis, pairs), total)
        longer = join(earlier, total)
        reach = (mine >= offset) if not backward else (mine <= count - 1 - offset)
        total = jax.tree.map(lambda new, old: jnp.where(reach, new, old), longer, total)
        offset *= 2
    return total


def stream_slope(padded, planes):
    summed = STENCIL[0] * (padded[..., 5 : 5 + planes] - padded[..., 3 : 3 + planes])
    for offset in range(2, 5):
        summed = summed + STENCIL[offset - 1] * (
            padded[..., 4 + offset : 4 + offset + planes]
            - padded[..., 4 - offset : 4 - offset + planes]
        )
    return summed


def roll_slope(values, along_axis):
    summed = STENCIL[0] * (jnp.roll(values, -1, along_axis) - jnp.roll(values, 1, along_axis))
    for offset in range(2, 5):
        summed = summed + STENCIL[offset - 1] * (
            jnp.roll(values, -offset, along_axis) - jnp.roll(values, offset, along_axis)
        )
    return summed


def compose(earlier, latter):
    return (latter[0] * earlier[0], latter[1] + latter[0] * earlier[1])


def chain_ratio(earlier, latter):
    product = jnp.dot(latter, earlier, precision=lax.Precision.HIGHEST)
    return product / jnp.max(jnp.abs(product))


def ratio_matrix(cross_term, top_right, bottom_left):
    unit_entry = jnp.ones((), jnp.float32)
    return jnp.stack([jnp.stack([cross_term, top_right]), jnp.stack([bottom_left, unit_entry])])


def shards(velocity, old_advection, lower_gap, upper_gap):
    planes = velocity.shape[3]
    padded = extended(velocity, (("gx", 3),), 4, True)
    stream = stream_slope(padded, planes)
    spanwise = roll_slope(velocity, 2)
    rimmed = extended(velocity, (("gy", 1),), 1, False)
    gap_sum = lower_gap + upper_gap
    normal_slope = (rimmed[:, 2:] - rimmed[:, :-2]) / gap_sum[None, :, None, None]
    advection = -(
        velocity[0][None] * stream + velocity[1][None] * normal_slope + velocity[2][None] * spanwise
    )
    forcing = velocity + GAMMA * advection + ZETA * old_advection
    lower_coef = -2.0 * STIFF / (gap_sum * lower_gap)
    upper_coef = -2.0 * STIFF / (gap_sum * upper_gap)
    diagonal = 1.0 - lower_coef - upper_coef
    below_band = lower_coef.at[0].set(0.0)
    above_band = upper_coef.at[-1].set(0.0)
    rows_here = velocity.shape[1]
    line_values = forcing.reshape(3, rows_here, -1)
    solved = lax.linalg.tridiagonal_solve(
        jnp.stack([below_band] * 3),
        jnp.stack([diagonal] * 3),
        jnp.stack([above_band] * 3),
        line_values,
    )
    columns = jnp.zeros((rows_here, 2), jnp.float32)
    columns = columns.at[0, 0].set(lower_coef[0]).at[rows_here - 1, 1].set(upper_coef[-1])
    spikes = lax.linalg.tridiagonal_solve(below_band, diagonal, above_band, columns)
    left_spike = spikes[:, 0]
    right_spike = spikes[:, 1]
    left_first = left_spike[0]
    left_last = left_spike[-1]
    right_first = right_spike[0]
    right_last = right_spike[-1]
    cross_term = left_last * right_first - right_last * left_first
    unit_matrix = jnp.eye(2, dtype=jnp.float32)
    below_prefix = prefix(
        ratio_matrix(cross_term, right_last, -left_first), "gy", chain_ratio, unit_matrix, False
    )
    below_ratio = below_prefix[0, 1] / below_prefix[1, 1]
    first_solved = solved[:, 0]
    last_solved = solved[:, -1]
    lower_denom = 1.0 - left_first * below_ratio
    lower_step = (
        jnp.reshape(-left_last / lower_denom, (1, 1)),
        last_solved + left_last * below_ratio / lower_denom * first_solved,
    )
    identity_step = (jnp.ones((1, 1), jnp.float32), jnp.zeros_like(first_solved))
    below_offset = prefix(lower_step, "gy", compose, identity_step, False)[1]
    first_base = (first_solved - left_first * below_offset) / lower_denom
    first_slope = right_first / lower_denom
    upper_step = (jnp.reshape(-first_slope, (1, 1)), first_base)
    above_value = prefix(upper_step, "gy", compose, identity_step, True)[1]
    first_value = first_base - first_slope * above_value
    below_value = below_offset - below_ratio * first_value
    finished = (
        solved
        - below_value[:, None, :] * left_spike[None, :, None]
        - above_value[:, None, :] * right_spike[None, :, None]
    )
    return (finished.reshape(velocity.shape), advection)


def solution(mesh):
    return jax.shard_map(
        shards,
        mesh=mesh,
        in_specs=(P(None, "gy", None, "gx"), P(None, "gy", None, "gx"), P("gy"), P("gy")),
        out_specs=(P(None, "gy", None, "gx"), P(None, "gy", None, "gx")),
        check_vma=False,
    )
```

```python
import functools

import jax
import jax.numpy as jnp
from jax import lax
from jax.sharding import PartitionSpec as P
from jax.experimental import pallas as pl
from jax.experimental.pallas import tpu as pltpu

MESH = pl.DeviceIdType.MESH
LINES = 96

STIFF = 1024


STENCIL = (0.8, -0.2, 4.0 / 105.0, -1.0 / 280.0)
GAMMA = 5.0 / 12.0
ZETA = -17.0 / 60.0


def extended(array, sides, width, wrap):
    for axis, dim in sides:
        size, length = (lax.axis_size(axis), array.shape[dim])
        up = [(i, (i + 1) % size) for i in range(size if wrap else size - 1)]
        down = [(j, i) for i, j in up]
        last = lax.slice_in_dim(array, length - width, length, axis=dim)
        first = lax.slice_in_dim(array, 0, width, axis=dim)
        before = lax.ppermute(last, axis, up)
        after = lax.ppermute(first, axis, down)
        array = jnp.concatenate([before, array, after], axis=dim)
    return array


def prefix(value, axis, join, neutral, backward):
    count, mine = (lax.axis_size(axis), lax.axis_index(axis))
    step = -1 if backward else 1
    order = [(i, i + step) for i in range(count) if 0 <= i + step < count]
    total = jax.tree.map(lambda part: lax.ppermute(part, axis, order), value)
    inside = (mine >= 1) if not backward else (mine <= count - 2)
    total = jax.tree.map(
        lambda part, zero: jnp.where(inside, part, jnp.full_like(part, 0) + jnp.asarray(zero, part.dtype)),
        total,
        neutral,
    )
    offset = 1
    while offset < count:
        pairs = [(i, i + step * offset) for i in range(count) if 0 <= i + step * offset < count]
        earlier = jax.tree.map(lambda part: lax.ppermute(part, axis, pairs), total)
        longer = join(earlier, total)
        reach = (mine >= offset) if not backward else (mine <= count - 1 - offset)
        total = jax.tree.map(lambda new, old: jnp.where(reach, new, old), longer, total)
        offset *= 2
    return total


def scan_kernel(count, backward, x_ref, out_ref, totals, recv, send_sem, recv_sem):
    me = lax.axis_index("gy")
    row = lax.axis_index("gx")
    sign = -1 if backward else 1
    offsets = [1]
    while offsets[-1] * 2 < count:
        offsets.append(offsets[-1] * 2)
    partners = []
    for offset in offsets:
        partners.append((me + offset) % count)
        if 2 * offset != count:
            partners.append((me + count - offset) % count)
    barrier = pltpu.get_barrier_semaphore()
    for partner in partners:
        pl.semaphore_signal(barrier, inc=1, device_id=(row, partner), device_id_type=MESH)
    pl.semaphore_wait(barrier, len(partners))
    rounds = [1] + offsets
    copies = []
    for step, offset in enumerate(rounds):
        source = x_ref if step == 0 else totals.at[step - 1]
        target = (me + count + sign * offset) % count
        copy = pltpu.make_async_remote_copy(
            src_ref=source,
            dst_ref=recv.at[step],
            send_sem=send_sem.at[step],
            recv_sem=recv_sem.at[step],
            device_id=(row, target),
            device_id_type=MESH,
        )
        copy.start()
        copy.wait_recv()
        copies.append(copy)
        valid = (me + offset <= count - 1) if backward else (me >= offset)
        earlier = recv[step]
        if step == 0:
            lines = jnp.zeros((LINES, 128), jnp.float32)
            scale = jnp.ones((8, 128), jnp.float32)
            neutral = jnp.concatenate([lines, scale], axis=0)
            totals[step] = jnp.where(valid, earlier, neutral)
        else:
            latter = totals[step - 1]
            factor = latter[LINES : LINES + 1, :]
            joined_lines = latter[:LINES] + factor * earlier[:LINES]
            joined_scale = latter[LINES:] * earlier[LINES:]
            joined = jnp.concatenate([joined_lines, joined_scale], axis=0)
            totals[step] = jnp.where(valid, joined, latter)
    out_ref[...] = totals[len(rounds) - 1]
    for copy in copies:
        copy.wait_send()


def line_scan(step_value, backward):
    count = lax.axis_size("gy")
    factor, lines = step_value
    shape = lines.shape
    packed = jnp.concatenate(
        [lines.reshape(LINES, 128), jnp.broadcast_to(factor.reshape(1, 1), (8, 128))], axis=0
    )
    rounds = 1
    while (1 << (rounds - 1)) * 2 < count:
        rounds += 1
    rounds += 1
    result = pl.pallas_call(
        functools.partial(scan_kernel, count, backward),
        out_shape=jax.ShapeDtypeStruct(packed.shape, jnp.float32),
        in_specs=[pl.BlockSpec(memory_space=pltpu.VMEM)],
        out_specs=pl.BlockSpec(memory_space=pltpu.VMEM),
        scratch_shapes=[
            pltpu.VMEM((rounds,) + packed.shape, jnp.float32),
            pltpu.VMEM((rounds,) + packed.shape, jnp.float32),
            pltpu.SemaphoreType.DMA((rounds,)),
            pltpu.SemaphoreType.DMA((rounds,)),
        ],
        compiler_params=pltpu.CompilerParams(collective_id=1 if backward else 0, has_side_effects=True),
    )(packed)
    return result[:LINES].reshape(shape)


def stream_slope(padded, planes):
    summed = STENCIL[0] * (padded[..., 5 : 5 + planes] - padded[..., 3 : 3 + planes])
    for offset in range(2, 5):
        summed = summed + STENCIL[offset - 1] * (
            padded[..., 4 + offset : 4 + offset + planes]
            - padded[..., 4 - offset : 4 - offset + planes]
        )
    return summed


def roll_slope(values, along_axis):
    summed = STENCIL[0] * (jnp.roll(values, -1, along_axis) - jnp.roll(values, 1, along_axis))
    for offset in range(2, 5):
        summed = summed + STENCIL[offset - 1] * (
            jnp.roll(values, -offset, along_axis) - jnp.roll(values, offset, along_axis)
        )
    return summed


def compose(earlier, latter):
    return (latter[0] * earlier[0], latter[1] + latter[0] * earlier[1])


def chain_ratio(earlier, latter):
    product = jnp.dot(latter, earlier, precision=lax.Precision.HIGHEST)
    return product / jnp.max(jnp.abs(product))


def ratio_matrix(cross_term, top_right, bottom_left):
    unit_entry = jnp.ones((), jnp.float32)
    return jnp.stack([jnp.stack([cross_term, top_right]), jnp.stack([bottom_left, unit_entry])])


def shards(velocity, old_advection, lower_gap, upper_gap):
    planes = velocity.shape[3]
    padded = extended(velocity, (("gx", 3),), 4, True)
    stream = stream_slope(padded, planes)
    spanwise = roll_slope(velocity, 2)
    rimmed = extended(velocity, (("gy", 1),), 1, False)
    gap_sum = lower_gap + upper_gap
    normal_slope = (rimmed[:, 2:] - rimmed[:, :-2]) / gap_sum[None, :, None, None]
    advection = -(
        velocity[0][None] * stream + velocity[1][None] * normal_slope + velocity[2][None] * spanwise
    )
    forcing = velocity + GAMMA * advection + ZETA * old_advection
    lower_coef = -2.0 * STIFF / (gap_sum * lower_gap)
    upper_coef = -2.0 * STIFF / (gap_sum * upper_gap)
    diagonal = 1.0 - lower_coef - upper_coef
    below_band = lower_coef.at[0].set(0.0)
    above_band = upper_coef.at[-1].set(0.0)
    rows_here = velocity.shape[1]
    line_values = forcing.reshape(3, rows_here, -1)
    solved = lax.linalg.tridiagonal_solve(
        jnp.stack([below_band] * 3),
        jnp.stack([diagonal] * 3),
        jnp.stack([above_band] * 3),
        line_values,
    )
    columns = jnp.zeros((rows_here, 2), jnp.float32)
    columns = columns.at[0, 0].set(lower_coef[0]).at[rows_here - 1, 1].set(upper_coef[-1])
    spikes = lax.linalg.tridiagonal_solve(below_band, diagonal, above_band, columns)
    left_spike = spikes[:, 0]
    right_spike = spikes[:, 1]
    left_first = left_spike[0]
    left_last = left_spike[-1]
    right_first = right_spike[0]
    right_last = right_spike[-1]
    cross_term = left_last * right_first - right_last * left_first
    unit_matrix = jnp.eye(2, dtype=jnp.float32)
    below_prefix = prefix(
        ratio_matrix(cross_term, right_last, -left_first), "gy", chain_ratio, unit_matrix, False
    )
    below_ratio = below_prefix[0, 1] / below_prefix[1, 1]
    first_solved = solved[:, 0]
    last_solved = solved[:, -1]
    lower_denom = 1.0 - left_first * below_ratio
    lower_step = (
        jnp.reshape(-left_last / lower_denom, (1, 1)),
        last_solved + left_last * below_ratio / lower_denom * first_solved,
    )
    identity_step = (jnp.ones((1, 1), jnp.float32), jnp.zeros_like(first_solved))
    below_offset = line_scan(lower_step, False)
    first_base = (first_solved - left_first * below_offset) / lower_denom
    first_slope = right_first / lower_denom
    upper_step = (jnp.reshape(-first_slope, (1, 1)), first_base)
    above_value = line_scan(upper_step, True)
    first_value = first_base - first_slope * above_value
    below_value = below_offset - below_ratio * first_value
    finished = (
        solved
        - below_value[:, None, :] * left_spike[None, :, None]
        - above_value[:, None, :] * right_spike[None, :, None]
    )
    return (finished.reshape(velocity.shape), advection)


def solution(mesh):
    return jax.shard_map(
        shards,
        mesh=mesh,
        in_specs=(P(None, "gy", None, "gx"), P(None, "gy", None, "gx"), P("gy"), P("gy")),
        out_specs=(P(None, "gy", None, "gx"), P(None, "gy", None, "gx")),
        check_vma=False,
    )
```

```python
import functools

import jax
import jax.numpy as jnp
from jax import lax
from jax.sharding import PartitionSpec as P
from jax.experimental import pallas as pl
from jax.experimental.pallas import tpu as pltpu

MESH = pl.DeviceIdType.MESH
LINES = 96

STIFF = 1024


STENCIL = (0.8, -0.2, 4.0 / 105.0, -1.0 / 280.0)
GAMMA = 5.0 / 12.0
ZETA = -17.0 / 60.0


def extended(array, sides, width, wrap):
    for axis, dim in sides:
        size, length = (lax.axis_size(axis), array.shape[dim])
        up = [(i, (i + 1) % size) for i in range(size if wrap else size - 1)]
        down = [(j, i) for i, j in up]
        last = lax.slice_in_dim(array, length - width, length, axis=dim)
        first = lax.slice_in_dim(array, 0, width, axis=dim)
        before = lax.ppermute(last, axis, up)
        after = lax.ppermute(first, axis, down)
        array = jnp.concatenate([before, array, after], axis=dim)
    return array


def prefix(value, axis, join, neutral, backward):
    count, mine = (lax.axis_size(axis), lax.axis_index(axis))
    step = -1 if backward else 1
    order = [(i, i + step) for i in range(count) if 0 <= i + step < count]
    total = jax.tree.map(lambda part: lax.ppermute(part, axis, order), value)
    inside = (mine >= 1) if not backward else (mine <= count - 2)
    total = jax.tree.map(
        lambda part, zero: jnp.where(inside, part, jnp.full_like(part, 0) + jnp.asarray(zero, part.dtype)),
        total,
        neutral,
    )
    offset = 1
    while offset < count:
        pairs = [(i, i + step * offset) for i in range(count) if 0 <= i + step * offset < count]
        earlier = jax.tree.map(lambda part: lax.ppermute(part, axis, pairs), total)
        longer = join(earlier, total)
        reach = (mine >= offset) if not backward else (mine <= count - 1 - offset)
        total = jax.tree.map(lambda new, old: jnp.where(reach, new, old), longer, total)
        offset *= 2
    return total


def ratio_join(earlier, latter):
    def entry(i, j):
        return latter[2 * i : 2 * i + 1] * earlier[j : j + 1] + latter[2 * i + 1 : 2 * i + 2] * earlier[2 + j : 3 + j]

    entries = [entry(0, 0), entry(0, 1), entry(1, 0), entry(1, 1)]
    big = jnp.maximum(
        jnp.maximum(jnp.abs(entries[0]), jnp.abs(entries[1])),
        jnp.maximum(jnp.abs(entries[2]), jnp.abs(entries[3])),
    )
    rows = [part / big for part in entries]
    return jnp.concatenate(rows + [jnp.zeros((4, 128), jnp.float32)], axis=0)


def line_join(earlier, latter):
    factor = latter[LINES : LINES + 1, :]
    joined_lines = latter[:LINES] + factor * earlier[:LINES]
    joined_scale = latter[LINES:] * earlier[LINES:]
    return jnp.concatenate([joined_lines, joined_scale], axis=0)


def ratio_neutral():
    unit = jnp.ones((1, 128), jnp.float32)
    blank = jnp.zeros((1, 128), jnp.float32)
    return jnp.concatenate([unit, blank, blank, unit, blank, blank, blank, blank], axis=0)


def line_neutral():
    return jnp.concatenate([jnp.zeros((LINES, 128), jnp.float32), jnp.ones((8, 128), jnp.float32)], axis=0)


def scan_kernel(count, backward, join, neutral, x_ref, out_ref, totals, recv, send_sem, recv_sem):
    me = lax.axis_index("gy")
    row = lax.axis_index("gx")
    sign = -1 if backward else 1
    offsets = [1]
    while offsets[-1] * 2 < count:
        offsets.append(offsets[-1] * 2)
    partners = []
    for offset in offsets:
        partners.append((me + offset) % count)
        if 2 * offset != count:
            partners.append((me + count - offset) % count)
    barrier = pltpu.get_barrier_semaphore()
    for partner in partners:
        pl.semaphore_signal(barrier, inc=1, device_id=(row, partner), device_id_type=MESH)
    pl.semaphore_wait(barrier, len(partners))
    rounds = [1] + offsets
    copies = []
    for step, offset in enumerate(rounds):
        source = x_ref if step == 0 else totals.at[step - 1]
        target = (me + count + sign * offset) % count
        copy = pltpu.make_async_remote_copy(
            src_ref=source,
            dst_ref=recv.at[step],
            send_sem=send_sem.at[step],
            recv_sem=recv_sem.at[step],
            device_id=(row, target),
            device_id_type=MESH,
        )
        copy.start()
        copy.wait_recv()
        copies.append(copy)
        valid = (me + offset <= count - 1) if backward else (me >= offset)
        earlier = recv[step]
        if step == 0:
            totals[step] = jnp.where(valid, earlier, neutral())
        else:
            latter = totals[step - 1]
            totals[step] = jnp.where(valid, join(earlier, latter), latter)
    out_ref[...] = totals[len(rounds) - 1]
    for copy in copies:
        copy.wait_send()


def line_scan(step_value, backward):
    count = lax.axis_size("gy")
    factor, lines = step_value
    shape = lines.shape
    packed = jnp.concatenate(
        [lines.reshape(LINES, 128), jnp.broadcast_to(factor.reshape(1, 1), (8, 128))], axis=0
    )
    rounds = 1
    while (1 << (rounds - 1)) * 2 < count:
        rounds += 1
    rounds += 1
    result = pl.pallas_call(
        functools.partial(scan_kernel, count, backward, line_join, line_neutral),
        out_shape=jax.ShapeDtypeStruct(packed.shape, jnp.float32),
        in_specs=[pl.BlockSpec(memory_space=pltpu.VMEM)],
        out_specs=pl.BlockSpec(memory_space=pltpu.VMEM),
        scratch_shapes=[
            pltpu.VMEM((rounds,) + packed.shape, jnp.float32),
            pltpu.VMEM((rounds,) + packed.shape, jnp.float32),
            pltpu.SemaphoreType.DMA((rounds,)),
            pltpu.SemaphoreType.DMA((rounds,)),
        ],
        compiler_params=pltpu.CompilerParams(collective_id=1 if backward else 0, has_side_effects=True),
    )(packed)
    return result[:LINES].reshape(shape)


def ratio_scan(matrix):
    count = lax.axis_size("gy")
    packed = jnp.concatenate(
        [jnp.broadcast_to(matrix.reshape(4, 1), (4, 128)), jnp.zeros((4, 128), jnp.float32)], axis=0
    )
    rounds = 1
    while (1 << (rounds - 1)) * 2 < count:
        rounds += 1
    rounds += 1
    result = pl.pallas_call(
        functools.partial(scan_kernel, count, False, ratio_join, ratio_neutral),
        out_shape=jax.ShapeDtypeStruct(packed.shape, jnp.float32),
        in_specs=[pl.BlockSpec(memory_space=pltpu.VMEM)],
        out_specs=pl.BlockSpec(memory_space=pltpu.VMEM),
        scratch_shapes=[
            pltpu.VMEM((rounds,) + packed.shape, jnp.float32),
            pltpu.VMEM((rounds,) + packed.shape, jnp.float32),
            pltpu.SemaphoreType.DMA((rounds,)),
            pltpu.SemaphoreType.DMA((rounds,)),
        ],
        compiler_params=pltpu.CompilerParams(collective_id=2, has_side_effects=True),
    )(packed)
    return result[:4, 0].reshape(2, 2)


def ratio_prefix(matrix):
    count, mine = (lax.axis_size("gy"), lax.axis_index("gy"))
    pieces = lax.all_gather(matrix, "gy")

    def join(earlier, latter):
        def entry(i, j):
            return latter[:, 2 * i] * earlier[:, j] + latter[:, 2 * i + 1] * earlier[:, 2 + j]

        entries = jnp.stack([entry(0, 0), entry(0, 1), entry(1, 0), entry(1, 1)], axis=1)
        return entries / jnp.max(jnp.abs(entries), axis=1, keepdims=True)

    inclusive = lax.associative_scan(join, pieces, axis=0)
    identity = jnp.array([[1.0, 0.0, 0.0, 1.0]], jnp.float32)
    exclusive = jnp.concatenate([identity, inclusive[: count - 1]], axis=0)
    own = lax.dynamic_index_in_dim(exclusive, mine, axis=0, keepdims=False)
    return own[1] / own[3]


def stream_slope(padded, planes):
    summed = STENCIL[0] * (padded[..., 5 : 5 + planes] - padded[..., 3 : 3 + planes])
    for offset in range(2, 5):
        summed = summed + STENCIL[offset - 1] * (
            padded[..., 4 + offset : 4 + offset + planes]
            - padded[..., 4 - offset : 4 - offset + planes]
        )
    return summed


def roll_slope(values, along_axis):
    summed = STENCIL[0] * (jnp.roll(values, -1, along_axis) - jnp.roll(values, 1, along_axis))
    for offset in range(2, 5):
        summed = summed + STENCIL[offset - 1] * (
            jnp.roll(values, -offset, along_axis) - jnp.roll(values, offset, along_axis)
        )
    return summed


def compose(earlier, latter):
    return (latter[0] * earlier[0], latter[1] + latter[0] * earlier[1])


def chain_ratio(earlier, latter):
    product = jnp.dot(latter, earlier, precision=lax.Precision.HIGHEST)
    return product / jnp.max(jnp.abs(product))


def ratio_matrix(cross_term, top_right, bottom_left):
    unit_entry = jnp.ones((), jnp.float32)
    return jnp.stack([jnp.stack([cross_term, top_right]), jnp.stack([bottom_left, unit_entry])])


def shards(velocity, old_advection, lower_gap, upper_gap):
    planes = velocity.shape[3]
    padded = extended(velocity, (("gx", 3),), 4, True)
    stream = stream_slope(padded, planes)
    spanwise = roll_slope(velocity, 2)
    rimmed = extended(velocity, (("gy", 1),), 1, False)
    gap_sum = lower_gap + upper_gap
    normal_slope = (rimmed[:, 2:] - rimmed[:, :-2]) / gap_sum[None, :, None, None]
    advection = -(
        velocity[0][None] * stream + velocity[1][None] * normal_slope + velocity[2][None] * spanwise
    )
    forcing = velocity + GAMMA * advection + ZETA * old_advection
    lower_coef = -2.0 * STIFF / (gap_sum * lower_gap)
    upper_coef = -2.0 * STIFF / (gap_sum * upper_gap)
    diagonal = 1.0 - lower_coef - upper_coef
    rows_here = velocity.shape[1]

    top = (jnp.ones((), jnp.float32), jnp.zeros((), jnp.float32))
    bottom = (jnp.zeros((), jnp.float32), jnp.ones((), jnp.float32))
    for i in range(rows_here):
        scale = 1.0 / diagonal[i]
        up, low = upper_coef[i] * scale, -lower_coef[i] * scale
        top, bottom = (
            (up * bottom[0], up * bottom[1]),
            (low * top[0] + bottom[0], low * top[1] + bottom[1]),
        )
    big = jnp.maximum(
        jnp.maximum(jnp.abs(top[0]), jnp.abs(top[1])), jnp.maximum(jnp.abs(bottom[0]), jnp.abs(bottom[1]))
    )
    matrix = jnp.stack([top[0], top[1], bottom[0], bottom[1]]) / big
    modified_prev = ratio_prefix(matrix)

    pivots, modified = [], []
    for i in range(rows_here):
        pivot = diagonal[i] - lower_coef[i] * modified_prev
        modified_prev = upper_coef[i] / pivot
        pivots.append(pivot)
        modified.append(modified_prev)

    line_rows = forcing.reshape(3, rows_here, -1)
    zero_lines = jnp.zeros_like(line_rows[:, 0])
    carried = zero_lines
    weight = jnp.ones((), jnp.float32)
    reduced, weights = [], []
    for i in range(rows_here):
        carried = (line_rows[:, i] - lower_coef[i] * carried) / pivots[i]
        weight = -lower_coef[i] / pivots[i] * weight
        reduced.append(carried)
        weights.append(weight)
    below_carry = line_scan((jnp.reshape(weight, (1, 1)), carried), False)
    reduced = [value + w * below_carry for value, w in zip(reduced, weights)]

    carried = zero_lines
    weight = jnp.ones((), jnp.float32)
    local, back_weights = [None] * rows_here, [None] * rows_here
    for i in reversed(range(rows_here)):
        carried = reduced[i] - modified[i] * carried
        weight = -modified[i] * weight
        local[i] = carried
        back_weights[i] = weight
    above_carry = line_scan((jnp.reshape(weight, (1, 1)), carried), True)
    finished = jnp.stack([value + w * above_carry for value, w in zip(local, back_weights)], axis=1)
    return (finished.reshape(velocity.shape), advection)


def solution(mesh):
    return jax.shard_map(
        shards,
        mesh=mesh,
        in_specs=(P(None, "gy", None, "gx"), P(None, "gy", None, "gx"), P("gy"), P("gy")),
        out_specs=(P(None, "gy", None, "gx"), P(None, "gy", None, "gx")),
        check_vma=False,
    )
```

```python
import functools

import jax
import jax.numpy as jnp
from jax import lax
from jax.sharding import PartitionSpec as P
from jax.experimental import pallas as pl
from jax.experimental.pallas import tpu as pltpu

MESH = pl.DeviceIdType.MESH
LINES = 96

STIFF = 1024


STENCIL = (0.8, -0.2, 4.0 / 105.0, -1.0 / 280.0)
GAMMA = 5.0 / 12.0
ZETA = -17.0 / 60.0


def extended(array, sides, width, wrap):
    for axis, dim in sides:
        size, length = (lax.axis_size(axis), array.shape[dim])
        up = [(i, (i + 1) % size) for i in range(size if wrap else size - 1)]
        down = [(j, i) for i, j in up]
        last = lax.slice_in_dim(array, length - width, length, axis=dim)
        first = lax.slice_in_dim(array, 0, width, axis=dim)
        before = lax.ppermute(last, axis, up)
        after = lax.ppermute(first, axis, down)
        array = jnp.concatenate([before, array, after], axis=dim)
    return array


def prefix(value, axis, join, neutral, backward):
    count, mine = (lax.axis_size(axis), lax.axis_index(axis))
    step = -1 if backward else 1
    order = [(i, i + step) for i in range(count) if 0 <= i + step < count]
    total = jax.tree.map(lambda part: lax.ppermute(part, axis, order), value)
    inside = (mine >= 1) if not backward else (mine <= count - 2)
    total = jax.tree.map(
        lambda part, zero: jnp.where(inside, part, jnp.full_like(part, 0) + jnp.asarray(zero, part.dtype)),
        total,
        neutral,
    )
    offset = 1
    while offset < count:
        pairs = [(i, i + step * offset) for i in range(count) if 0 <= i + step * offset < count]
        earlier = jax.tree.map(lambda part: lax.ppermute(part, axis, pairs), total)
        longer = join(earlier, total)
        reach = (mine >= offset) if not backward else (mine <= count - 1 - offset)
        total = jax.tree.map(lambda new, old: jnp.where(reach, new, old), longer, total)
        offset *= 2
    return total


def ratio_join(earlier, latter):
    def entry(i, j):
        return latter[2 * i : 2 * i + 1] * earlier[j : j + 1] + latter[2 * i + 1 : 2 * i + 2] * earlier[2 + j : 3 + j]

    entries = [entry(0, 0), entry(0, 1), entry(1, 0), entry(1, 1)]
    big = jnp.maximum(
        jnp.maximum(jnp.abs(entries[0]), jnp.abs(entries[1])),
        jnp.maximum(jnp.abs(entries[2]), jnp.abs(entries[3])),
    )
    rows = [part / big for part in entries]
    return jnp.concatenate(rows + [jnp.zeros((4, 128), jnp.float32)], axis=0)


def line_join(earlier, latter):
    factor = latter[LINES : LINES + 1, :]
    joined_lines = latter[:LINES] + factor * earlier[:LINES]
    joined_scale = latter[LINES:] * earlier[LINES:]
    return jnp.concatenate([joined_lines, joined_scale], axis=0)


def ratio_neutral():
    unit = jnp.ones((1, 128), jnp.float32)
    blank = jnp.zeros((1, 128), jnp.float32)
    return jnp.concatenate([unit, blank, blank, unit, blank, blank, blank, blank], axis=0)


def line_neutral():
    return jnp.concatenate([jnp.zeros((LINES, 128), jnp.float32), jnp.ones((8, 128), jnp.float32)], axis=0)


def scan_kernel(count, backward, join, neutral, x_ref, out_ref, totals, recv, send_sem, recv_sem):
    me = lax.axis_index("gy")
    row = lax.axis_index("gx")
    sign = -1 if backward else 1
    offsets = [1]
    while offsets[-1] * 2 < count:
        offsets.append(offsets[-1] * 2)
    partners = []
    for offset in offsets:
        partners.append((me + offset) % count)
        if 2 * offset != count:
            partners.append((me + count - offset) % count)
    barrier = pltpu.get_barrier_semaphore()
    for partner in partners:
        pl.semaphore_signal(barrier, inc=1, device_id=(row, partner), device_id_type=MESH)
    pl.semaphore_wait(barrier, len(partners))
    rounds = [1] + offsets
    copies = []
    for step, offset in enumerate(rounds):
        source = x_ref if step == 0 else totals.at[step - 1]
        target = (me + count + sign * offset) % count
        copy = pltpu.make_async_remote_copy(
            src_ref=source,
            dst_ref=recv.at[step],
            send_sem=send_sem.at[step],
            recv_sem=recv_sem.at[step],
            device_id=(row, target),
            device_id_type=MESH,
        )
        copy.start()
        copy.wait_recv()
        copies.append(copy)
        valid = (me + offset <= count - 1) if backward else (me >= offset)
        earlier = recv[step]
        if step == 0:
            totals[step] = jnp.where(valid, earlier, neutral())
        else:
            latter = totals[step - 1]
            totals[step] = jnp.where(valid, join(earlier, latter), latter)
    out_ref[...] = totals[len(rounds) - 1]
    for copy in copies:
        copy.wait_send()


def line_scan(step_value, backward):
    count = lax.axis_size("gy")
    factor, lines = step_value
    shape = lines.shape
    packed = jnp.concatenate(
        [lines.reshape(LINES, 128), jnp.broadcast_to(factor.reshape(1, 1), (8, 128))], axis=0
    )
    rounds = 1
    while (1 << (rounds - 1)) * 2 < count:
        rounds += 1
    rounds += 1
    result = pl.pallas_call(
        functools.partial(scan_kernel, count, backward, line_join, line_neutral),
        out_shape=jax.ShapeDtypeStruct(packed.shape, jnp.float32),
        in_specs=[pl.BlockSpec(memory_space=pltpu.VMEM)],
        out_specs=pl.BlockSpec(memory_space=pltpu.VMEM),
        scratch_shapes=[
            pltpu.VMEM((rounds,) + packed.shape, jnp.float32),
            pltpu.VMEM((rounds,) + packed.shape, jnp.float32),
            pltpu.SemaphoreType.DMA((rounds,)),
            pltpu.SemaphoreType.DMA((rounds,)),
        ],
        compiler_params=pltpu.CompilerParams(collective_id=1 if backward else 0, has_side_effects=True),
    )(packed)
    return result[:LINES].reshape(shape)


def ratio_scan(matrix):
    count = lax.axis_size("gy")
    packed = jnp.concatenate(
        [jnp.broadcast_to(matrix.reshape(4, 1), (4, 128)), jnp.zeros((4, 128), jnp.float32)], axis=0
    )
    rounds = 1
    while (1 << (rounds - 1)) * 2 < count:
        rounds += 1
    rounds += 1
    result = pl.pallas_call(
        functools.partial(scan_kernel, count, False, ratio_join, ratio_neutral),
        out_shape=jax.ShapeDtypeStruct(packed.shape, jnp.float32),
        in_specs=[pl.BlockSpec(memory_space=pltpu.VMEM)],
        out_specs=pl.BlockSpec(memory_space=pltpu.VMEM),
        scratch_shapes=[
            pltpu.VMEM((rounds,) + packed.shape, jnp.float32),
            pltpu.VMEM((rounds,) + packed.shape, jnp.float32),
            pltpu.SemaphoreType.DMA((rounds,)),
            pltpu.SemaphoreType.DMA((rounds,)),
        ],
        compiler_params=pltpu.CompilerParams(collective_id=2, has_side_effects=True),
    )(packed)
    return result[:4, 0].reshape(2, 2)


def ratio_prefix(matrix):
    count, mine = (lax.axis_size("gy"), lax.axis_index("gy"))
    pieces = lax.all_gather(matrix, "gy")

    def join(earlier, latter):
        def entry(i, j):
            return latter[:, 2 * i] * earlier[:, j] + latter[:, 2 * i + 1] * earlier[:, 2 + j]

        entries = jnp.stack([entry(0, 0), entry(0, 1), entry(1, 0), entry(1, 1)], axis=1)
        return entries / jnp.max(jnp.abs(entries), axis=1, keepdims=True)

    inclusive = lax.associative_scan(join, pieces, axis=0)
    identity = jnp.array([[1.0, 0.0, 0.0, 1.0]], jnp.float32)
    exclusive = jnp.concatenate([identity, inclusive[: count - 1]], axis=0)
    own = lax.dynamic_index_in_dim(exclusive, mine, axis=0, keepdims=False)
    return own[1] / own[3]


def stream_slope(padded, planes):
    summed = STENCIL[0] * (padded[..., 5 : 5 + planes] - padded[..., 3 : 3 + planes])
    for offset in range(2, 5):
        summed = summed + STENCIL[offset - 1] * (
            padded[..., 4 + offset : 4 + offset + planes]
            - padded[..., 4 - offset : 4 - offset + planes]
        )
    return summed


def roll_slope(values, along_axis):
    summed = STENCIL[0] * (jnp.roll(values, -1, along_axis) - jnp.roll(values, 1, along_axis))
    for offset in range(2, 5):
        summed = summed + STENCIL[offset - 1] * (
            jnp.roll(values, -offset, along_axis) - jnp.roll(values, offset, along_axis)
        )
    return summed


def compose(earlier, latter):
    return (latter[0] * earlier[0], latter[1] + latter[0] * earlier[1])


def chain_ratio(earlier, latter):
    product = jnp.dot(latter, earlier, precision=lax.Precision.HIGHEST)
    return product / jnp.max(jnp.abs(product))


def ratio_matrix(cross_term, top_right, bottom_left):
    unit_entry = jnp.ones((), jnp.float32)
    return jnp.stack([jnp.stack([cross_term, top_right]), jnp.stack([bottom_left, unit_entry])])


def radix_plan(count):
    plan = [list(range(1, min(4, count - 1) + 1))]
    span = len(plan[0])
    while span < count - 1:
        offsets = [span * j for j in range(1, 4) if span * j < count]
        plan.append(offsets)
        span = span * (1 + len(offsets))
    return plan


def radix_scan(me, row, count, backward, element, parts, recv, send_sem, recv_sem, base, copies):
    sign = -1 if backward else 1
    plan = radix_plan(count)
    slot = base
    for level, offsets in enumerate(plan):
        source = element if level == 0 else parts.at[level - 1]
        started = []
        for offset in offsets:
            target = (me + count + sign * offset) % count
            copy = pltpu.make_async_remote_copy(
                src_ref=source,
                dst_ref=recv.at[slot],
                send_sem=send_sem.at[slot],
                recv_sem=recv_sem.at[slot],
                device_id=(row, target),
                device_id_type=MESH,
            )
            copy.start()
            started.append((offset, slot, copy))
            slot += 1
        acc = line_neutral() if level == 0 else parts[level - 1]
        for offset, index, copy in started:
            copy.wait_recv()
            copies.append(copy)
            valid = (me + offset <= count - 1) if backward else (me >= offset)
            acc = jnp.where(valid, line_join(recv[index], acc), acc)
        parts[level] = acc
    return parts[len(plan) - 1]


def carry_kernel(count, rows_here, element_ref, rows_ref, coef_ref, out_ref, parts_down, up_element, parts_up,
                 recv, send_sem, recv_sem):
    me = lax.axis_index("gy")
    row = lax.axis_index("gx")
    plan = radix_plan(count)
    residues = set()
    for offsets in plan:
        for offset in offsets:
            residues.add(offset % count)
            residues.add((count - offset) % count)
    residues.discard(0)
    barrier = pltpu.get_barrier_semaphore()
    for residue in sorted(residues):
        pl.semaphore_signal(barrier, inc=1, device_id=(row, (me + residue) % count), device_id_type=MESH)
    pl.semaphore_wait(barrier, len(residues))
    copies = []
    slots = sum(len(offsets) for offsets in plan)

    below_carry = radix_scan(
        me, row, count, False, element_ref, parts_down, recv, send_sem, recv_sem, 0, copies
    )[:LINES]
    coef = coef_ref[...]
    carried = None
    weight = None
    for i in reversed(range(rows_here)):
        sensitivity = coef[i : i + 1]
        modified = coef[16 + i : 17 + i]
        reduced = rows_ref[i] + sensitivity * below_carry
        if carried is None:
            carried = reduced
            weight = -modified
        else:
            carried = reduced - modified * carried
            weight = -modified * weight
        out_ref[i] = carried
    up_element[...] = jnp.concatenate([carried, jnp.broadcast_to(weight, (8, 128))], axis=0)
    above_carry = radix_scan(
        me, row, count, True, up_element, parts_up, recv, send_sem, recv_sem, slots, copies
    )[:LINES]
    weight = None
    for i in reversed(range(rows_here)):
        modified = coef[16 + i : 17 + i]
        weight = -modified if weight is None else -modified * weight
        out_ref[i] = out_ref[i] + weight * above_carry
    for copy in copies:
        copy.wait_send()


def carry_solve(element_factor, element_lines, rows, sensitivities, modified):
    count = lax.axis_size("gy")
    rows_here = len(rows)
    packed = jnp.concatenate(
        [element_lines.reshape(LINES, 128), jnp.broadcast_to(element_factor.reshape(1, 1), (8, 128))], axis=0
    )
    stacked = jnp.stack([value.reshape(LINES, 128) for value in rows], axis=0)
    scalars = (
        [jnp.reshape(value, (1,)) for value in sensitivities]
        + [jnp.zeros((16 - rows_here,), jnp.float32)]
        + [jnp.reshape(value, (1,)) for value in modified]
        + [jnp.zeros((16 - rows_here,), jnp.float32)]
    )
    coef = jnp.broadcast_to(jnp.concatenate(scalars).reshape(32, 1), (32, 128))
    plan = radix_plan(count)
    slots = 2 * sum(len(offsets) for offsets in plan)
    big = (LINES + 8, 128)
    return pl.pallas_call(
        functools.partial(carry_kernel, count, rows_here),
        out_shape=jax.ShapeDtypeStruct((rows_here, LINES, 128), jnp.float32),
        in_specs=[pl.BlockSpec(memory_space=pltpu.VMEM)] * 3,
        out_specs=pl.BlockSpec(memory_space=pltpu.VMEM),
        scratch_shapes=[
            pltpu.VMEM((len(plan),) + big, jnp.float32),
            pltpu.VMEM(big, jnp.float32),
            pltpu.VMEM((len(plan),) + big, jnp.float32),
            pltpu.VMEM((slots,) + big, jnp.float32),
            pltpu.SemaphoreType.DMA((slots,)),
            pltpu.SemaphoreType.DMA((slots,)),
        ],
        compiler_params=pltpu.CompilerParams(collective_id=0, has_side_effects=True),
    )(packed, stacked, coef)


def shards(velocity, old_advection, lower_gap, upper_gap):
    planes = velocity.shape[3]
    padded = extended(velocity, (("gx", 3),), 4, True)
    stream = stream_slope(padded, planes)
    spanwise = roll_slope(velocity, 2)
    rimmed = extended(velocity, (("gy", 1),), 1, False)
    gap_sum = lower_gap + upper_gap
    normal_slope = (rimmed[:, 2:] - rimmed[:, :-2]) / gap_sum[None, :, None, None]
    advection = -(
        velocity[0][None] * stream + velocity[1][None] * normal_slope + velocity[2][None] * spanwise
    )
    forcing = velocity + GAMMA * advection + ZETA * old_advection
    lower_coef = -2.0 * STIFF / (gap_sum * lower_gap)
    upper_coef = -2.0 * STIFF / (gap_sum * upper_gap)
    diagonal = 1.0 - lower_coef - upper_coef
    rows_here = velocity.shape[1]

    top = (jnp.ones((), jnp.float32), jnp.zeros((), jnp.float32))
    bottom = (jnp.zeros((), jnp.float32), jnp.ones((), jnp.float32))
    for i in range(rows_here):
        scale = 1.0 / diagonal[i]
        up, low = upper_coef[i] * scale, -lower_coef[i] * scale
        top, bottom = (
            (up * bottom[0], up * bottom[1]),
            (low * top[0] + bottom[0], low * top[1] + bottom[1]),
        )
    big = jnp.maximum(
        jnp.maximum(jnp.abs(top[0]), jnp.abs(top[1])), jnp.maximum(jnp.abs(bottom[0]), jnp.abs(bottom[1]))
    )
    matrix = jnp.stack([top[0], top[1], bottom[0], bottom[1]]) / big
    modified_prev = ratio_prefix(matrix)

    pivots, modified = [], []
    for i in range(rows_here):
        pivot = diagonal[i] - lower_coef[i] * modified_prev
        modified_prev = upper_coef[i] / pivot
        pivots.append(pivot)
        modified.append(modified_prev)

    line_rows = forcing.reshape(3, rows_here, -1)
    zero_lines = jnp.zeros_like(line_rows[:, 0])
    carried = zero_lines
    weight = jnp.ones((), jnp.float32)
    reduced, weights = [], []
    for i in range(rows_here):
        carried = (line_rows[:, i] - lower_coef[i] * carried) / pivots[i]
        weight = -lower_coef[i] / pivots[i] * weight
        reduced.append(carried)
        weights.append(weight)
    solved = carry_solve(weight, carried, reduced, weights, modified)
    finished = jnp.transpose(solved.reshape(rows_here, 3, 32, -1), (1, 0, 2, 3))
    return (finished.reshape(velocity.shape), advection)


def solution(mesh):
    return jax.shard_map(
        shards,
        mesh=mesh,
        in_specs=(P(None, "gy", None, "gx"), P(None, "gy", None, "gx"), P("gy"), P("gy")),
        out_specs=(P(None, "gy", None, "gx"), P(None, "gy", None, "gx")),
        check_vma=False,
    )
```

```python
import functools

import jax
import jax.numpy as jnp
from jax import lax
from jax.sharding import PartitionSpec as P
from jax.experimental import pallas as pl
from jax.experimental.pallas import tpu as pltpu

MESH = pl.DeviceIdType.MESH
LINES = 96

STIFF = 1024


STENCIL = (0.8, -0.2, 4.0 / 105.0, -1.0 / 280.0)
GAMMA = 5.0 / 12.0
ZETA = -17.0 / 60.0


def extended(array, sides, width, wrap):
    for axis, dim in sides:
        size, length = (lax.axis_size(axis), array.shape[dim])
        up = [(i, (i + 1) % size) for i in range(size if wrap else size - 1)]
        down = [(j, i) for i, j in up]
        last = lax.slice_in_dim(array, length - width, length, axis=dim)
        first = lax.slice_in_dim(array, 0, width, axis=dim)
        before = lax.ppermute(last, axis, up)
        after = lax.ppermute(first, axis, down)
        array = jnp.concatenate([before, array, after], axis=dim)
    return array


def prefix(value, axis, join, neutral, backward):
    count, mine = (lax.axis_size(axis), lax.axis_index(axis))
    step = -1 if backward else 1
    order = [(i, i + step) for i in range(count) if 0 <= i + step < count]
    total = jax.tree.map(lambda part: lax.ppermute(part, axis, order), value)
    inside = (mine >= 1) if not backward else (mine <= count - 2)
    total = jax.tree.map(
        lambda part, zero: jnp.where(inside, part, jnp.full_like(part, 0) + jnp.asarray(zero, part.dtype)),
        total,
        neutral,
    )
    offset = 1
    while offset < count:
        pairs = [(i, i + step * offset) for i in range(count) if 0 <= i + step * offset < count]
        earlier = jax.tree.map(lambda part: lax.ppermute(part, axis, pairs), total)
        longer = join(earlier, total)
        reach = (mine >= offset) if not backward else (mine <= count - 1 - offset)
        total = jax.tree.map(lambda new, old: jnp.where(reach, new, old), longer, total)
        offset *= 2
    return total


def ratio_join(earlier, latter):
    def entry(i, j):
        return latter[2 * i : 2 * i + 1] * earlier[j : j + 1] + latter[2 * i + 1 : 2 * i + 2] * earlier[2 + j : 3 + j]

    entries = [entry(0, 0), entry(0, 1), entry(1, 0), entry(1, 1)]
    big = jnp.maximum(
        jnp.maximum(jnp.abs(entries[0]), jnp.abs(entries[1])),
        jnp.maximum(jnp.abs(entries[2]), jnp.abs(entries[3])),
    )
    rows = [part / big for part in entries]
    return jnp.concatenate(rows + [jnp.zeros((4, 128), jnp.float32)], axis=0)


def line_join(earlier, latter):
    factor = latter[LINES : LINES + 1, :]
    joined_lines = latter[:LINES] + factor * earlier[:LINES]
    joined_scale = latter[LINES:] * earlier[LINES:]
    return jnp.concatenate([joined_lines, joined_scale], axis=0)


def ratio_neutral():
    unit = jnp.ones((1, 128), jnp.float32)
    blank = jnp.zeros((1, 128), jnp.float32)
    return jnp.concatenate([unit, blank, blank, unit, blank, blank, blank, blank], axis=0)


def line_neutral():
    return jnp.concatenate([jnp.zeros((LINES, 128), jnp.float32), jnp.ones((8, 128), jnp.float32)], axis=0)


def scan_kernel(count, backward, join, neutral, x_ref, out_ref, totals, recv, send_sem, recv_sem):
    me = lax.axis_index("gy")
    row = lax.axis_index("gx")
    sign = -1 if backward else 1
    offsets = [1]
    while offsets[-1] * 2 < count:
        offsets.append(offsets[-1] * 2)
    partners = []
    for offset in offsets:
        partners.append((me + offset) % count)
        if 2 * offset != count:
            partners.append((me + count - offset) % count)
    barrier = pltpu.get_barrier_semaphore()
    for partner in partners:
        pl.semaphore_signal(barrier, inc=1, device_id=(row, partner), device_id_type=MESH)
    pl.semaphore_wait(barrier, len(partners))
    rounds = [1] + offsets
    copies = []
    for step, offset in enumerate(rounds):
        source = x_ref if step == 0 else totals.at[step - 1]
        target = (me + count + sign * offset) % count
        copy = pltpu.make_async_remote_copy(
            src_ref=source,
            dst_ref=recv.at[step],
            send_sem=send_sem.at[step],
            recv_sem=recv_sem.at[step],
            device_id=(row, target),
            device_id_type=MESH,
        )
        copy.start()
        copy.wait_recv()
        copies.append(copy)
        valid = (me + offset <= count - 1) if backward else (me >= offset)
        earlier = recv[step]
        if step == 0:
            totals[step] = jnp.where(valid, earlier, neutral())
        else:
            latter = totals[step - 1]
            totals[step] = jnp.where(valid, join(earlier, latter), latter)
    out_ref[...] = totals[len(rounds) - 1]
    for copy in copies:
        copy.wait_send()


def line_scan(step_value, backward):
    count = lax.axis_size("gy")
    factor, lines = step_value
    shape = lines.shape
    packed = jnp.concatenate(
        [lines.reshape(LINES, 128), jnp.broadcast_to(factor.reshape(1, 1), (8, 128))], axis=0
    )
    rounds = 1
    while (1 << (rounds - 1)) * 2 < count:
        rounds += 1
    rounds += 1
    result = pl.pallas_call(
        functools.partial(scan_kernel, count, backward, line_join, line_neutral),
        out_shape=jax.ShapeDtypeStruct(packed.shape, jnp.float32),
        in_specs=[pl.BlockSpec(memory_space=pltpu.VMEM)],
        out_specs=pl.BlockSpec(memory_space=pltpu.VMEM),
        scratch_shapes=[
            pltpu.VMEM((rounds,) + packed.shape, jnp.float32),
            pltpu.VMEM((rounds,) + packed.shape, jnp.float32),
            pltpu.SemaphoreType.DMA((rounds,)),
            pltpu.SemaphoreType.DMA((rounds,)),
        ],
        compiler_params=pltpu.CompilerParams(collective_id=1 if backward else 0, has_side_effects=True),
    )(packed)
    return result[:LINES].reshape(shape)


def ratio_scan(matrix):
    count = lax.axis_size("gy")
    packed = jnp.concatenate(
        [jnp.broadcast_to(matrix.reshape(4, 1), (4, 128)), jnp.zeros((4, 128), jnp.float32)], axis=0
    )
    rounds = 1
    while (1 << (rounds - 1)) * 2 < count:
        rounds += 1
    rounds += 1
    result = pl.pallas_call(
        functools.partial(scan_kernel, count, False, ratio_join, ratio_neutral),
        out_shape=jax.ShapeDtypeStruct(packed.shape, jnp.float32),
        in_specs=[pl.BlockSpec(memory_space=pltpu.VMEM)],
        out_specs=pl.BlockSpec(memory_space=pltpu.VMEM),
        scratch_shapes=[
            pltpu.VMEM((rounds,) + packed.shape, jnp.float32),
            pltpu.VMEM((rounds,) + packed.shape, jnp.float32),
            pltpu.SemaphoreType.DMA((rounds,)),
            pltpu.SemaphoreType.DMA((rounds,)),
        ],
        compiler_params=pltpu.CompilerParams(collective_id=2, has_side_effects=True),
    )(packed)
    return result[:4, 0].reshape(2, 2)


def ratio_prefix(matrix):
    count, mine = (lax.axis_size("gy"), lax.axis_index("gy"))
    pieces = lax.all_gather(matrix, "gy")
    total = [jnp.ones((), jnp.float32), jnp.zeros((), jnp.float32), jnp.zeros((), jnp.float32), jnp.ones((), jnp.float32)]
    for position in range(count - 1):
        piece = pieces[position]
        entries = [
            piece[2 * i] * total[j] + piece[2 * i + 1] * total[2 + j] for i in range(2) for j in range(2)
        ]
        big = jnp.maximum(jnp.maximum(jnp.abs(entries[0]), jnp.abs(entries[1])), jnp.maximum(jnp.abs(entries[2]), jnp.abs(entries[3])))
        inside = position < mine
        total = [jnp.where(inside, value / big, old) for value, old in zip(entries, total)]
    return total[1] / total[3]


def stream_slope(padded, planes):
    summed = STENCIL[0] * (padded[..., 5 : 5 + planes] - padded[..., 3 : 3 + planes])
    for offset in range(2, 5):
        summed = summed + STENCIL[offset - 1] * (
            padded[..., 4 + offset : 4 + offset + planes]
            - padded[..., 4 - offset : 4 - offset + planes]
        )
    return summed


def roll_slope(values, along_axis):
    summed = STENCIL[0] * (jnp.roll(values, -1, along_axis) - jnp.roll(values, 1, along_axis))
    for offset in range(2, 5):
        summed = summed + STENCIL[offset - 1] * (
            jnp.roll(values, -offset, along_axis) - jnp.roll(values, offset, along_axis)
        )
    return summed


def compose(earlier, latter):
    return (latter[0] * earlier[0], latter[1] + latter[0] * earlier[1])


def chain_ratio(earlier, latter):
    product = jnp.dot(latter, earlier, precision=lax.Precision.HIGHEST)
    return product / jnp.max(jnp.abs(product))


def ratio_matrix(cross_term, top_right, bottom_left):
    unit_entry = jnp.ones((), jnp.float32)
    return jnp.stack([jnp.stack([cross_term, top_right]), jnp.stack([bottom_left, unit_entry])])


def radix_plan(count):
    plan = [list(range(1, min(4, count - 1) + 1))]
    span = len(plan[0])
    while span < count - 1:
        offsets = [span * j for j in range(1, 4) if span * j < count]
        plan.append(offsets)
        span = span * (1 + len(offsets))
    return plan


def radix_scan(me, row, count, backward, element, parts, recv, send_sem, recv_sem, base, copies):
    sign = -1 if backward else 1
    plan = radix_plan(count)
    slot = base
    for level, offsets in enumerate(plan):
        source = element if level == 0 else parts.at[level - 1]
        started = []
        for offset in offsets:
            target = (me + count + sign * offset) % count
            copy = pltpu.make_async_remote_copy(
                src_ref=source,
                dst_ref=recv.at[slot],
                send_sem=send_sem.at[slot],
                recv_sem=recv_sem.at[slot],
                device_id=(row, target),
                device_id_type=MESH,
            )
            copy.start()
            started.append((offset, slot, copy))
            slot += 1
        acc = line_neutral() if level == 0 else parts[level - 1]
        for offset, index, copy in started:
            copy.wait_recv()
            copies.append(copy)
            valid = (me + offset <= count - 1) if backward else (me >= offset)
            acc = jnp.where(valid, line_join(recv[index], acc), acc)
        parts[level] = acc
    return parts[len(plan) - 1]


def carry_kernel(count, rows_here, element_ref, rows_ref, coef_ref, out_ref, parts_down, up_element, parts_up,
                 recv, send_sem, recv_sem):
    me = lax.axis_index("gy")
    row = lax.axis_index("gx")
    plan = radix_plan(count)
    residues = set()
    for offsets in plan:
        for offset in offsets:
            residues.add(offset % count)
            residues.add((count - offset) % count)
    residues.discard(0)
    barrier = pltpu.get_barrier_semaphore()
    for residue in sorted(residues):
        pl.semaphore_signal(barrier, inc=1, device_id=(row, (me + residue) % count), device_id_type=MESH)
    pl.semaphore_wait(barrier, len(residues))
    copies = []
    slots = sum(len(offsets) for offsets in plan)

    below_carry = radix_scan(
        me, row, count, False, element_ref, parts_down, recv, send_sem, recv_sem, 0, copies
    )[:LINES]
    coef = coef_ref[...]
    carried = None
    weight = None
    for i in reversed(range(rows_here)):
        sensitivity = coef[i : i + 1]
        modified = coef[16 + i : 17 + i]
        reduced = rows_ref[i] + sensitivity * below_carry
        if carried is None:
            carried = reduced
            weight = -modified
        else:
            carried = reduced - modified * carried
            weight = -modified * weight
        out_ref[i] = carried
    up_element[...] = jnp.concatenate([carried, jnp.broadcast_to(weight, (8, 128))], axis=0)
    above_carry = radix_scan(
        me, row, count, True, up_element, parts_up, recv, send_sem, recv_sem, slots, copies
    )[:LINES]
    weight = None
    for i in reversed(range(rows_here)):
        modified = coef[16 + i : 17 + i]
        weight = -modified if weight is None else -modified * weight
        out_ref[i] = out_ref[i] + weight * above_carry
    for copy in copies:
        copy.wait_send()


def carry_solve(element_factor, element_lines, rows, sensitivities, modified):
    count = lax.axis_size("gy")
    rows_here = len(rows)
    packed = jnp.concatenate(
        [element_lines.reshape(LINES, 128), jnp.broadcast_to(element_factor.reshape(1, 1), (8, 128))], axis=0
    )
    stacked = jnp.stack([value.reshape(LINES, 128) for value in rows], axis=0)
    scalars = (
        [jnp.reshape(value, (1,)) for value in sensitivities]
        + [jnp.zeros((16 - rows_here,), jnp.float32)]
        + [jnp.reshape(value, (1,)) for value in modified]
        + [jnp.zeros((16 - rows_here,), jnp.float32)]
    )
    coef = jnp.broadcast_to(jnp.concatenate(scalars).reshape(32, 1), (32, 128))
    plan = radix_plan(count)
    slots = 2 * sum(len(offsets) for offsets in plan)
    big = (LINES + 8, 128)
    return pl.pallas_call(
        functools.partial(carry_kernel, count, rows_here),
        out_shape=jax.ShapeDtypeStruct((rows_here, LINES, 128), jnp.float32),
        in_specs=[pl.BlockSpec(memory_space=pltpu.VMEM)] * 3,
        out_specs=pl.BlockSpec(memory_space=pltpu.VMEM),
        scratch_shapes=[
            pltpu.VMEM((len(plan),) + big, jnp.float32),
            pltpu.VMEM(big, jnp.float32),
            pltpu.VMEM((len(plan),) + big, jnp.float32),
            pltpu.VMEM((slots,) + big, jnp.float32),
            pltpu.SemaphoreType.DMA((slots,)),
            pltpu.SemaphoreType.DMA((slots,)),
        ],
        compiler_params=pltpu.CompilerParams(collective_id=0, has_side_effects=True),
    )(packed, stacked, coef)


def shards(velocity, old_advection, lower_gap, upper_gap):
    planes = velocity.shape[3]
    padded = extended(velocity, (("gx", 3),), 4, True)
    stream = stream_slope(padded, planes)
    spanwise = roll_slope(velocity, 2)
    rimmed = extended(velocity, (("gy", 1),), 1, False)
    gap_sum = lower_gap + upper_gap
    normal_slope = (rimmed[:, 2:] - rimmed[:, :-2]) / gap_sum[None, :, None, None]
    advection = -(
        velocity[0][None] * stream + velocity[1][None] * normal_slope + velocity[2][None] * spanwise
    )
    forcing = velocity + GAMMA * advection + ZETA * old_advection
    lower_coef = -2.0 * STIFF / (gap_sum * lower_gap)
    upper_coef = -2.0 * STIFF / (gap_sum * upper_gap)
    diagonal = 1.0 - lower_coef - upper_coef
    rows_here = velocity.shape[1]

    top = (jnp.ones((), jnp.float32), jnp.zeros((), jnp.float32))
    bottom = (jnp.zeros((), jnp.float32), jnp.ones((), jnp.float32))
    for i in range(rows_here):
        scale = 1.0 / diagonal[i]
        up, low = upper_coef[i] * scale, -lower_coef[i] * scale
        top, bottom = (
            (up * bottom[0], up * bottom[1]),
            (low * top[0] + bottom[0], low * top[1] + bottom[1]),
        )
    big = jnp.maximum(
        jnp.maximum(jnp.abs(top[0]), jnp.abs(top[1])), jnp.maximum(jnp.abs(bottom[0]), jnp.abs(bottom[1]))
    )
    matrix = jnp.stack([top[0], top[1], bottom[0], bottom[1]]) / big
    modified_prev = ratio_prefix(matrix)

    pivots, modified = [], []
    for i in range(rows_here):
        pivot = diagonal[i] - lower_coef[i] * modified_prev
        modified_prev = upper_coef[i] / pivot
        pivots.append(pivot)
        modified.append(modified_prev)

    line_rows = forcing.reshape(3, rows_here, -1)
    zero_lines = jnp.zeros_like(line_rows[:, 0])
    carried = zero_lines
    weight = jnp.ones((), jnp.float32)
    reduced, weights = [], []
    for i in range(rows_here):
        carried = (line_rows[:, i] - lower_coef[i] * carried) / pivots[i]
        weight = -lower_coef[i] / pivots[i] * weight
        reduced.append(carried)
        weights.append(weight)
    solved = carry_solve(weight, carried, reduced, weights, modified)
    finished = jnp.transpose(solved.reshape(rows_here, 3, 32, -1), (1, 0, 2, 3))
    return (finished.reshape(velocity.shape), advection)


def solution(mesh):
    return jax.shard_map(
        shards,
        mesh=mesh,
        in_specs=(P(None, "gy", None, "gx"), P(None, "gy", None, "gx"), P("gy"), P("gy")),
        out_specs=(P(None, "gy", None, "gx"), P(None, "gy", None, "gx")),
        check_vma=False,
    )
```

```python
import functools

import jax
import jax.numpy as jnp
from jax import lax
from jax.sharding import PartitionSpec as P
from jax.experimental import pallas as pl
from jax.experimental.pallas import tpu as pltpu

MESH = pl.DeviceIdType.MESH
LINES = 96

STIFF = 1024


STENCIL = (0.8, -0.2, 4.0 / 105.0, -1.0 / 280.0)
GAMMA = 5.0 / 12.0
ZETA = -17.0 / 60.0


def extended(array, sides, width, wrap):
    for axis, dim in sides:
        size, length = (lax.axis_size(axis), array.shape[dim])
        up = [(i, (i + 1) % size) for i in range(size if wrap else size - 1)]
        down = [(j, i) for i, j in up]
        last = lax.slice_in_dim(array, length - width, length, axis=dim)
        first = lax.slice_in_dim(array, 0, width, axis=dim)
        before = lax.ppermute(last, axis, up)
        after = lax.ppermute(first, axis, down)
        array = jnp.concatenate([before, array, after], axis=dim)
    return array


def prefix(value, axis, join, neutral, backward):
    count, mine = (lax.axis_size(axis), lax.axis_index(axis))
    step = -1 if backward else 1
    order = [(i, i + step) for i in range(count) if 0 <= i + step < count]
    total = jax.tree.map(lambda part: lax.ppermute(part, axis, order), value)
    inside = (mine >= 1) if not backward else (mine <= count - 2)
    total = jax.tree.map(
        lambda part, zero: jnp.where(inside, part, jnp.full_like(part, 0) + jnp.asarray(zero, part.dtype)),
        total,
        neutral,
    )
    offset = 1
    while offset < count:
        pairs = [(i, i + step * offset) for i in range(count) if 0 <= i + step * offset < count]
        earlier = jax.tree.map(lambda part: lax.ppermute(part, axis, pairs), total)
        longer = join(earlier, total)
        reach = (mine >= offset) if not backward else (mine <= count - 1 - offset)
        total = jax.tree.map(lambda new, old: jnp.where(reach, new, old), longer, total)
        offset *= 2
    return total


def ratio_join(earlier, latter):
    def entry(i, j):
        return latter[2 * i : 2 * i + 1] * earlier[j : j + 1] + latter[2 * i + 1 : 2 * i + 2] * earlier[2 + j : 3 + j]

    entries = [entry(0, 0), entry(0, 1), entry(1, 0), entry(1, 1)]
    big = jnp.maximum(
        jnp.maximum(jnp.abs(entries[0]), jnp.abs(entries[1])),
        jnp.maximum(jnp.abs(entries[2]), jnp.abs(entries[3])),
    )
    rows = [part / big for part in entries]
    return jnp.concatenate(rows + [jnp.zeros((4, 128), jnp.float32)], axis=0)


def line_join(earlier, latter):
    factor = latter[LINES : LINES + 1, :]
    joined_lines = latter[:LINES] + factor * earlier[:LINES]
    joined_scale = latter[LINES:] * earlier[LINES:]
    return jnp.concatenate([joined_lines, joined_scale], axis=0)


def ratio_neutral():
    unit = jnp.ones((1, 128), jnp.float32)
    blank = jnp.zeros((1, 128), jnp.float32)
    return jnp.concatenate([unit, blank, blank, unit, blank, blank, blank, blank], axis=0)


def line_neutral():
    return jnp.concatenate([jnp.zeros((LINES, 128), jnp.float32), jnp.ones((8, 128), jnp.float32)], axis=0)


def scan_kernel(count, backward, join, neutral, x_ref, out_ref, totals, recv, send_sem, recv_sem):
    me = lax.axis_index("gy")
    row = lax.axis_index("gx")
    sign = -1 if backward else 1
    offsets = [1]
    while offsets[-1] * 2 < count:
        offsets.append(offsets[-1] * 2)
    partners = []
    for offset in offsets:
        partners.append((me + offset) % count)
        if 2 * offset != count:
            partners.append((me + count - offset) % count)
    barrier = pltpu.get_barrier_semaphore()
    for partner in partners:
        pl.semaphore_signal(barrier, inc=1, device_id=(row, partner), device_id_type=MESH)
    pl.semaphore_wait(barrier, len(partners))
    rounds = [1] + offsets
    copies = []
    for step, offset in enumerate(rounds):
        source = x_ref if step == 0 else totals.at[step - 1]
        target = (me + count + sign * offset) % count
        copy = pltpu.make_async_remote_copy(
            src_ref=source,
            dst_ref=recv.at[step],
            send_sem=send_sem.at[step],
            recv_sem=recv_sem.at[step],
            device_id=(row, target),
            device_id_type=MESH,
        )
        copy.start()
        copy.wait_recv()
        copies.append(copy)
        valid = (me + offset <= count - 1) if backward else (me >= offset)
        earlier = recv[step]
        if step == 0:
            totals[step] = jnp.where(valid, earlier, neutral())
        else:
            latter = totals[step - 1]
            totals[step] = jnp.where(valid, join(earlier, latter), latter)
    out_ref[...] = totals[len(rounds) - 1]
    for copy in copies:
        copy.wait_send()


def line_scan(step_value, backward):
    count = lax.axis_size("gy")
    factor, lines = step_value
    shape = lines.shape
    packed = jnp.concatenate(
        [lines.reshape(LINES, 128), jnp.broadcast_to(factor.reshape(1, 1), (8, 128))], axis=0
    )
    rounds = 1
    while (1 << (rounds - 1)) * 2 < count:
        rounds += 1
    rounds += 1
    result = pl.pallas_call(
        functools.partial(scan_kernel, count, backward, line_join, line_neutral),
        out_shape=jax.ShapeDtypeStruct(packed.shape, jnp.float32),
        in_specs=[pl.BlockSpec(memory_space=pltpu.VMEM)],
        out_specs=pl.BlockSpec(memory_space=pltpu.VMEM),
        scratch_shapes=[
            pltpu.VMEM((rounds,) + packed.shape, jnp.float32),
            pltpu.VMEM((rounds,) + packed.shape, jnp.float32),
            pltpu.SemaphoreType.DMA((rounds,)),
            pltpu.SemaphoreType.DMA((rounds,)),
        ],
        compiler_params=pltpu.CompilerParams(collective_id=1 if backward else 0, has_side_effects=True),
    )(packed)
    return result[:LINES].reshape(shape)


def ratio_scan(matrix):
    count = lax.axis_size("gy")
    packed = jnp.concatenate(
        [jnp.broadcast_to(matrix.reshape(4, 1), (4, 128)), jnp.zeros((4, 128), jnp.float32)], axis=0
    )
    rounds = 1
    while (1 << (rounds - 1)) * 2 < count:
        rounds += 1
    rounds += 1
    result = pl.pallas_call(
        functools.partial(scan_kernel, count, False, ratio_join, ratio_neutral),
        out_shape=jax.ShapeDtypeStruct(packed.shape, jnp.float32),
        in_specs=[pl.BlockSpec(memory_space=pltpu.VMEM)],
        out_specs=pl.BlockSpec(memory_space=pltpu.VMEM),
        scratch_shapes=[
            pltpu.VMEM((rounds,) + packed.shape, jnp.float32),
            pltpu.VMEM((rounds,) + packed.shape, jnp.float32),
            pltpu.SemaphoreType.DMA((rounds,)),
            pltpu.SemaphoreType.DMA((rounds,)),
        ],
        compiler_params=pltpu.CompilerParams(collective_id=2, has_side_effects=True),
    )(packed)
    return result[:4, 0].reshape(2, 2)


def prefix_kernel(count, pieces_ref, out_ref):
    mine = lax.axis_index("gy")

    def turn(position, total):
        piece = pieces_ref[pl.ds(pl.multiple_of(position * 8, 8), 8), :]
        entries = [
            piece[2 * i : 2 * i + 1] * total[j] + piece[2 * i + 1 : 2 * i + 2] * total[2 + j]
            for i in range(2)
            for j in range(2)
        ]
        big = jnp.maximum(
            jnp.maximum(jnp.abs(entries[0]), jnp.abs(entries[1])),
            jnp.maximum(jnp.abs(entries[2]), jnp.abs(entries[3])),
        )
        inside = position < mine
        return tuple(jnp.where(inside, value / big, old) for value, old in zip(entries, total))

    unit = jnp.ones((1, 128), jnp.float32)
    blank = jnp.zeros((1, 128), jnp.float32)
    total = lax.fori_loop(0, count - 1, turn, (unit, blank, blank, unit))
    out_ref[...] = jnp.broadcast_to(total[1] / total[3], (8, 128))


def ratio_prefix(matrix):
    count = lax.axis_size("gy")
    pieces = lax.all_gather(matrix, "gy")
    padded = jnp.concatenate([pieces, jnp.zeros((count, 4), jnp.float32)], axis=1)
    spread = jnp.broadcast_to(padded.reshape(count * 8, 1), (count * 8, 128))
    result = pl.pallas_call(
        functools.partial(prefix_kernel, count),
        out_shape=jax.ShapeDtypeStruct((8, 128), jnp.float32),
        in_specs=[pl.BlockSpec(memory_space=pltpu.VMEM)],
        out_specs=pl.BlockSpec(memory_space=pltpu.VMEM),
    )(spread)
    return result[0, 0]


def stream_slope(padded, planes):
    summed = STENCIL[0] * (padded[..., 5 : 5 + planes] - padded[..., 3 : 3 + planes])
    for offset in range(2, 5):
        summed = summed + STENCIL[offset - 1] * (
            padded[..., 4 + offset : 4 + offset + planes]
            - padded[..., 4 - offset : 4 - offset + planes]
        )
    return summed


def roll_slope(values, along_axis):
    summed = STENCIL[0] * (jnp.roll(values, -1, along_axis) - jnp.roll(values, 1, along_axis))
    for offset in range(2, 5):
        summed = summed + STENCIL[offset - 1] * (
            jnp.roll(values, -offset, along_axis) - jnp.roll(values, offset, along_axis)
        )
    return summed


def compose(earlier, latter):
    return (latter[0] * earlier[0], latter[1] + latter[0] * earlier[1])


def chain_ratio(earlier, latter):
    product = jnp.dot(latter, earlier, precision=lax.Precision.HIGHEST)
    return product / jnp.max(jnp.abs(product))


def ratio_matrix(cross_term, top_right, bottom_left):
    unit_entry = jnp.ones((), jnp.float32)
    return jnp.stack([jnp.stack([cross_term, top_right]), jnp.stack([bottom_left, unit_entry])])


def radix_plan(count):
    plan = [list(range(1, min(4, count - 1) + 1))]
    span = len(plan[0])
    while span < count - 1:
        offsets = [span * j for j in range(1, 4) if span * j < count]
        plan.append(offsets)
        span = span * (1 + len(offsets))
    return plan


def radix_scan(me, row, count, backward, element, parts, recv, send_sem, recv_sem, base, copies):
    sign = -1 if backward else 1
    plan = radix_plan(count)
    slot = base
    for level, offsets in enumerate(plan):
        source = element if level == 0 else parts.at[level - 1]
        started = []
        for offset in offsets:
            target = (me + count + sign * offset) % count
            copy = pltpu.make_async_remote_copy(
                src_ref=source,
                dst_ref=recv.at[slot],
                send_sem=send_sem.at[slot],
                recv_sem=recv_sem.at[slot],
                device_id=(row, target),
                device_id_type=MESH,
            )
            copy.start()
            started.append((offset, slot, copy))
            slot += 1
        acc = line_neutral() if level == 0 else parts[level - 1]
        for offset, index, copy in started:
            copy.wait_recv()
            copies.append(copy)
            valid = (me + offset <= count - 1) if backward else (me >= offset)
            acc = jnp.where(valid, line_join(recv[index], acc), acc)
        parts[level] = acc
    return parts[len(plan) - 1]


def carry_kernel(count, rows_here, element_ref, rows_ref, coef_ref, out_ref, parts_down, up_element, parts_up,
                 recv, send_sem, recv_sem):
    me = lax.axis_index("gy")
    row = lax.axis_index("gx")
    plan = radix_plan(count)
    residues = set()
    for offsets in plan:
        for offset in offsets:
            residues.add(offset % count)
            residues.add((count - offset) % count)
    residues.discard(0)
    barrier = pltpu.get_barrier_semaphore()
    for residue in sorted(residues):
        pl.semaphore_signal(barrier, inc=1, device_id=(row, (me + residue) % count), device_id_type=MESH)
    pl.semaphore_wait(barrier, len(residues))
    copies = []
    slots = sum(len(offsets) for offsets in plan)

    below_carry = radix_scan(
        me, row, count, False, element_ref, parts_down, recv, send_sem, recv_sem, 0, copies
    )[:LINES]
    coef = coef_ref[...]
    carried = None
    weight = None
    for i in reversed(range(rows_here)):
        sensitivity = coef[i : i + 1]
        modified = coef[16 + i : 17 + i]
        reduced = rows_ref[i] + sensitivity * below_carry
        if carried is None:
            carried = reduced
            weight = -modified
        else:
            carried = reduced - modified * carried
            weight = -modified * weight
        out_ref[i] = carried
    up_element[...] = jnp.concatenate([carried, jnp.broadcast_to(weight, (8, 128))], axis=0)
    above_carry = radix_scan(
        me, row, count, True, up_element, parts_up, recv, send_sem, recv_sem, slots, copies
    )[:LINES]
    weight = None
    for i in reversed(range(rows_here)):
        modified = coef[16 + i : 17 + i]
        weight = -modified if weight is None else -modified * weight
        out_ref[i] = out_ref[i] + weight * above_carry
    for copy in copies:
        copy.wait_send()


def carry_solve(element_factor, element_lines, rows, sensitivities, modified):
    count = lax.axis_size("gy")
    rows_here = len(rows)
    packed = jnp.concatenate(
        [element_lines.reshape(LINES, 128), jnp.broadcast_to(element_factor.reshape(1, 1), (8, 128))], axis=0
    )
    stacked = jnp.stack([value.reshape(LINES, 128) for value in rows], axis=0)
    scalars = (
        [jnp.reshape(value, (1,)) for value in sensitivities]
        + [jnp.zeros((16 - rows_here,), jnp.float32)]
        + [jnp.reshape(value, (1,)) for value in modified]
        + [jnp.zeros((16 - rows_here,), jnp.float32)]
    )
    coef = jnp.broadcast_to(jnp.concatenate(scalars).reshape(32, 1), (32, 128))
    plan = radix_plan(count)
    slots = 2 * sum(len(offsets) for offsets in plan)
    big = (LINES + 8, 128)
    return pl.pallas_call(
        functools.partial(carry_kernel, count, rows_here),
        out_shape=jax.ShapeDtypeStruct((rows_here, LINES, 128), jnp.float32),
        in_specs=[pl.BlockSpec(memory_space=pltpu.VMEM)] * 3,
        out_specs=pl.BlockSpec(memory_space=pltpu.VMEM),
        scratch_shapes=[
            pltpu.VMEM((len(plan),) + big, jnp.float32),
            pltpu.VMEM(big, jnp.float32),
            pltpu.VMEM((len(plan),) + big, jnp.float32),
            pltpu.VMEM((slots,) + big, jnp.float32),
            pltpu.SemaphoreType.DMA((slots,)),
            pltpu.SemaphoreType.DMA((slots,)),
        ],
        compiler_params=pltpu.CompilerParams(collective_id=0, has_side_effects=True),
    )(packed, stacked, coef)


def shards(velocity, old_advection, lower_gap, upper_gap):
    planes = velocity.shape[3]
    padded = extended(velocity, (("gx", 3),), 4, True)
    stream = stream_slope(padded, planes)
    spanwise = roll_slope(velocity, 2)
    rimmed = extended(velocity, (("gy", 1),), 1, False)
    gap_sum = lower_gap + upper_gap
    normal_slope = (rimmed[:, 2:] - rimmed[:, :-2]) / gap_sum[None, :, None, None]
    advection = -(
        velocity[0][None] * stream + velocity[1][None] * normal_slope + velocity[2][None] * spanwise
    )
    forcing = velocity + GAMMA * advection + ZETA * old_advection
    lower_coef = -2.0 * STIFF / (gap_sum * lower_gap)
    upper_coef = -2.0 * STIFF / (gap_sum * upper_gap)
    diagonal = 1.0 - lower_coef - upper_coef
    rows_here = velocity.shape[1]

    top = (jnp.ones((), jnp.float32), jnp.zeros((), jnp.float32))
    bottom = (jnp.zeros((), jnp.float32), jnp.ones((), jnp.float32))
    for i in range(rows_here):
        scale = 1.0 / diagonal[i]
        up, low = upper_coef[i] * scale, -lower_coef[i] * scale
        top, bottom = (
            (up * bottom[0], up * bottom[1]),
            (low * top[0] + bottom[0], low * top[1] + bottom[1]),
        )
    big = jnp.maximum(
        jnp.maximum(jnp.abs(top[0]), jnp.abs(top[1])), jnp.maximum(jnp.abs(bottom[0]), jnp.abs(bottom[1]))
    )
    matrix = jnp.stack([top[0], top[1], bottom[0], bottom[1]]) / big
    modified_prev = ratio_prefix(matrix)

    pivots, modified = [], []
    for i in range(rows_here):
        pivot = diagonal[i] - lower_coef[i] * modified_prev
        modified_prev = upper_coef[i] / pivot
        pivots.append(pivot)
        modified.append(modified_prev)

    line_rows = forcing.reshape(3, rows_here, -1)
    zero_lines = jnp.zeros_like(line_rows[:, 0])
    carried = zero_lines
    weight = jnp.ones((), jnp.float32)
    reduced, weights = [], []
    for i in range(rows_here):
        carried = (line_rows[:, i] - lower_coef[i] * carried) / pivots[i]
        weight = -lower_coef[i] / pivots[i] * weight
        reduced.append(carried)
        weights.append(weight)
    solved = carry_solve(weight, carried, reduced, weights, modified)
    finished = jnp.transpose(solved.reshape(rows_here, 3, 32, -1), (1, 0, 2, 3))
    return (finished.reshape(velocity.shape), advection)


def solution(mesh):
    return jax.shard_map(
        shards,
        mesh=mesh,
        in_specs=(P(None, "gy", None, "gx"), P(None, "gy", None, "gx"), P("gy"), P("gy")),
        out_specs=(P(None, "gy", None, "gx"), P(None, "gy", None, "gx")),
        check_vma=False,
    )
```

```python
import functools

import jax
import jax.numpy as jnp
from jax import lax
from jax.sharding import PartitionSpec as P
from jax.experimental import pallas as pl
from jax.experimental.pallas import tpu as pltpu

MESH = pl.DeviceIdType.MESH
LINES = 96

STIFF = 1024


STENCIL = (0.8, -0.2, 4.0 / 105.0, -1.0 / 280.0)
GAMMA = 5.0 / 12.0
ZETA = -17.0 / 60.0


def extended(array, sides, width, wrap):
    for axis, dim in sides:
        size, length = (lax.axis_size(axis), array.shape[dim])
        up = [(i, (i + 1) % size) for i in range(size if wrap else size - 1)]
        down = [(j, i) for i, j in up]
        last = lax.slice_in_dim(array, length - width, length, axis=dim)
        first = lax.slice_in_dim(array, 0, width, axis=dim)
        before = lax.ppermute(last, axis, up)
        after = lax.ppermute(first, axis, down)
        array = jnp.concatenate([before, array, after], axis=dim)
    return array


def prefix(value, axis, join, neutral, backward):
    count, mine = (lax.axis_size(axis), lax.axis_index(axis))
    step = -1 if backward else 1
    order = [(i, i + step) for i in range(count) if 0 <= i + step < count]
    total = jax.tree.map(lambda part: lax.ppermute(part, axis, order), value)
    inside = (mine >= 1) if not backward else (mine <= count - 2)
    total = jax.tree.map(
        lambda part, zero: jnp.where(inside, part, jnp.full_like(part, 0) + jnp.asarray(zero, part.dtype)),
        total,
        neutral,
    )
    offset = 1
    while offset < count:
        pairs = [(i, i + step * offset) for i in range(count) if 0 <= i + step * offset < count]
        earlier = jax.tree.map(lambda part: lax.ppermute(part, axis, pairs), total)
        longer = join(earlier, total)
        reach = (mine >= offset) if not backward else (mine <= count - 1 - offset)
        total = jax.tree.map(lambda new, old: jnp.where(reach, new, old), longer, total)
        offset *= 2
    return total


def ratio_join(earlier, latter):
    def entry(i, j):
        return latter[2 * i : 2 * i + 1] * earlier[j : j + 1] + latter[2 * i + 1 : 2 * i + 2] * earlier[2 + j : 3 + j]

    entries = [entry(0, 0), entry(0, 1), entry(1, 0), entry(1, 1)]
    big = jnp.maximum(
        jnp.maximum(jnp.abs(entries[0]), jnp.abs(entries[1])),
        jnp.maximum(jnp.abs(entries[2]), jnp.abs(entries[3])),
    )
    rows = [part / big for part in entries]
    return jnp.concatenate(rows + [jnp.zeros((4, 128), jnp.float32)], axis=0)


def line_join(earlier, latter):
    factor = latter[LINES : LINES + 1, :]
    joined_lines = latter[:LINES] + factor * earlier[:LINES]
    joined_scale = latter[LINES:] * earlier[LINES:]
    return jnp.concatenate([joined_lines, joined_scale], axis=0)


def ratio_neutral():
    unit = jnp.ones((1, 128), jnp.float32)
    blank = jnp.zeros((1, 128), jnp.float32)
    return jnp.concatenate([unit, blank, blank, unit, blank, blank, blank, blank], axis=0)


def line_neutral():
    return jnp.concatenate([jnp.zeros((LINES, 128), jnp.float32), jnp.ones((8, 128), jnp.float32)], axis=0)


def scan_kernel(count, backward, join, neutral, x_ref, out_ref, totals, recv, send_sem, recv_sem):
    me = lax.axis_index("gy")
    row = lax.axis_index("gx")
    sign = -1 if backward else 1
    offsets = [1]
    while offsets[-1] * 2 < count:
        offsets.append(offsets[-1] * 2)
    partners = []
    for offset in offsets:
        partners.append((me + offset) % count)
        if 2 * offset != count:
            partners.append((me + count - offset) % count)
    barrier = pltpu.get_barrier_semaphore()
    for partner in partners:
        pl.semaphore_signal(barrier, inc=1, device_id=(row, partner), device_id_type=MESH)
    pl.semaphore_wait(barrier, len(partners))
    rounds = [1] + offsets
    copies = []
    for step, offset in enumerate(rounds):
        source = x_ref if step == 0 else totals.at[step - 1]
        target = (me + count + sign * offset) % count
        copy = pltpu.make_async_remote_copy(
            src_ref=source,
            dst_ref=recv.at[step],
            send_sem=send_sem.at[step],
            recv_sem=recv_sem.at[step],
            device_id=(row, target),
            device_id_type=MESH,
        )
        copy.start()
        copy.wait_recv()
        copies.append(copy)
        valid = (me + offset <= count - 1) if backward else (me >= offset)
        earlier = recv[step]
        if step == 0:
            totals[step] = jnp.where(valid, earlier, neutral())
        else:
            latter = totals[step - 1]
            totals[step] = jnp.where(valid, join(earlier, latter), latter)
    out_ref[...] = totals[len(rounds) - 1]
    for copy in copies:
        copy.wait_send()


def line_scan(step_value, backward):
    count = lax.axis_size("gy")
    factor, lines = step_value
    shape = lines.shape
    packed = jnp.concatenate(
        [lines.reshape(LINES, 128), jnp.broadcast_to(factor.reshape(1, 1), (8, 128))], axis=0
    )
    rounds = 1
    while (1 << (rounds - 1)) * 2 < count:
        rounds += 1
    rounds += 1
    result = pl.pallas_call(
        functools.partial(scan_kernel, count, backward, line_join, line_neutral),
        out_shape=jax.ShapeDtypeStruct(packed.shape, jnp.float32),
        in_specs=[pl.BlockSpec(memory_space=pltpu.VMEM)],
        out_specs=pl.BlockSpec(memory_space=pltpu.VMEM),
        scratch_shapes=[
            pltpu.VMEM((rounds,) + packed.shape, jnp.float32),
            pltpu.VMEM((rounds,) + packed.shape, jnp.float32),
            pltpu.SemaphoreType.DMA((rounds,)),
            pltpu.SemaphoreType.DMA((rounds,)),
        ],
        compiler_params=pltpu.CompilerParams(collective_id=1 if backward else 0, has_side_effects=True),
    )(packed)
    return result[:LINES].reshape(shape)


def ratio_scan(matrix):
    count = lax.axis_size("gy")
    packed = jnp.concatenate(
        [jnp.broadcast_to(matrix.reshape(4, 1), (4, 128)), jnp.zeros((4, 128), jnp.float32)], axis=0
    )
    rounds = 1
    while (1 << (rounds - 1)) * 2 < count:
        rounds += 1
    rounds += 1
    result = pl.pallas_call(
        functools.partial(scan_kernel, count, False, ratio_join, ratio_neutral),
        out_shape=jax.ShapeDtypeStruct(packed.shape, jnp.float32),
        in_specs=[pl.BlockSpec(memory_space=pltpu.VMEM)],
        out_specs=pl.BlockSpec(memory_space=pltpu.VMEM),
        scratch_shapes=[
            pltpu.VMEM((rounds,) + packed.shape, jnp.float32),
            pltpu.VMEM((rounds,) + packed.shape, jnp.float32),
            pltpu.SemaphoreType.DMA((rounds,)),
            pltpu.SemaphoreType.DMA((rounds,)),
        ],
        compiler_params=pltpu.CompilerParams(collective_id=2, has_side_effects=True),
    )(packed)
    return result[:4, 0].reshape(2, 2)


def prefix_kernel(count, element_ref, out_ref, pieces, send_sem, recv_sem):
    mine = lax.axis_index("gy")
    row = lax.axis_index("gx")
    barrier = pltpu.get_barrier_semaphore()

    def greet(step, carry):
        pl.semaphore_signal(barrier, inc=1, device_id=(row, (mine + step) % count), device_id_type=MESH)
        return carry

    lax.fori_loop(1, count, greet, 0)
    pl.semaphore_wait(barrier, count - 1)

    def outgoing(step):
        return pltpu.make_async_remote_copy(
            src_ref=element_ref,
            dst_ref=pieces.at[mine],
            send_sem=send_sem.at[step],
            recv_sem=recv_sem.at[mine],
            device_id=(row, (mine + step) % count),
            device_id_type=MESH,
        )

    def incoming(step):
        source = (mine + count - step) % count
        return pltpu.make_async_remote_copy(
            src_ref=element_ref,
            dst_ref=pieces.at[source],
            send_sem=send_sem.at[step],
            recv_sem=recv_sem.at[source],
            device_id=(row, source),
            device_id_type=MESH,
        )

    def send(step, carry):
        outgoing(step).start()
        return carry

    def arrive(step, carry):
        incoming(step).wait_recv()
        return carry

    def drain(step, carry):
        outgoing(step).wait_send()
        return carry

    lax.fori_loop(1, count, send, 0)
    lax.fori_loop(1, count, arrive, 0)
    pieces[mine] = element_ref[...]

    def turn(position, total):
        piece = pieces[position]
        entries = [
            piece[2 * i : 2 * i + 1] * total[j] + piece[2 * i + 1 : 2 * i + 2] * total[2 + j]
            for i in range(2)
            for j in range(2)
        ]
        big = jnp.maximum(
            jnp.maximum(jnp.abs(entries[0]), jnp.abs(entries[1])),
            jnp.maximum(jnp.abs(entries[2]), jnp.abs(entries[3])),
        )
        inside = position < mine
        return tuple(jnp.where(inside, value / big, old) for value, old in zip(entries, total))

    unit = jnp.ones((1, 128), jnp.float32)
    blank = jnp.zeros((1, 128), jnp.float32)
    total = lax.fori_loop(0, count - 1, turn, (unit, blank, blank, unit))
    out_ref[...] = jnp.broadcast_to(total[1] / total[3], (8, 128))
    lax.fori_loop(1, count, drain, 0)


def ratio_prefix(matrix):
    count = lax.axis_size("gy")
    element = jnp.broadcast_to(
        jnp.concatenate([matrix, jnp.zeros((4,), jnp.float32)]).reshape(8, 1), (8, 128)
    )
    result = pl.pallas_call(
        functools.partial(prefix_kernel, count),
        out_shape=jax.ShapeDtypeStruct((8, 128), jnp.float32),
        in_specs=[pl.BlockSpec(memory_space=pltpu.VMEM)],
        out_specs=pl.BlockSpec(memory_space=pltpu.VMEM),
        scratch_shapes=[
            pltpu.VMEM((count, 8, 128), jnp.float32),
            pltpu.SemaphoreType.DMA((count,)),
            pltpu.SemaphoreType.DMA((count,)),
        ],
        compiler_params=pltpu.CompilerParams(collective_id=1, has_side_effects=True),
    )(element)
    return result[0, 0]


def stream_slope(padded, planes):
    summed = STENCIL[0] * (padded[..., 5 : 5 + planes] - padded[..., 3 : 3 + planes])
    for offset in range(2, 5):
        summed = summed + STENCIL[offset - 1] * (
            padded[..., 4 + offset : 4 + offset + planes]
            - padded[..., 4 - offset : 4 - offset + planes]
        )
    return summed


def roll_slope(values, along_axis):
    summed = STENCIL[0] * (jnp.roll(values, -1, along_axis) - jnp.roll(values, 1, along_axis))
    for offset in range(2, 5):
        summed = summed + STENCIL[offset - 1] * (
            jnp.roll(values, -offset, along_axis) - jnp.roll(values, offset, along_axis)
        )
    return summed


def compose(earlier, latter):
    return (latter[0] * earlier[0], latter[1] + latter[0] * earlier[1])


def chain_ratio(earlier, latter):
    product = jnp.dot(latter, earlier, precision=lax.Precision.HIGHEST)
    return product / jnp.max(jnp.abs(product))


def ratio_matrix(cross_term, top_right, bottom_left):
    unit_entry = jnp.ones((), jnp.float32)
    return jnp.stack([jnp.stack([cross_term, top_right]), jnp.stack([bottom_left, unit_entry])])


def radix_plan(count):
    plan = [list(range(1, min(4, count - 1) + 1))]
    span = len(plan[0])
    while span < count - 1:
        offsets = [span * j for j in range(1, 4) if span * j < count]
        plan.append(offsets)
        span = span * (1 + len(offsets))
    return plan


def radix_scan(me, row, count, backward, element, parts, recv, send_sem, recv_sem, base, copies):
    sign = -1 if backward else 1
    plan = radix_plan(count)
    slot = base
    for level, offsets in enumerate(plan):
        source = element if level == 0 else parts.at[level - 1]
        started = []
        for offset in offsets:
            target = (me + count + sign * offset) % count
            copy = pltpu.make_async_remote_copy(
                src_ref=source,
                dst_ref=recv.at[slot],
                send_sem=send_sem.at[slot],
                recv_sem=recv_sem.at[slot],
                device_id=(row, target),
                device_id_type=MESH,
            )
            copy.start()
            started.append((offset, slot, copy))
            slot += 1
        acc = line_neutral() if level == 0 else parts[level - 1]
        for offset, index, copy in started:
            copy.wait_recv()
            copies.append(copy)
            valid = (me + offset <= count - 1) if backward else (me >= offset)
            acc = jnp.where(valid, line_join(recv[index], acc), acc)
        parts[level] = acc
    return parts[len(plan) - 1]


def carry_kernel(count, rows_here, element_ref, rows_ref, coef_ref, out_ref, parts_down, up_element, parts_up,
                 recv, send_sem, recv_sem):
    me = lax.axis_index("gy")
    row = lax.axis_index("gx")
    plan = radix_plan(count)
    residues = set()
    for offsets in plan:
        for offset in offsets:
            residues.add(offset % count)
            residues.add((count - offset) % count)
    residues.discard(0)
    barrier = pltpu.get_barrier_semaphore()
    for residue in sorted(residues):
        pl.semaphore_signal(barrier, inc=1, device_id=(row, (me + residue) % count), device_id_type=MESH)
    pl.semaphore_wait(barrier, len(residues))
    copies = []
    slots = sum(len(offsets) for offsets in plan)

    below_carry = radix_scan(
        me, row, count, False, element_ref, parts_down, recv, send_sem, recv_sem, 0, copies
    )[:LINES]
    coef = coef_ref[...]
    carried = None
    weight = None
    for i in reversed(range(rows_here)):
        sensitivity = coef[i : i + 1]
        modified = coef[16 + i : 17 + i]
        reduced = rows_ref[i] + sensitivity * below_carry
        if carried is None:
            carried = reduced
            weight = -modified
        else:
            carried = reduced - modified * carried
            weight = -modified * weight
        out_ref[i] = carried
    up_element[...] = jnp.concatenate([carried, jnp.broadcast_to(weight, (8, 128))], axis=0)
    above_carry = radix_scan(
        me, row, count, True, up_element, parts_up, recv, send_sem, recv_sem, slots, copies
    )[:LINES]
    weight = None
    for i in reversed(range(rows_here)):
        modified = coef[16 + i : 17 + i]
        weight = -modified if weight is None else -modified * weight
        out_ref[i] = out_ref[i] + weight * above_carry
    for copy in copies:
        copy.wait_send()


def carry_solve(element_factor, element_lines, rows, sensitivities, modified):
    count = lax.axis_size("gy")
    rows_here = len(rows)
    packed = jnp.concatenate(
        [element_lines.reshape(LINES, 128), jnp.broadcast_to(element_factor.reshape(1, 1), (8, 128))], axis=0
    )
    stacked = jnp.stack([value.reshape(LINES, 128) for value in rows], axis=0)
    scalars = (
        [jnp.reshape(value, (1,)) for value in sensitivities]
        + [jnp.zeros((16 - rows_here,), jnp.float32)]
        + [jnp.reshape(value, (1,)) for value in modified]
        + [jnp.zeros((16 - rows_here,), jnp.float32)]
    )
    coef = jnp.broadcast_to(jnp.concatenate(scalars).reshape(32, 1), (32, 128))
    plan = radix_plan(count)
    slots = 2 * sum(len(offsets) for offsets in plan)
    big = (LINES + 8, 128)
    return pl.pallas_call(
        functools.partial(carry_kernel, count, rows_here),
        out_shape=jax.ShapeDtypeStruct((rows_here, LINES, 128), jnp.float32),
        in_specs=[pl.BlockSpec(memory_space=pltpu.VMEM)] * 3,
        out_specs=pl.BlockSpec(memory_space=pltpu.VMEM),
        scratch_shapes=[
            pltpu.VMEM((len(plan),) + big, jnp.float32),
            pltpu.VMEM(big, jnp.float32),
            pltpu.VMEM((len(plan),) + big, jnp.float32),
            pltpu.VMEM((slots,) + big, jnp.float32),
            pltpu.SemaphoreType.DMA((slots,)),
            pltpu.SemaphoreType.DMA((slots,)),
        ],
        compiler_params=pltpu.CompilerParams(collective_id=0, has_side_effects=True),
    )(packed, stacked, coef)


def shards(velocity, old_advection, lower_gap, upper_gap):
    planes = velocity.shape[3]
    padded = extended(velocity, (("gx", 3),), 4, True)
    stream = stream_slope(padded, planes)
    spanwise = roll_slope(velocity, 2)
    rimmed = extended(velocity, (("gy", 1),), 1, False)
    gap_sum = lower_gap + upper_gap
    normal_slope = (rimmed[:, 2:] - rimmed[:, :-2]) / gap_sum[None, :, None, None]
    advection = -(
        velocity[0][None] * stream + velocity[1][None] * normal_slope + velocity[2][None] * spanwise
    )
    forcing = velocity + GAMMA * advection + ZETA * old_advection
    lower_coef = -2.0 * STIFF / (gap_sum * lower_gap)
    upper_coef = -2.0 * STIFF / (gap_sum * upper_gap)
    diagonal = 1.0 - lower_coef - upper_coef
    rows_here = velocity.shape[1]

    top = (jnp.ones((), jnp.float32), jnp.zeros((), jnp.float32))
    bottom = (jnp.zeros((), jnp.float32), jnp.ones((), jnp.float32))
    for i in range(rows_here):
        scale = 1.0 / diagonal[i]
        up, low = upper_coef[i] * scale, -lower_coef[i] * scale
        top, bottom = (
            (up * bottom[0], up * bottom[1]),
            (low * top[0] + bottom[0], low * top[1] + bottom[1]),
        )
    big = jnp.maximum(
        jnp.maximum(jnp.abs(top[0]), jnp.abs(top[1])), jnp.maximum(jnp.abs(bottom[0]), jnp.abs(bottom[1]))
    )
    matrix = jnp.stack([top[0], top[1], bottom[0], bottom[1]]) / big
    modified_prev = ratio_prefix(matrix)

    pivots, modified = [], []
    for i in range(rows_here):
        pivot = diagonal[i] - lower_coef[i] * modified_prev
        modified_prev = upper_coef[i] / pivot
        pivots.append(pivot)
        modified.append(modified_prev)

    line_rows = forcing.reshape(3, rows_here, -1)
    zero_lines = jnp.zeros_like(line_rows[:, 0])
    carried = zero_lines
    weight = jnp.ones((), jnp.float32)
    reduced, weights = [], []
    for i in range(rows_here):
        carried = (line_rows[:, i] - lower_coef[i] * carried) / pivots[i]
        weight = -lower_coef[i] / pivots[i] * weight
        reduced.append(carried)
        weights.append(weight)
    solved = carry_solve(weight, carried, reduced, weights, modified)
    finished = jnp.transpose(solved.reshape(rows_here, 3, 32, -1), (1, 0, 2, 3))
    return (finished.reshape(velocity.shape), advection)


def solution(mesh):
    return jax.shard_map(
        shards,
        mesh=mesh,
        in_specs=(P(None, "gy", None, "gx"), P(None, "gy", None, "gx"), P("gy"), P("gy")),
        out_specs=(P(None, "gy", None, "gx"), P(None, "gy", None, "gx")),
        check_vma=False,
    )
```

```python
import functools

import jax
import jax.numpy as jnp
from jax import lax
from jax.sharding import PartitionSpec as P
from jax.experimental import pallas as pl
from jax.experimental.pallas import tpu as pltpu

MESH = pl.DeviceIdType.MESH
LINES = 96

STIFF = 1024


STENCIL = (0.8, -0.2, 4.0 / 105.0, -1.0 / 280.0)
GAMMA = 5.0 / 12.0
ZETA = -17.0 / 60.0


def extended(array, sides, width, wrap):
    for axis, dim in sides:
        size, length = (lax.axis_size(axis), array.shape[dim])
        up = [(i, (i + 1) % size) for i in range(size if wrap else size - 1)]
        down = [(j, i) for i, j in up]
        last = lax.slice_in_dim(array, length - width, length, axis=dim)
        first = lax.slice_in_dim(array, 0, width, axis=dim)
        before = lax.ppermute(last, axis, up)
        after = lax.ppermute(first, axis, down)
        array = jnp.concatenate([before, array, after], axis=dim)
    return array


def prefix(value, axis, join, neutral, backward):
    count, mine = (lax.axis_size(axis), lax.axis_index(axis))
    step = -1 if backward else 1
    order = [(i, i + step) for i in range(count) if 0 <= i + step < count]
    total = jax.tree.map(lambda part: lax.ppermute(part, axis, order), value)
    inside = (mine >= 1) if not backward else (mine <= count - 2)
    total = jax.tree.map(
        lambda part, zero: jnp.where(inside, part, jnp.full_like(part, 0) + jnp.asarray(zero, part.dtype)),
        total,
        neutral,
    )
    offset = 1
    while offset < count:
        pairs = [(i, i + step * offset) for i in range(count) if 0 <= i + step * offset < count]
        earlier = jax.tree.map(lambda part: lax.ppermute(part, axis, pairs), total)
        longer = join(earlier, total)
        reach = (mine >= offset) if not backward else (mine <= count - 1 - offset)
        total = jax.tree.map(lambda new, old: jnp.where(reach, new, old), longer, total)
        offset *= 2
    return total


def ratio_join(earlier, latter):
    def entry(i, j):
        return latter[2 * i : 2 * i + 1] * earlier[j : j + 1] + latter[2 * i + 1 : 2 * i + 2] * earlier[2 + j : 3 + j]

    entries = [entry(0, 0), entry(0, 1), entry(1, 0), entry(1, 1)]
    big = jnp.maximum(
        jnp.maximum(jnp.abs(entries[0]), jnp.abs(entries[1])),
        jnp.maximum(jnp.abs(entries[2]), jnp.abs(entries[3])),
    )
    rows = [part / big for part in entries]
    return jnp.concatenate(rows + [jnp.zeros((4, 128), jnp.float32)], axis=0)


def line_join(earlier, latter):
    factor = latter[LINES : LINES + 1, :]
    joined_lines = latter[:LINES] + factor * earlier[:LINES]
    joined_scale = latter[LINES:] * earlier[LINES:]
    return jnp.concatenate([joined_lines, joined_scale], axis=0)


def ratio_neutral():
    unit = jnp.ones((1, 128), jnp.float32)
    blank = jnp.zeros((1, 128), jnp.float32)
    return jnp.concatenate([unit, blank, blank, unit, blank, blank, blank, blank], axis=0)


def line_neutral():
    return jnp.concatenate([jnp.zeros((LINES, 128), jnp.float32), jnp.ones((8, 128), jnp.float32)], axis=0)


def scan_kernel(count, backward, join, neutral, x_ref, out_ref, totals, recv, send_sem, recv_sem):
    me = lax.axis_index("gy")
    row = lax.axis_index("gx")
    sign = -1 if backward else 1
    offsets = [1]
    while offsets[-1] * 2 < count:
        offsets.append(offsets[-1] * 2)
    partners = []
    for offset in offsets:
        partners.append((me + offset) % count)
        if 2 * offset != count:
            partners.append((me + count - offset) % count)
    barrier = pltpu.get_barrier_semaphore()
    for partner in partners:
        pl.semaphore_signal(barrier, inc=1, device_id=(row, partner), device_id_type=MESH)
    pl.semaphore_wait(barrier, len(partners))
    rounds = [1] + offsets
    copies = []
    for step, offset in enumerate(rounds):
        source = x_ref if step == 0 else totals.at[step - 1]
        target = (me + count + sign * offset) % count
        copy = pltpu.make_async_remote_copy(
            src_ref=source,
            dst_ref=recv.at[step],
            send_sem=send_sem.at[step],
            recv_sem=recv_sem.at[step],
            device_id=(row, target),
            device_id_type=MESH,
        )
        copy.start()
        copy.wait_recv()
        copies.append(copy)
        valid = (me + offset <= count - 1) if backward else (me >= offset)
        earlier = recv[step]
        if step == 0:
            totals[step] = jnp.where(valid, earlier, neutral())
        else:
            latter = totals[step - 1]
            totals[step] = jnp.where(valid, join(earlier, latter), latter)
    out_ref[...] = totals[len(rounds) - 1]
    for copy in copies:
        copy.wait_send()


def line_scan(step_value, backward):
    count = lax.axis_size("gy")
    factor, lines = step_value
    shape = lines.shape
    packed = jnp.concatenate(
        [lines.reshape(LINES, 128), jnp.broadcast_to(factor.reshape(1, 1), (8, 128))], axis=0
    )
    rounds = 1
    while (1 << (rounds - 1)) * 2 < count:
        rounds += 1
    rounds += 1
    result = pl.pallas_call(
        functools.partial(scan_kernel, count, backward, line_join, line_neutral),
        out_shape=jax.ShapeDtypeStruct(packed.shape, jnp.float32),
        in_specs=[pl.BlockSpec(memory_space=pltpu.VMEM)],
        out_specs=pl.BlockSpec(memory_space=pltpu.VMEM),
        scratch_shapes=[
            pltpu.VMEM((rounds,) + packed.shape, jnp.float32),
            pltpu.VMEM((rounds,) + packed.shape, jnp.float32),
            pltpu.SemaphoreType.DMA((rounds,)),
            pltpu.SemaphoreType.DMA((rounds,)),
        ],
        compiler_params=pltpu.CompilerParams(collective_id=1 if backward else 0, has_side_effects=True),
    )(packed)
    return result[:LINES].reshape(shape)


def ratio_scan(matrix):
    count = lax.axis_size("gy")
    packed = jnp.concatenate(
        [jnp.broadcast_to(matrix.reshape(4, 1), (4, 128)), jnp.zeros((4, 128), jnp.float32)], axis=0
    )
    rounds = 1
    while (1 << (rounds - 1)) * 2 < count:
        rounds += 1
    rounds += 1
    result = pl.pallas_call(
        functools.partial(scan_kernel, count, False, ratio_join, ratio_neutral),
        out_shape=jax.ShapeDtypeStruct(packed.shape, jnp.float32),
        in_specs=[pl.BlockSpec(memory_space=pltpu.VMEM)],
        out_specs=pl.BlockSpec(memory_space=pltpu.VMEM),
        scratch_shapes=[
            pltpu.VMEM((rounds,) + packed.shape, jnp.float32),
            pltpu.VMEM((rounds,) + packed.shape, jnp.float32),
            pltpu.SemaphoreType.DMA((rounds,)),
            pltpu.SemaphoreType.DMA((rounds,)),
        ],
        compiler_params=pltpu.CompilerParams(collective_id=2, has_side_effects=True),
    )(packed)
    return result[:4, 0].reshape(2, 2)


def prefix_kernel(count, rows_here, element_ref, table_ref, out_ref, pieces, send_sem, recv_sem):
    mine = lax.axis_index("gy")
    row = lax.axis_index("gx")
    barrier = pltpu.get_barrier_semaphore()

    def greet(step, carry):
        pl.semaphore_signal(barrier, inc=1, device_id=(row, (mine + step) % count), device_id_type=MESH)
        return carry

    lax.fori_loop(1, count, greet, 0)
    pl.semaphore_wait(barrier, count - 1)

    def outgoing(step):
        return pltpu.make_async_remote_copy(
            src_ref=element_ref,
            dst_ref=pieces.at[mine],
            send_sem=send_sem.at[step],
            recv_sem=recv_sem.at[mine],
            device_id=(row, (mine + step) % count),
            device_id_type=MESH,
        )

    def incoming(step):
        source = (mine + count - step) % count
        return pltpu.make_async_remote_copy(
            src_ref=element_ref,
            dst_ref=pieces.at[source],
            send_sem=send_sem.at[step],
            recv_sem=recv_sem.at[source],
            device_id=(row, source),
            device_id_type=MESH,
        )

    def send(step, carry):
        outgoing(step).start()
        return carry

    def arrive(step, carry):
        incoming(step).wait_recv()
        return carry

    def drain(step, carry):
        outgoing(step).wait_send()
        return carry

    lax.fori_loop(1, count, send, 0)
    lax.fori_loop(1, count, arrive, 0)
    pieces[mine] = element_ref[...]

    def turn(position, total):
        piece = pieces[position]
        entries = [
            piece[2 * i : 2 * i + 1] * total[j] + piece[2 * i + 1 : 2 * i + 2] * total[2 + j]
            for i in range(2)
            for j in range(2)
        ]
        big = jnp.maximum(
            jnp.maximum(jnp.abs(entries[0]), jnp.abs(entries[1])),
            jnp.maximum(jnp.abs(entries[2]), jnp.abs(entries[3])),
        )
        inside = position < mine
        return tuple(jnp.where(inside, value / big, old) for value, old in zip(entries, total))

    unit = jnp.ones((1, 128), jnp.float32)
    blank = jnp.zeros((1, 128), jnp.float32)
    total = lax.fori_loop(0, count - 1, turn, (unit, blank, blank, unit))
    modified_prev = total[1] / total[3]
    weight = unit
    for i in range(rows_here):
        lower = table_ref[i : i + 1]
        upper = table_ref[16 + i : 17 + i]
        diagonal = table_ref[32 + i : 33 + i]
        pivot = diagonal - lower * modified_prev
        modified_prev = upper / pivot
        weight = -lower / pivot * weight
        out_ref[i : i + 1] = pivot
        out_ref[16 + i : 17 + i] = modified_prev
        out_ref[32 + i : 33 + i] = weight
    lax.fori_loop(1, count, drain, 0)


def matrix_kernel(rows_here, table_ref, out_ref):
    unit = jnp.ones((1, 128), jnp.float32)
    blank = jnp.zeros((1, 128), jnp.float32)
    top = (unit, blank)
    bottom = (blank, unit)
    for i in range(rows_here):
        scale = 1.0 / table_ref[32 + i : 33 + i]
        up = table_ref[16 + i : 17 + i] * scale
        low = -table_ref[i : i + 1] * scale
        top, bottom = (
            (up * bottom[0], up * bottom[1]),
            (low * top[0] + bottom[0], low * top[1] + bottom[1]),
        )
    big = jnp.maximum(
        jnp.maximum(jnp.abs(top[0]), jnp.abs(top[1])), jnp.maximum(jnp.abs(bottom[0]), jnp.abs(bottom[1]))
    )
    out_ref[...] = jnp.concatenate(
        [top[0] / big, top[1] / big, bottom[0] / big, bottom[1] / big, blank, blank, blank, blank], axis=0
    )


def coefficient_table(lower_coef, upper_coef, diagonal):
    count = lax.axis_size("gy")
    rows_here = lower_coef.shape[0]
    filler = jnp.zeros((16 - rows_here,), jnp.float32)
    column = jnp.concatenate([lower_coef, filler, upper_coef, filler, diagonal, filler])
    table = jnp.broadcast_to(column.reshape(48, 1), (48, 128))
    element = pl.pallas_call(
        functools.partial(matrix_kernel, rows_here),
        out_shape=jax.ShapeDtypeStruct((8, 128), jnp.float32),
        in_specs=[pl.BlockSpec(memory_space=pltpu.VMEM)],
        out_specs=pl.BlockSpec(memory_space=pltpu.VMEM),
    )(table)
    return pl.pallas_call(
        functools.partial(prefix_kernel, count, rows_here),
        out_shape=jax.ShapeDtypeStruct((48, 128), jnp.float32),
        in_specs=[pl.BlockSpec(memory_space=pltpu.VMEM)] * 2,
        out_specs=pl.BlockSpec(memory_space=pltpu.VMEM),
        scratch_shapes=[
            pltpu.VMEM((count, 8, 128), jnp.float32),
            pltpu.SemaphoreType.DMA((count,)),
            pltpu.SemaphoreType.DMA((count,)),
        ],
        compiler_params=pltpu.CompilerParams(collective_id=1, has_side_effects=True),
    )(element, table)


def stream_slope(padded, planes):
    summed = STENCIL[0] * (padded[..., 5 : 5 + planes] - padded[..., 3 : 3 + planes])
    for offset in range(2, 5):
        summed = summed + STENCIL[offset - 1] * (
            padded[..., 4 + offset : 4 + offset + planes]
            - padded[..., 4 - offset : 4 - offset + planes]
        )
    return summed


def roll_slope(values, along_axis):
    summed = STENCIL[0] * (jnp.roll(values, -1, along_axis) - jnp.roll(values, 1, along_axis))
    for offset in range(2, 5):
        summed = summed + STENCIL[offset - 1] * (
            jnp.roll(values, -offset, along_axis) - jnp.roll(values, offset, along_axis)
        )
    return summed


def compose(earlier, latter):
    return (latter[0] * earlier[0], latter[1] + latter[0] * earlier[1])


def chain_ratio(earlier, latter):
    product = jnp.dot(latter, earlier, precision=lax.Precision.HIGHEST)
    return product / jnp.max(jnp.abs(product))


def ratio_matrix(cross_term, top_right, bottom_left):
    unit_entry = jnp.ones((), jnp.float32)
    return jnp.stack([jnp.stack([cross_term, top_right]), jnp.stack([bottom_left, unit_entry])])


def radix_plan(count):
    plan = [list(range(1, min(4, count - 1) + 1))]
    span = len(plan[0])
    while span < count - 1:
        offsets = [span * j for j in range(1, 4) if span * j < count]
        plan.append(offsets)
        span = span * (1 + len(offsets))
    return plan


def radix_scan(me, row, count, backward, element, parts, recv, send_sem, recv_sem, base, copies):
    sign = -1 if backward else 1
    plan = radix_plan(count)
    slot = base
    for level, offsets in enumerate(plan):
        source = element if level == 0 else parts.at[level - 1]
        started = []
        for offset in offsets:
            target = (me + count + sign * offset) % count
            copy = pltpu.make_async_remote_copy(
                src_ref=source,
                dst_ref=recv.at[slot],
                send_sem=send_sem.at[slot],
                recv_sem=recv_sem.at[slot],
                device_id=(row, target),
                device_id_type=MESH,
            )
            copy.start()
            started.append((offset, slot, copy))
            slot += 1
        acc = line_neutral() if level == 0 else parts[level - 1]
        for offset, index, copy in started:
            copy.wait_recv()
            copies.append(copy)
            valid = (me + offset <= count - 1) if backward else (me >= offset)
            acc = jnp.where(valid, line_join(recv[index], acc), acc)
        parts[level] = acc
    return parts[len(plan) - 1]


def carry_kernel(count, rows_here, element_ref, rows_ref, coef_ref, out_ref, parts_down, up_element, parts_up,
                 recv, send_sem, recv_sem):
    me = lax.axis_index("gy")
    row = lax.axis_index("gx")
    plan = radix_plan(count)
    residues = set()
    for offsets in plan:
        for offset in offsets:
            residues.add(offset % count)
            residues.add((count - offset) % count)
    residues.discard(0)
    barrier = pltpu.get_barrier_semaphore()
    for residue in sorted(residues):
        pl.semaphore_signal(barrier, inc=1, device_id=(row, (me + residue) % count), device_id_type=MESH)
    pl.semaphore_wait(barrier, len(residues))
    copies = []
    slots = sum(len(offsets) for offsets in plan)

    below_carry = radix_scan(
        me, row, count, False, element_ref, parts_down, recv, send_sem, recv_sem, 0, copies
    )[:LINES]
    coef = coef_ref[...]
    carried = None
    weight = None
    for i in reversed(range(rows_here)):
        sensitivity = coef[32 + i : 33 + i]
        modified = coef[16 + i : 17 + i]
        reduced = rows_ref[i] + sensitivity * below_carry
        if carried is None:
            carried = reduced
            weight = -modified
        else:
            carried = reduced - modified * carried
            weight = -modified * weight
        out_ref[i] = carried
    up_element[...] = jnp.concatenate([carried, jnp.broadcast_to(weight, (8, 128))], axis=0)
    above_carry = radix_scan(
        me, row, count, True, up_element, parts_up, recv, send_sem, recv_sem, slots, copies
    )[:LINES]
    weight = None
    for i in reversed(range(rows_here)):
        modified = coef[16 + i : 17 + i]
        weight = -modified if weight is None else -modified * weight
        out_ref[i] = out_ref[i] + weight * above_carry
    for copy in copies:
        copy.wait_send()


def carry_solve(element_factor, element_lines, rows, coef):
    count = lax.axis_size("gy")
    rows_here = len(rows)
    packed = jnp.concatenate(
        [element_lines.reshape(LINES, 128), jnp.broadcast_to(element_factor.reshape(1, 1), (8, 128))], axis=0
    )
    stacked = jnp.stack([value.reshape(LINES, 128) for value in rows], axis=0)
    plan = radix_plan(count)
    slots = 2 * sum(len(offsets) for offsets in plan)
    big = (LINES + 8, 128)
    return pl.pallas_call(
        functools.partial(carry_kernel, count, rows_here),
        out_shape=jax.ShapeDtypeStruct((rows_here, LINES, 128), jnp.float32),
        in_specs=[pl.BlockSpec(memory_space=pltpu.VMEM)] * 3,
        out_specs=pl.BlockSpec(memory_space=pltpu.VMEM),
        scratch_shapes=[
            pltpu.VMEM((len(plan),) + big, jnp.float32),
            pltpu.VMEM(big, jnp.float32),
            pltpu.VMEM((len(plan),) + big, jnp.float32),
            pltpu.VMEM((slots,) + big, jnp.float32),
            pltpu.SemaphoreType.DMA((slots,)),
            pltpu.SemaphoreType.DMA((slots,)),
        ],
        compiler_params=pltpu.CompilerParams(collective_id=0, has_side_effects=True),
    )(packed, stacked, coef)


def shards(velocity, old_advection, lower_gap, upper_gap):
    planes = velocity.shape[3]
    padded = extended(velocity, (("gx", 3),), 4, True)
    stream = stream_slope(padded, planes)
    spanwise = roll_slope(velocity, 2)
    rimmed = extended(velocity, (("gy", 1),), 1, False)
    gap_sum = lower_gap + upper_gap
    normal_slope = (rimmed[:, 2:] - rimmed[:, :-2]) / gap_sum[None, :, None, None]
    advection = -(
        velocity[0][None] * stream + velocity[1][None] * normal_slope + velocity[2][None] * spanwise
    )
    forcing = velocity + GAMMA * advection + ZETA * old_advection
    lower_coef = -2.0 * STIFF / (gap_sum * lower_gap)
    upper_coef = -2.0 * STIFF / (gap_sum * upper_gap)
    diagonal = 1.0 - lower_coef - upper_coef
    rows_here = velocity.shape[1]

    table = coefficient_table(lower_coef, upper_coef, diagonal)
    line_rows = forcing.reshape(3, rows_here, -1)
    carried = jnp.zeros_like(line_rows[:, 0])
    reduced = []
    for i in range(rows_here):
        carried = (line_rows[:, i] - lower_coef[i] * carried) / table[i, 0]
        reduced.append(carried)
    weight = table[32 + rows_here - 1, 0]
    solved = carry_solve(weight, carried, reduced, table)
    finished = jnp.transpose(solved.reshape(rows_here, 3, 32, -1), (1, 0, 2, 3))
    return (finished.reshape(velocity.shape), advection)


def solution(mesh):
    return jax.shard_map(
        shards,
        mesh=mesh,
        in_specs=(P(None, "gy", None, "gx"), P(None, "gy", None, "gx"), P("gy"), P("gy")),
        out_specs=(P(None, "gy", None, "gx"), P(None, "gy", None, "gx")),
        check_vma=False,
    )
```

```python
import functools

import jax
import jax.numpy as jnp
from jax import lax
from jax.sharding import PartitionSpec as P
from jax.experimental import pallas as pl
from jax.experimental.pallas import tpu as pltpu

MESH = pl.DeviceIdType.MESH
LINES = 96

STIFF = 1024


STENCIL = (0.8, -0.2, 4.0 / 105.0, -1.0 / 280.0)
GAMMA = 5.0 / 12.0
ZETA = -17.0 / 60.0


def extended(array, sides, width, wrap):
    for axis, dim in sides:
        size, length = (lax.axis_size(axis), array.shape[dim])
        up = [(i, (i + 1) % size) for i in range(size if wrap else size - 1)]
        down = [(j, i) for i, j in up]
        last = lax.slice_in_dim(array, length - width, length, axis=dim)
        first = lax.slice_in_dim(array, 0, width, axis=dim)
        before = lax.ppermute(last, axis, up)
        after = lax.ppermute(first, axis, down)
        array = jnp.concatenate([before, array, after], axis=dim)
    return array


def prefix(value, axis, join, neutral, backward):
    count, mine = (lax.axis_size(axis), lax.axis_index(axis))
    step = -1 if backward else 1
    order = [(i, i + step) for i in range(count) if 0 <= i + step < count]
    total = jax.tree.map(lambda part: lax.ppermute(part, axis, order), value)
    inside = (mine >= 1) if not backward else (mine <= count - 2)
    total = jax.tree.map(
        lambda part, zero: jnp.where(inside, part, jnp.full_like(part, 0) + jnp.asarray(zero, part.dtype)),
        total,
        neutral,
    )
    offset = 1
    while offset < count:
        pairs = [(i, i + step * offset) for i in range(count) if 0 <= i + step * offset < count]
        earlier = jax.tree.map(lambda part: lax.ppermute(part, axis, pairs), total)
        longer = join(earlier, total)
        reach = (mine >= offset) if not backward else (mine <= count - 1 - offset)
        total = jax.tree.map(lambda new, old: jnp.where(reach, new, old), longer, total)
        offset *= 2
    return total


def ratio_join(earlier, latter):
    def entry(i, j):
        return latter[2 * i : 2 * i + 1] * earlier[j : j + 1] + latter[2 * i + 1 : 2 * i + 2] * earlier[2 + j : 3 + j]

    entries = [entry(0, 0), entry(0, 1), entry(1, 0), entry(1, 1)]
    big = jnp.maximum(
        jnp.maximum(jnp.abs(entries[0]), jnp.abs(entries[1])),
        jnp.maximum(jnp.abs(entries[2]), jnp.abs(entries[3])),
    )
    rows = [part / big for part in entries]
    return jnp.concatenate(rows + [jnp.zeros((4, 128), jnp.float32)], axis=0)


def line_join(earlier, latter):
    factor = latter[LINES : LINES + 1, :]
    joined_lines = latter[:LINES] + factor * earlier[:LINES]
    joined_scale = latter[LINES:] * earlier[LINES:]
    return jnp.concatenate([joined_lines, joined_scale], axis=0)


def ratio_neutral():
    unit = jnp.ones((1, 128), jnp.float32)
    blank = jnp.zeros((1, 128), jnp.float32)
    return jnp.concatenate([unit, blank, blank, unit, blank, blank, blank, blank], axis=0)


def line_neutral():
    return jnp.concatenate([jnp.zeros((LINES, 128), jnp.float32), jnp.ones((8, 128), jnp.float32)], axis=0)


def scan_kernel(count, backward, join, neutral, x_ref, out_ref, totals, recv, send_sem, recv_sem):
    me = lax.axis_index("gy")
    row = lax.axis_index("gx")
    sign = -1 if backward else 1
    offsets = [1]
    while offsets[-1] * 2 < count:
        offsets.append(offsets[-1] * 2)
    partners = []
    for offset in offsets:
        partners.append((me + offset) % count)
        if 2 * offset != count:
            partners.append((me + count - offset) % count)
    barrier = pltpu.get_barrier_semaphore()
    for partner in partners:
        pl.semaphore_signal(barrier, inc=1, device_id=(row, partner), device_id_type=MESH)
    pl.semaphore_wait(barrier, len(partners))
    rounds = [1] + offsets
    copies = []
    for step, offset in enumerate(rounds):
        source = x_ref if step == 0 else totals.at[step - 1]
        target = (me + count + sign * offset) % count
        copy = pltpu.make_async_remote_copy(
            src_ref=source,
            dst_ref=recv.at[step],
            send_sem=send_sem.at[step],
            recv_sem=recv_sem.at[step],
            device_id=(row, target),
            device_id_type=MESH,
        )
        copy.start()
        copy.wait_recv()
        copies.append(copy)
        valid = (me + offset <= count - 1) if backward else (me >= offset)
        earlier = recv[step]
        if step == 0:
            totals[step] = jnp.where(valid, earlier, neutral())
        else:
            latter = totals[step - 1]
            totals[step] = jnp.where(valid, join(earlier, latter), latter)
    out_ref[...] = totals[len(rounds) - 1]
    for copy in copies:
        copy.wait_send()


def line_scan(step_value, backward):
    count = lax.axis_size("gy")
    factor, lines = step_value
    shape = lines.shape
    packed = jnp.concatenate(
        [lines.reshape(LINES, 128), jnp.broadcast_to(factor.reshape(1, 1), (8, 128))], axis=0
    )
    rounds = 1
    while (1 << (rounds - 1)) * 2 < count:
        rounds += 1
    rounds += 1
    result = pl.pallas_call(
        functools.partial(scan_kernel, count, backward, line_join, line_neutral),
        out_shape=jax.ShapeDtypeStruct(packed.shape, jnp.float32),
        in_specs=[pl.BlockSpec(memory_space=pltpu.VMEM)],
        out_specs=pl.BlockSpec(memory_space=pltpu.VMEM),
        scratch_shapes=[
            pltpu.VMEM((rounds,) + packed.shape, jnp.float32),
            pltpu.VMEM((rounds,) + packed.shape, jnp.float32),
            pltpu.SemaphoreType.DMA((rounds,)),
            pltpu.SemaphoreType.DMA((rounds,)),
        ],
        compiler_params=pltpu.CompilerParams(collective_id=1 if backward else 0, has_side_effects=True),
    )(packed)
    return result[:LINES].reshape(shape)


def ratio_scan(matrix):
    count = lax.axis_size("gy")
    packed = jnp.concatenate(
        [jnp.broadcast_to(matrix.reshape(4, 1), (4, 128)), jnp.zeros((4, 128), jnp.float32)], axis=0
    )
    rounds = 1
    while (1 << (rounds - 1)) * 2 < count:
        rounds += 1
    rounds += 1
    result = pl.pallas_call(
        functools.partial(scan_kernel, count, False, ratio_join, ratio_neutral),
        out_shape=jax.ShapeDtypeStruct(packed.shape, jnp.float32),
        in_specs=[pl.BlockSpec(memory_space=pltpu.VMEM)],
        out_specs=pl.BlockSpec(memory_space=pltpu.VMEM),
        scratch_shapes=[
            pltpu.VMEM((rounds,) + packed.shape, jnp.float32),
            pltpu.VMEM((rounds,) + packed.shape, jnp.float32),
            pltpu.SemaphoreType.DMA((rounds,)),
            pltpu.SemaphoreType.DMA((rounds,)),
        ],
        compiler_params=pltpu.CompilerParams(collective_id=2, has_side_effects=True),
    )(packed)
    return result[:4, 0].reshape(2, 2)


def prefix_kernel(count, rows_here, element_ref, table_ref, out_ref, pieces, send_sem, recv_sem):
    mine = lax.axis_index("gy")
    row = lax.axis_index("gx")
    barrier = pltpu.get_barrier_semaphore()

    def greet(step, carry):
        pl.semaphore_signal(barrier, inc=1, device_id=(row, (mine + step) % count), device_id_type=MESH)
        return carry

    lax.fori_loop(1, count, greet, 0)
    pl.semaphore_wait(barrier, count - 1)

    def outgoing(step):
        return pltpu.make_async_remote_copy(
            src_ref=element_ref,
            dst_ref=pieces.at[mine],
            send_sem=send_sem.at[step],
            recv_sem=recv_sem.at[mine],
            device_id=(row, (mine + step) % count),
            device_id_type=MESH,
        )

    def incoming(step):
        source = (mine + count - step) % count
        return pltpu.make_async_remote_copy(
            src_ref=element_ref,
            dst_ref=pieces.at[source],
            send_sem=send_sem.at[step],
            recv_sem=recv_sem.at[source],
            device_id=(row, source),
            device_id_type=MESH,
        )

    def send(step, carry):
        outgoing(step).start()
        return carry

    def arrive(step, carry):
        incoming(step).wait_recv()
        return carry

    def drain(step, carry):
        outgoing(step).wait_send()
        return carry

    lax.fori_loop(1, count, send, 0)
    lax.fori_loop(1, count, arrive, 0)
    pieces[mine] = element_ref[...]

    def turn(position, total):
        piece = pieces[position]
        entries = [
            piece[2 * i : 2 * i + 1] * total[j] + piece[2 * i + 1 : 2 * i + 2] * total[2 + j]
            for i in range(2)
            for j in range(2)
        ]
        big = jnp.maximum(
            jnp.maximum(jnp.abs(entries[0]), jnp.abs(entries[1])),
            jnp.maximum(jnp.abs(entries[2]), jnp.abs(entries[3])),
        )
        inside = position < mine
        return tuple(jnp.where(inside, value / big, old) for value, old in zip(entries, total))

    unit = jnp.ones((1, 128), jnp.float32)
    blank = jnp.zeros((1, 128), jnp.float32)
    total = lax.fori_loop(0, count - 1, turn, (unit, blank, blank, unit))
    modified_prev = total[1] / total[3]
    weight = unit
    for i in range(rows_here):
        lower = table_ref[i : i + 1]
        upper = table_ref[16 + i : 17 + i]
        diagonal = table_ref[32 + i : 33 + i]
        pivot = diagonal - lower * modified_prev
        modified_prev = upper / pivot
        weight = -lower / pivot * weight
        out_ref[i : i + 1] = pivot
        out_ref[16 + i : 17 + i] = modified_prev
        out_ref[32 + i : 33 + i] = weight
    lax.fori_loop(1, count, drain, 0)


def matrix_kernel(rows_here, table_ref, out_ref):
    unit = jnp.ones((1, 128), jnp.float32)
    blank = jnp.zeros((1, 128), jnp.float32)
    top = (unit, blank)
    bottom = (blank, unit)
    for i in range(rows_here):
        scale = 1.0 / table_ref[32 + i : 33 + i]
        up = table_ref[16 + i : 17 + i] * scale
        low = -table_ref[i : i + 1] * scale
        top, bottom = (
            (up * bottom[0], up * bottom[1]),
            (low * top[0] + bottom[0], low * top[1] + bottom[1]),
        )
    big = jnp.maximum(
        jnp.maximum(jnp.abs(top[0]), jnp.abs(top[1])), jnp.maximum(jnp.abs(bottom[0]), jnp.abs(bottom[1]))
    )
    out_ref[...] = jnp.concatenate(
        [top[0] / big, top[1] / big, bottom[0] / big, bottom[1] / big, blank, blank, blank, blank], axis=0
    )


def coefficient_table(lower_coef, upper_coef, diagonal):
    count = lax.axis_size("gy")
    rows_here = lower_coef.shape[0]
    filler = jnp.zeros((16 - rows_here,), jnp.float32)
    column = jnp.concatenate([lower_coef, filler, upper_coef, filler, diagonal, filler])
    table = jnp.broadcast_to(column.reshape(48, 1), (48, 128))
    element = pl.pallas_call(
        functools.partial(matrix_kernel, rows_here),
        out_shape=jax.ShapeDtypeStruct((8, 128), jnp.float32),
        in_specs=[pl.BlockSpec(memory_space=pltpu.VMEM)],
        out_specs=pl.BlockSpec(memory_space=pltpu.VMEM),
    )(table)
    return table, pl.pallas_call(
        functools.partial(prefix_kernel, count, rows_here),
        out_shape=jax.ShapeDtypeStruct((48, 128), jnp.float32),
        in_specs=[pl.BlockSpec(memory_space=pltpu.VMEM)] * 2,
        out_specs=pl.BlockSpec(memory_space=pltpu.VMEM),
        scratch_shapes=[
            pltpu.VMEM((count, 8, 128), jnp.float32),
            pltpu.SemaphoreType.DMA((count,)),
            pltpu.SemaphoreType.DMA((count,)),
        ],
        compiler_params=pltpu.CompilerParams(collective_id=1, has_side_effects=True),
    )(element, table)


def stream_slope(padded, planes):
    summed = STENCIL[0] * (padded[..., 5 : 5 + planes] - padded[..., 3 : 3 + planes])
    for offset in range(2, 5):
        summed = summed + STENCIL[offset - 1] * (
            padded[..., 4 + offset : 4 + offset + planes]
            - padded[..., 4 - offset : 4 - offset + planes]
        )
    return summed


def roll_slope(values, along_axis):
    summed = STENCIL[0] * (jnp.roll(values, -1, along_axis) - jnp.roll(values, 1, along_axis))
    for offset in range(2, 5):
        summed = summed + STENCIL[offset - 1] * (
            jnp.roll(values, -offset, along_axis) - jnp.roll(values, offset, along_axis)
        )
    return summed


def compose(earlier, latter):
    return (latter[0] * earlier[0], latter[1] + latter[0] * earlier[1])


def chain_ratio(earlier, latter):
    product = jnp.dot(latter, earlier, precision=lax.Precision.HIGHEST)
    return product / jnp.max(jnp.abs(product))


def ratio_matrix(cross_term, top_right, bottom_left):
    unit_entry = jnp.ones((), jnp.float32)
    return jnp.stack([jnp.stack([cross_term, top_right]), jnp.stack([bottom_left, unit_entry])])


def radix_plan(count):
    plan = [list(range(1, min(4, count - 1) + 1))]
    span = len(plan[0])
    while span < count - 1:
        offsets = [span * j for j in range(1, 4) if span * j < count]
        plan.append(offsets)
        span = span * (1 + len(offsets))
    return plan


def radix_scan(me, row, count, backward, element, parts, recv, send_sem, recv_sem, base, copies):
    sign = -1 if backward else 1
    plan = radix_plan(count)
    slot = base
    for level, offsets in enumerate(plan):
        source = element if level == 0 else parts.at[level - 1]
        started = []
        for offset in offsets:
            target = (me + count + sign * offset) % count
            copy = pltpu.make_async_remote_copy(
                src_ref=source,
                dst_ref=recv.at[slot],
                send_sem=send_sem.at[slot],
                recv_sem=recv_sem.at[slot],
                device_id=(row, target),
                device_id_type=MESH,
            )
            copy.start()
            started.append((offset, slot, copy))
            slot += 1
        acc = line_neutral() if level == 0 else parts[level - 1]
        for offset, index, copy in started:
            copy.wait_recv()
            copies.append(copy)
            valid = (me + offset <= count - 1) if backward else (me >= offset)
            acc = jnp.where(valid, line_join(recv[index], acc), acc)
        parts[level] = acc
    return parts[len(plan) - 1]


def carry_kernel(count, rows_here, rows_ref, given_ref, coef_ref, out_ref, down_element, parts_down, up_element,
                 parts_up, recv, send_sem, recv_sem):
    me = lax.axis_index("gy")
    row = lax.axis_index("gx")
    plan = radix_plan(count)
    residues = set()
    for offsets in plan:
        for offset in offsets:
            residues.add(offset % count)
            residues.add((count - offset) % count)
    residues.discard(0)
    barrier = pltpu.get_barrier_semaphore()
    for residue in sorted(residues):
        pl.semaphore_signal(barrier, inc=1, device_id=(row, (me + residue) % count), device_id_type=MESH)
    pl.semaphore_wait(barrier, len(residues))
    copies = []
    slots = sum(len(offsets) for offsets in plan)

    coef = coef_ref[...]
    given = given_ref[...]
    carried = None
    for i in range(rows_here):
        lower = given[i : i + 1]
        pivot = coef[i : i + 1]
        carried = rows_ref[i] / pivot if carried is None else (rows_ref[i] - lower * carried) / pivot
        out_ref[i] = carried
    down_element[...] = jnp.concatenate(
        [carried, jnp.broadcast_to(coef[32 + rows_here - 1 : 32 + rows_here], (8, 128))], axis=0
    )
    below_carry = radix_scan(
        me, row, count, False, down_element, parts_down, recv, send_sem, recv_sem, 0, copies
    )[:LINES]
    carried = None
    weight = None
    for i in reversed(range(rows_here)):
        sensitivity = coef[32 + i : 33 + i]
        modified = coef[16 + i : 17 + i]
        reduced = out_ref[i] + sensitivity * below_carry
        if carried is None:
            carried = reduced
            weight = -modified
        else:
            carried = reduced - modified * carried
            weight = -modified * weight
        out_ref[i] = carried
    up_element[...] = jnp.concatenate([carried, jnp.broadcast_to(weight, (8, 128))], axis=0)
    above_carry = radix_scan(
        me, row, count, True, up_element, parts_up, recv, send_sem, recv_sem, slots, copies
    )[:LINES]
    weight = None
    for i in reversed(range(rows_here)):
        modified = coef[16 + i : 17 + i]
        weight = -modified if weight is None else -modified * weight
        out_ref[i] = out_ref[i] + weight * above_carry
    for copy in copies:
        copy.wait_send()


def carry_solve(stacked, given, coef):
    count = lax.axis_size("gy")
    rows_here = stacked.shape[0]
    plan = radix_plan(count)
    slots = 2 * sum(len(offsets) for offsets in plan)
    big = (LINES + 8, 128)
    return pl.pallas_call(
        functools.partial(carry_kernel, count, rows_here),
        out_shape=jax.ShapeDtypeStruct((rows_here, LINES, 128), jnp.float32),
        in_specs=[pl.BlockSpec(memory_space=pltpu.VMEM)] * 3,
        out_specs=pl.BlockSpec(memory_space=pltpu.VMEM),
        scratch_shapes=[
            pltpu.VMEM(big, jnp.float32),
            pltpu.VMEM((len(plan),) + big, jnp.float32),
            pltpu.VMEM(big, jnp.float32),
            pltpu.VMEM((len(plan),) + big, jnp.float32),
            pltpu.VMEM((slots,) + big, jnp.float32),
            pltpu.SemaphoreType.DMA((slots,)),
            pltpu.SemaphoreType.DMA((slots,)),
        ],
        compiler_params=pltpu.CompilerParams(collective_id=0, has_side_effects=True),
    )(stacked, given, coef)


def shards(velocity, old_advection, lower_gap, upper_gap):
    planes = velocity.shape[3]
    padded = extended(velocity, (("gx", 3),), 4, True)
    stream = stream_slope(padded, planes)
    spanwise = roll_slope(velocity, 2)
    rimmed = extended(velocity, (("gy", 1),), 1, False)
    gap_sum = lower_gap + upper_gap
    normal_slope = (rimmed[:, 2:] - rimmed[:, :-2]) / gap_sum[None, :, None, None]
    advection = -(
        velocity[0][None] * stream + velocity[1][None] * normal_slope + velocity[2][None] * spanwise
    )
    forcing = velocity + GAMMA * advection + ZETA * old_advection
    lower_coef = -2.0 * STIFF / (gap_sum * lower_gap)
    upper_coef = -2.0 * STIFF / (gap_sum * upper_gap)
    diagonal = 1.0 - lower_coef - upper_coef
    rows_here = velocity.shape[1]

    given, table = coefficient_table(lower_coef, upper_coef, diagonal)
    stacked = jnp.transpose(forcing, (1, 0, 2, 3)).reshape(rows_here, LINES, 128)
    solved = carry_solve(stacked, given, table)
    finished = jnp.transpose(solved.reshape(rows_here, 3, 32, -1), (1, 0, 2, 3))
    return (finished.reshape(velocity.shape), advection)


def solution(mesh):
    return jax.shard_map(
        shards,
        mesh=mesh,
        in_specs=(P(None, "gy", None, "gx"), P(None, "gy", None, "gx"), P("gy"), P("gy")),
        out_specs=(P(None, "gy", None, "gx"), P(None, "gy", None, "gx")),
        check_vma=False,
    )
```

```python
import functools

import jax
import jax.numpy as jnp
from jax import lax
from jax.sharding import PartitionSpec as P
from jax.experimental import pallas as pl
from jax.experimental.pallas import tpu as pltpu

MESH = pl.DeviceIdType.MESH
LINES = 96

STIFF = 1024


STENCIL = (0.8, -0.2, 4.0 / 105.0, -1.0 / 280.0)
GAMMA = 5.0 / 12.0
ZETA = -17.0 / 60.0


def extended(array, sides, width, wrap):
    for axis, dim in sides:
        size, length = (lax.axis_size(axis), array.shape[dim])
        up = [(i, (i + 1) % size) for i in range(size if wrap else size - 1)]
        down = [(j, i) for i, j in up]
        last = lax.slice_in_dim(array, length - width, length, axis=dim)
        first = lax.slice_in_dim(array, 0, width, axis=dim)
        before = lax.ppermute(last, axis, up)
        after = lax.ppermute(first, axis, down)
        array = jnp.concatenate([before, array, after], axis=dim)
    return array


def prefix(value, axis, join, neutral, backward):
    count, mine = (lax.axis_size(axis), lax.axis_index(axis))
    step = -1 if backward else 1
    order = [(i, i + step) for i in range(count) if 0 <= i + step < count]
    total = jax.tree.map(lambda part: lax.ppermute(part, axis, order), value)
    inside = (mine >= 1) if not backward else (mine <= count - 2)
    total = jax.tree.map(
        lambda part, zero: jnp.where(inside, part, jnp.full_like(part, 0) + jnp.asarray(zero, part.dtype)),
        total,
        neutral,
    )
    offset = 1
    while offset < count:
        pairs = [(i, i + step * offset) for i in range(count) if 0 <= i + step * offset < count]
        earlier = jax.tree.map(lambda part: lax.ppermute(part, axis, pairs), total)
        longer = join(earlier, total)
        reach = (mine >= offset) if not backward else (mine <= count - 1 - offset)
        total = jax.tree.map(lambda new, old: jnp.where(reach, new, old), longer, total)
        offset *= 2
    return total


def ratio_join(earlier, latter):
    def entry(i, j):
        return latter[2 * i : 2 * i + 1] * earlier[j : j + 1] + latter[2 * i + 1 : 2 * i + 2] * earlier[2 + j : 3 + j]

    entries = [entry(0, 0), entry(0, 1), entry(1, 0), entry(1, 1)]
    big = jnp.maximum(
        jnp.maximum(jnp.abs(entries[0]), jnp.abs(entries[1])),
        jnp.maximum(jnp.abs(entries[2]), jnp.abs(entries[3])),
    )
    rows = [part / big for part in entries]
    return jnp.concatenate(rows + [jnp.zeros((4, 128), jnp.float32)], axis=0)


def line_join(earlier, latter):
    factor = latter[LINES : LINES + 1, :]
    joined_lines = latter[:LINES] + factor * earlier[:LINES]
    joined_scale = latter[LINES:] * earlier[LINES:]
    return jnp.concatenate([joined_lines, joined_scale], axis=0)


def ratio_neutral():
    unit = jnp.ones((1, 128), jnp.float32)
    blank = jnp.zeros((1, 128), jnp.float32)
    return jnp.concatenate([unit, blank, blank, unit, blank, blank, blank, blank], axis=0)


def line_neutral():
    return jnp.concatenate([jnp.zeros((LINES, 128), jnp.float32), jnp.ones((8, 128), jnp.float32)], axis=0)


def scan_kernel(count, backward, join, neutral, x_ref, out_ref, totals, recv, send_sem, recv_sem):
    me = lax.axis_index("gy")
    row = lax.axis_index("gx")
    sign = -1 if backward else 1
    offsets = [1]
    while offsets[-1] * 2 < count:
        offsets.append(offsets[-1] * 2)
    partners = []
    for offset in offsets:
        partners.append((me + offset) % count)
        if 2 * offset != count:
            partners.append((me + count - offset) % count)
    barrier = pltpu.get_barrier_semaphore()
    for partner in partners:
        pl.semaphore_signal(barrier, inc=1, device_id=(row, partner), device_id_type=MESH)
    pl.semaphore_wait(barrier, len(partners))
    rounds = [1] + offsets
    copies = []
    for step, offset in enumerate(rounds):
        source = x_ref if step == 0 else totals.at[step - 1]
        target = (me + count + sign * offset) % count
        copy = pltpu.make_async_remote_copy(
            src_ref=source,
            dst_ref=recv.at[step],
            send_sem=send_sem.at[step],
            recv_sem=recv_sem.at[step],
            device_id=(row, target),
            device_id_type=MESH,
        )
        copy.start()
        copy.wait_recv()
        copies.append(copy)
        valid = (me + offset <= count - 1) if backward else (me >= offset)
        earlier = recv[step]
        if step == 0:
            totals[step] = jnp.where(valid, earlier, neutral())
        else:
            latter = totals[step - 1]
            totals[step] = jnp.where(valid, join(earlier, latter), latter)
    out_ref[...] = totals[len(rounds) - 1]
    for copy in copies:
        copy.wait_send()


def line_scan(step_value, backward):
    count = lax.axis_size("gy")
    factor, lines = step_value
    shape = lines.shape
    packed = jnp.concatenate(
        [lines.reshape(LINES, 128), jnp.broadcast_to(factor.reshape(1, 1), (8, 128))], axis=0
    )
    rounds = 1
    while (1 << (rounds - 1)) * 2 < count:
        rounds += 1
    rounds += 1
    result = pl.pallas_call(
        functools.partial(scan_kernel, count, backward, line_join, line_neutral),
        out_shape=jax.ShapeDtypeStruct(packed.shape, jnp.float32),
        in_specs=[pl.BlockSpec(memory_space=pltpu.VMEM)],
        out_specs=pl.BlockSpec(memory_space=pltpu.VMEM),
        scratch_shapes=[
            pltpu.VMEM((rounds,) + packed.shape, jnp.float32),
            pltpu.VMEM((rounds,) + packed.shape, jnp.float32),
            pltpu.SemaphoreType.DMA((rounds,)),
            pltpu.SemaphoreType.DMA((rounds,)),
        ],
        compiler_params=pltpu.CompilerParams(collective_id=1 if backward else 0, has_side_effects=True),
    )(packed)
    return result[:LINES].reshape(shape)


def ratio_scan(matrix):
    count = lax.axis_size("gy")
    packed = jnp.concatenate(
        [jnp.broadcast_to(matrix.reshape(4, 1), (4, 128)), jnp.zeros((4, 128), jnp.float32)], axis=0
    )
    rounds = 1
    while (1 << (rounds - 1)) * 2 < count:
        rounds += 1
    rounds += 1
    result = pl.pallas_call(
        functools.partial(scan_kernel, count, False, ratio_join, ratio_neutral),
        out_shape=jax.ShapeDtypeStruct(packed.shape, jnp.float32),
        in_specs=[pl.BlockSpec(memory_space=pltpu.VMEM)],
        out_specs=pl.BlockSpec(memory_space=pltpu.VMEM),
        scratch_shapes=[
            pltpu.VMEM((rounds,) + packed.shape, jnp.float32),
            pltpu.VMEM((rounds,) + packed.shape, jnp.float32),
            pltpu.SemaphoreType.DMA((rounds,)),
            pltpu.SemaphoreType.DMA((rounds,)),
        ],
        compiler_params=pltpu.CompilerParams(collective_id=2, has_side_effects=True),
    )(packed)
    return result[:4, 0].reshape(2, 2)


def prefix_kernel(count, rows_here, element_ref, table_ref, out_ref, pieces, send_sem, recv_sem):
    mine = lax.axis_index("gy")
    row = lax.axis_index("gx")
    barrier = pltpu.get_barrier_semaphore()

    def greet(step, carry):
        pl.semaphore_signal(barrier, inc=1, device_id=(row, (mine + step) % count), device_id_type=MESH)
        return carry

    lax.fori_loop(1, count, greet, 0)
    pl.semaphore_wait(barrier, count - 1)

    def outgoing(step):
        return pltpu.make_async_remote_copy(
            src_ref=element_ref,
            dst_ref=pieces.at[mine],
            send_sem=send_sem.at[step],
            recv_sem=recv_sem.at[mine],
            device_id=(row, (mine + step) % count),
            device_id_type=MESH,
        )

    def incoming(step):
        source = (mine + count - step) % count
        return pltpu.make_async_remote_copy(
            src_ref=element_ref,
            dst_ref=pieces.at[source],
            send_sem=send_sem.at[step],
            recv_sem=recv_sem.at[source],
            device_id=(row, source),
            device_id_type=MESH,
        )

    def send(step, carry):
        outgoing(step).start()
        return carry

    def arrive(step, carry):
        incoming(step).wait_recv()
        return carry

    def drain(step, carry):
        outgoing(step).wait_send()
        return carry

    lax.fori_loop(1, count, send, 0)
    lax.fori_loop(1, count, arrive, 0)
    pieces[mine] = element_ref[...]

    def turn(position, total):
        piece = pieces[position]
        entries = [
            piece[2 * i : 2 * i + 1] * total[j] + piece[2 * i + 1 : 2 * i + 2] * total[2 + j]
            for i in range(2)
            for j in range(2)
        ]
        big = jnp.maximum(
            jnp.maximum(jnp.abs(entries[0]), jnp.abs(entries[1])),
            jnp.maximum(jnp.abs(entries[2]), jnp.abs(entries[3])),
        )
        inside = position < mine
        return tuple(jnp.where(inside, value / big, old) for value, old in zip(entries, total))

    unit = jnp.ones((1, 128), jnp.float32)
    blank = jnp.zeros((1, 128), jnp.float32)
    total = lax.fori_loop(0, count - 1, turn, (unit, blank, blank, unit))
    modified_prev = total[1] / total[3]
    weight = unit
    for i in range(rows_here):
        lower = table_ref[i : i + 1]
        upper = table_ref[16 + i : 17 + i]
        diagonal = table_ref[32 + i : 33 + i]
        pivot = diagonal - lower * modified_prev
        modified_prev = upper / pivot
        weight = -lower / pivot * weight
        out_ref[i : i + 1] = pivot
        out_ref[16 + i : 17 + i] = modified_prev
        out_ref[32 + i : 33 + i] = weight
    lax.fori_loop(1, count, drain, 0)


def matrix_kernel(rows_here, table_ref, out_ref):
    unit = jnp.ones((1, 128), jnp.float32)
    blank = jnp.zeros((1, 128), jnp.float32)
    top = (unit, blank)
    bottom = (blank, unit)
    for i in range(rows_here):
        scale = 1.0 / table_ref[32 + i : 33 + i]
        up = table_ref[16 + i : 17 + i] * scale
        low = -table_ref[i : i + 1] * scale
        top, bottom = (
            (up * bottom[0], up * bottom[1]),
            (low * top[0] + bottom[0], low * top[1] + bottom[1]),
        )
    big = jnp.maximum(
        jnp.maximum(jnp.abs(top[0]), jnp.abs(top[1])), jnp.maximum(jnp.abs(bottom[0]), jnp.abs(bottom[1]))
    )
    out_ref[...] = jnp.concatenate(
        [top[0] / big, top[1] / big, bottom[0] / big, bottom[1] / big, blank, blank, blank, blank], axis=0
    )


def coefficient_table(lower_coef, upper_coef, diagonal):
    count = lax.axis_size("gy")
    rows_here = lower_coef.shape[0]
    filler = jnp.zeros((16 - rows_here,), jnp.float32)
    column = jnp.concatenate([lower_coef, filler, upper_coef, filler, diagonal, filler])
    table = jnp.broadcast_to(column.reshape(48, 1), (48, 128))
    element = pl.pallas_call(
        functools.partial(matrix_kernel, rows_here),
        out_shape=jax.ShapeDtypeStruct((8, 128), jnp.float32),
        in_specs=[pl.BlockSpec(memory_space=pltpu.VMEM)],
        out_specs=pl.BlockSpec(memory_space=pltpu.VMEM),
    )(table)
    return table, pl.pallas_call(
        functools.partial(prefix_kernel, count, rows_here),
        out_shape=jax.ShapeDtypeStruct((48, 128), jnp.float32),
        in_specs=[pl.BlockSpec(memory_space=pltpu.VMEM)] * 2,
        out_specs=pl.BlockSpec(memory_space=pltpu.VMEM),
        scratch_shapes=[
            pltpu.VMEM((count, 8, 128), jnp.float32),
            pltpu.SemaphoreType.DMA((count,)),
            pltpu.SemaphoreType.DMA((count,)),
        ],
        compiler_params=pltpu.CompilerParams(collective_id=1, has_side_effects=True),
    )(element, table)


def stream_slope(padded, planes):
    summed = STENCIL[0] * (padded[..., 5 : 5 + planes] - padded[..., 3 : 3 + planes])
    for offset in range(2, 5):
        summed = summed + STENCIL[offset - 1] * (
            padded[..., 4 + offset : 4 + offset + planes]
            - padded[..., 4 - offset : 4 - offset + planes]
        )
    return summed


def roll_slope(values, along_axis):
    summed = STENCIL[0] * (jnp.roll(values, -1, along_axis) - jnp.roll(values, 1, along_axis))
    for offset in range(2, 5):
        summed = summed + STENCIL[offset - 1] * (
            jnp.roll(values, -offset, along_axis) - jnp.roll(values, offset, along_axis)
        )
    return summed


def compose(earlier, latter):
    return (latter[0] * earlier[0], latter[1] + latter[0] * earlier[1])


def chain_ratio(earlier, latter):
    product = jnp.dot(latter, earlier, precision=lax.Precision.HIGHEST)
    return product / jnp.max(jnp.abs(product))


def ratio_matrix(cross_term, top_right, bottom_left):
    unit_entry = jnp.ones((), jnp.float32)
    return jnp.stack([jnp.stack([cross_term, top_right]), jnp.stack([bottom_left, unit_entry])])


def radix_plan(count):
    plan = [list(range(1, min(4, count - 1) + 1))]
    span = len(plan[0])
    while span < count - 1:
        offsets = [span * j for j in range(1, 4) if span * j < count]
        plan.append(offsets)
        span = span * (1 + len(offsets))
    return plan


def radix_scan(me, row, count, backward, element, parts, recv, send_sem, recv_sem, base, copies):
    sign = -1 if backward else 1
    plan = radix_plan(count)
    slot = base
    for level, offsets in enumerate(plan):
        source = element if level == 0 else parts.at[level - 1]
        started = []
        for offset in offsets:
            target = (me + count + sign * offset) % count
            copy = pltpu.make_async_remote_copy(
                src_ref=source,
                dst_ref=recv.at[slot],
                send_sem=send_sem.at[slot],
                recv_sem=recv_sem.at[slot],
                device_id=(row, target),
                device_id_type=MESH,
            )
            copy.start()
            started.append((offset, slot, copy))
            slot += 1
        acc = line_neutral() if level == 0 else parts[level - 1]
        for offset, index, copy in started:
            copy.wait_recv()
            copies.append(copy)
            valid = (me + offset <= count - 1) if backward else (me >= offset)
            acc = jnp.where(valid, line_join(recv[index], acc), acc)
        parts[level] = acc
    return parts[len(plan) - 1]


def carry_kernel(count, rows_here, rows_ref, given_ref, coef_ref, out_ref, down_element, parts_down, up_element,
                 parts_up, recv, send_sem, recv_sem):
    me = lax.axis_index("gy")
    row = lax.axis_index("gx")
    plan = radix_plan(count)
    residues = set()
    for offsets in plan:
        for offset in offsets:
            residues.add(offset % count)
            residues.add((count - offset) % count)
    residues.discard(0)
    barrier = pltpu.get_barrier_semaphore()
    for residue in sorted(residues):
        pl.semaphore_signal(barrier, inc=1, device_id=(row, (me + residue) % count), device_id_type=MESH)
    pl.semaphore_wait(barrier, len(residues))
    copies = []
    slots = sum(len(offsets) for offsets in plan)

    coef = coef_ref[...]
    given = given_ref[...]
    carried = None
    for i in range(rows_here):
        lower = given[i : i + 1]
        pivot = coef[i : i + 1]
        carried = rows_ref[i] / pivot if carried is None else (rows_ref[i] - lower * carried) / pivot
        out_ref[i] = carried
    down_element[...] = jnp.concatenate(
        [carried, jnp.broadcast_to(coef[32 + rows_here - 1 : 32 + rows_here], (8, 128))], axis=0
    )
    below_carry = radix_scan(
        me, row, count, False, down_element, parts_down, recv, send_sem, recv_sem, 0, copies
    )[:LINES]
    carried = None
    weight = None
    for i in reversed(range(rows_here)):
        sensitivity = coef[32 + i : 33 + i]
        modified = coef[16 + i : 17 + i]
        reduced = out_ref[i] + sensitivity * below_carry
        if carried is None:
            carried = reduced
            weight = -modified
        else:
            carried = reduced - modified * carried
            weight = -modified * weight
        out_ref[i] = carried
    up_element[...] = jnp.concatenate([carried, jnp.broadcast_to(weight, (8, 128))], axis=0)
    above_carry = radix_scan(
        me, row, count, True, up_element, parts_up, recv, send_sem, recv_sem, slots, copies
    )[:LINES]
    weight = None
    for i in reversed(range(rows_here)):
        modified = coef[16 + i : 17 + i]
        weight = -modified if weight is None else -modified * weight
        out_ref[i] = out_ref[i] + weight * above_carry
    for copy in copies:
        copy.wait_send()


def carry_solve(stacked, given, coef):
    count = lax.axis_size("gy")
    rows_here = stacked.shape[0]
    plan = radix_plan(count)
    slots = 2 * sum(len(offsets) for offsets in plan)
    big = (LINES + 8, 128)
    return pl.pallas_call(
        functools.partial(carry_kernel, count, rows_here),
        out_shape=jax.ShapeDtypeStruct((rows_here, LINES, 128), jnp.float32),
        in_specs=[pl.BlockSpec(memory_space=pltpu.VMEM)] * 3,
        out_specs=pl.BlockSpec(memory_space=pltpu.VMEM),
        scratch_shapes=[
            pltpu.VMEM(big, jnp.float32),
            pltpu.VMEM((len(plan),) + big, jnp.float32),
            pltpu.VMEM(big, jnp.float32),
            pltpu.VMEM((len(plan),) + big, jnp.float32),
            pltpu.VMEM((slots,) + big, jnp.float32),
            pltpu.SemaphoreType.DMA((slots,)),
            pltpu.SemaphoreType.DMA((slots,)),
        ],
        compiler_params=pltpu.CompilerParams(collective_id=0, has_side_effects=True),
    )(stacked, given, coef)


def shards(velocity, old_advection, lower_gap, upper_gap):
    gap_sum = lower_gap + upper_gap
    lower_coef = -2.0 * STIFF / (gap_sum * lower_gap)
    upper_coef = -2.0 * STIFF / (gap_sum * upper_gap)
    diagonal = 1.0 - lower_coef - upper_coef
    given, table = coefficient_table(lower_coef, upper_coef, diagonal)
    given, table, velocity, old_advection = lax.optimization_barrier((given, table, velocity, old_advection))
    planes = velocity.shape[3]
    padded = extended(velocity, (("gx", 3),), 4, True)
    stream = stream_slope(padded, planes)
    spanwise = roll_slope(velocity, 2)
    rimmed = extended(velocity, (("gy", 1),), 1, False)
    gap_sum = lower_gap + upper_gap
    normal_slope = (rimmed[:, 2:] - rimmed[:, :-2]) / gap_sum[None, :, None, None]
    advection = -(
        velocity[0][None] * stream + velocity[1][None] * normal_slope + velocity[2][None] * spanwise
    )
    forcing = velocity + GAMMA * advection + ZETA * old_advection
    rows_here = velocity.shape[1]

    stacked = jnp.transpose(forcing, (1, 0, 2, 3)).reshape(rows_here, LINES, 128)
    solved = carry_solve(stacked, given, table)
    finished = jnp.transpose(solved.reshape(rows_here, 3, 32, -1), (1, 0, 2, 3))
    return (finished.reshape(velocity.shape), advection)


def solution(mesh):
    return jax.shard_map(
        shards,
        mesh=mesh,
        in_specs=(P(None, "gy", None, "gx"), P(None, "gy", None, "gx"), P("gy"), P("gy")),
        out_specs=(P(None, "gy", None, "gx"), P(None, "gy", None, "gx")),
        check_vma=False,
    )
```

```python
import functools

import jax
import jax.numpy as jnp
from jax import lax
from jax.sharding import PartitionSpec as P
from jax.experimental import pallas as pl
from jax.experimental.pallas import tpu as pltpu

MESH = pl.DeviceIdType.MESH
LINES = 96

STIFF = 1024


STENCIL = (0.8, -0.2, 4.0 / 105.0, -1.0 / 280.0)
GAMMA = 5.0 / 12.0
ZETA = -17.0 / 60.0


def extended(array, sides, width, wrap):
    for axis, dim in sides:
        size, length = (lax.axis_size(axis), array.shape[dim])
        up = [(i, (i + 1) % size) for i in range(size if wrap else size - 1)]
        down = [(j, i) for i, j in up]
        last = lax.slice_in_dim(array, length - width, length, axis=dim)
        first = lax.slice_in_dim(array, 0, width, axis=dim)
        before = lax.ppermute(last, axis, up)
        after = lax.ppermute(first, axis, down)
        array = jnp.concatenate([before, array, after], axis=dim)
    return array


def prefix(value, axis, join, neutral, backward):
    count, mine = (lax.axis_size(axis), lax.axis_index(axis))
    step = -1 if backward else 1
    order = [(i, i + step) for i in range(count) if 0 <= i + step < count]
    total = jax.tree.map(lambda part: lax.ppermute(part, axis, order), value)
    inside = (mine >= 1) if not backward else (mine <= count - 2)
    total = jax.tree.map(
        lambda part, zero: jnp.where(inside, part, jnp.full_like(part, 0) + jnp.asarray(zero, part.dtype)),
        total,
        neutral,
    )
    offset = 1
    while offset < count:
        pairs = [(i, i + step * offset) for i in range(count) if 0 <= i + step * offset < count]
        earlier = jax.tree.map(lambda part: lax.ppermute(part, axis, pairs), total)
        longer = join(earlier, total)
        reach = (mine >= offset) if not backward else (mine <= count - 1 - offset)
        total = jax.tree.map(lambda new, old: jnp.where(reach, new, old), longer, total)
        offset *= 2
    return total


def ratio_join(earlier, latter):
    def entry(i, j):
        return latter[2 * i : 2 * i + 1] * earlier[j : j + 1] + latter[2 * i + 1 : 2 * i + 2] * earlier[2 + j : 3 + j]

    entries = [entry(0, 0), entry(0, 1), entry(1, 0), entry(1, 1)]
    big = jnp.maximum(
        jnp.maximum(jnp.abs(entries[0]), jnp.abs(entries[1])),
        jnp.maximum(jnp.abs(entries[2]), jnp.abs(entries[3])),
    )
    rows = [part / big for part in entries]
    return jnp.concatenate(rows + [jnp.zeros((4, 128), jnp.float32)], axis=0)


def line_join(earlier, latter):
    factor = latter[LINES : LINES + 1, :]
    joined_lines = latter[:LINES] + factor * earlier[:LINES]
    joined_scale = latter[LINES:] * earlier[LINES:]
    return jnp.concatenate([joined_lines, joined_scale], axis=0)


def ratio_neutral():
    unit = jnp.ones((1, 128), jnp.float32)
    blank = jnp.zeros((1, 128), jnp.float32)
    return jnp.concatenate([unit, blank, blank, unit, blank, blank, blank, blank], axis=0)


def line_neutral():
    return jnp.concatenate([jnp.zeros((LINES, 128), jnp.float32), jnp.ones((8, 128), jnp.float32)], axis=0)


def scan_kernel(count, backward, join, neutral, x_ref, out_ref, totals, recv, send_sem, recv_sem):
    me = lax.axis_index("gy")
    row = lax.axis_index("gx")
    sign = -1 if backward else 1
    offsets = [1]
    while offsets[-1] * 2 < count:
        offsets.append(offsets[-1] * 2)
    partners = []
    for offset in offsets:
        partners.append((me + offset) % count)
        if 2 * offset != count:
            partners.append((me + count - offset) % count)
    barrier = pltpu.get_barrier_semaphore()
    for partner in partners:
        pl.semaphore_signal(barrier, inc=1, device_id=(row, partner), device_id_type=MESH)
    pl.semaphore_wait(barrier, len(partners))
    rounds = [1] + offsets
    copies = []
    for step, offset in enumerate(rounds):
        source = x_ref if step == 0 else totals.at[step - 1]
        target = (me + count + sign * offset) % count
        copy = pltpu.make_async_remote_copy(
            src_ref=source,
            dst_ref=recv.at[step],
            send_sem=send_sem.at[step],
            recv_sem=recv_sem.at[step],
            device_id=(row, target),
            device_id_type=MESH,
        )
        copy.start()
        copy.wait_recv()
        copies.append(copy)
        valid = (me + offset <= count - 1) if backward else (me >= offset)
        earlier = recv[step]
        if step == 0:
            totals[step] = jnp.where(valid, earlier, neutral())
        else:
            latter = totals[step - 1]
            totals[step] = jnp.where(valid, join(earlier, latter), latter)
    out_ref[...] = totals[len(rounds) - 1]
    for copy in copies:
        copy.wait_send()


def line_scan(step_value, backward):
    count = lax.axis_size("gy")
    factor, lines = step_value
    shape = lines.shape
    packed = jnp.concatenate(
        [lines.reshape(LINES, 128), jnp.broadcast_to(factor.reshape(1, 1), (8, 128))], axis=0
    )
    rounds = 1
    while (1 << (rounds - 1)) * 2 < count:
        rounds += 1
    rounds += 1
    result = pl.pallas_call(
        functools.partial(scan_kernel, count, backward, line_join, line_neutral),
        out_shape=jax.ShapeDtypeStruct(packed.shape, jnp.float32),
        in_specs=[pl.BlockSpec(memory_space=pltpu.VMEM)],
        out_specs=pl.BlockSpec(memory_space=pltpu.VMEM),
        scratch_shapes=[
            pltpu.VMEM((rounds,) + packed.shape, jnp.float32),
            pltpu.VMEM((rounds,) + packed.shape, jnp.float32),
            pltpu.SemaphoreType.DMA((rounds,)),
            pltpu.SemaphoreType.DMA((rounds,)),
        ],
        compiler_params=pltpu.CompilerParams(collective_id=1 if backward else 0, has_side_effects=True),
    )(packed)
    return result[:LINES].reshape(shape)


def ratio_scan(matrix):
    count = lax.axis_size("gy")
    packed = jnp.concatenate(
        [jnp.broadcast_to(matrix.reshape(4, 1), (4, 128)), jnp.zeros((4, 128), jnp.float32)], axis=0
    )
    rounds = 1
    while (1 << (rounds - 1)) * 2 < count:
        rounds += 1
    rounds += 1
    result = pl.pallas_call(
        functools.partial(scan_kernel, count, False, ratio_join, ratio_neutral),
        out_shape=jax.ShapeDtypeStruct(packed.shape, jnp.float32),
        in_specs=[pl.BlockSpec(memory_space=pltpu.VMEM)],
        out_specs=pl.BlockSpec(memory_space=pltpu.VMEM),
        scratch_shapes=[
            pltpu.VMEM((rounds,) + packed.shape, jnp.float32),
            pltpu.VMEM((rounds,) + packed.shape, jnp.float32),
            pltpu.SemaphoreType.DMA((rounds,)),
            pltpu.SemaphoreType.DMA((rounds,)),
        ],
        compiler_params=pltpu.CompilerParams(collective_id=2, has_side_effects=True),
    )(packed)
    return result[:4, 0].reshape(2, 2)


def prefix_kernel(count, group, rows_here, element_ref, table_ref, out_ref, pieces, send_sem, recv_sem, local_sem):
    mine = lax.axis_index("gy")
    row = lax.axis_index("gx")
    teams = count // group
    team = mine // group
    seat = mine % group
    barrier = pltpu.get_barrier_semaphore()
    partners = [team * group + (seat + step) % group for step in range(1, group)]
    partners += [((team + step) % teams) * group + seat for step in range(1, teams)]
    for partner in partners:
        pl.semaphore_signal(barrier, inc=1, device_id=(row, partner), device_id_type=MESH)
    pl.semaphore_wait(barrier, len(partners))

    own = pltpu.make_async_copy(element_ref, pieces.at[mine], local_sem.at[0])
    own.start()

    def mate_copy(step, source_seat, target_seat):
        return pltpu.make_async_remote_copy(
            src_ref=element_ref,
            dst_ref=pieces.at[team * group + source_seat],
            send_sem=send_sem.at[step],
            recv_sem=recv_sem.at[source_seat],
            device_id=(row, team * group + target_seat),
            device_id_type=MESH,
        )

    def team_copy(step, source_team, target_team):
        block = pieces.at[pl.ds(source_team * group, group)]
        return pltpu.make_async_remote_copy(
            src_ref=block,
            dst_ref=block,
            send_sem=send_sem.at[group + step],
            recv_sem=recv_sem.at[group + source_team],
            device_id=(row, target_team * group + seat),
            device_id_type=MESH,
        )

    for step in range(1, group):
        mate_copy(step, seat, (seat + step) % group).start()
    for step in range(1, group):
        mate_copy(step, (seat + group - step) % group, seat).wait_recv()
    own.wait()
    for step in range(1, teams):
        team_copy(step, team, (team + step) % teams).start()
    for step in range(1, teams):
        team_copy(step, (team + teams - step) % teams, team).wait_recv()

    def turn(position, total):
        piece = pieces[position]
        entries = [
            piece[2 * i : 2 * i + 1] * total[j] + piece[2 * i + 1 : 2 * i + 2] * total[2 + j]
            for i in range(2)
            for j in range(2)
        ]
        big = jnp.maximum(
            jnp.maximum(jnp.abs(entries[0]), jnp.abs(entries[1])),
            jnp.maximum(jnp.abs(entries[2]), jnp.abs(entries[3])),
        )
        inside = position < mine
        return tuple(jnp.where(inside, value / big, old) for value, old in zip(entries, total))

    unit = jnp.ones((1, 128), jnp.float32)
    blank = jnp.zeros((1, 128), jnp.float32)
    total = lax.fori_loop(0, count - 1, turn, (unit, blank, blank, unit))
    modified_prev = total[1] / total[3]
    weight = unit
    for i in range(rows_here):
        lower = table_ref[i : i + 1]
        upper = table_ref[16 + i : 17 + i]
        diagonal = table_ref[32 + i : 33 + i]
        pivot = diagonal - lower * modified_prev
        modified_prev = upper / pivot
        weight = -lower / pivot * weight
        out_ref[i : i + 1] = pivot
        out_ref[16 + i : 17 + i] = modified_prev
        out_ref[32 + i : 33 + i] = weight
    for step in range(1, group):
        mate_copy(step, seat, (seat + step) % group).wait_send()
    for step in range(1, teams):
        team_copy(step, team, (team + step) % teams).wait_send()


def team_size(count):
    if count > 16 and count % 16 == 0:
        return 16
    return max(1, count // 2)


def matrix_kernel(rows_here, table_ref, out_ref):
    unit = jnp.ones((1, 128), jnp.float32)
    blank = jnp.zeros((1, 128), jnp.float32)
    top = (unit, blank)
    bottom = (blank, unit)
    for i in range(rows_here):
        scale = 1.0 / table_ref[32 + i : 33 + i]
        up = table_ref[16 + i : 17 + i] * scale
        low = -table_ref[i : i + 1] * scale
        top, bottom = (
            (up * bottom[0], up * bottom[1]),
            (low * top[0] + bottom[0], low * top[1] + bottom[1]),
        )
    big = jnp.maximum(
        jnp.maximum(jnp.abs(top[0]), jnp.abs(top[1])), jnp.maximum(jnp.abs(bottom[0]), jnp.abs(bottom[1]))
    )
    out_ref[...] = jnp.concatenate(
        [top[0] / big, top[1] / big, bottom[0] / big, bottom[1] / big, blank, blank, blank, blank], axis=0
    )


def coefficient_table(lower_coef, upper_coef, diagonal):
    count = lax.axis_size("gy")
    rows_here = lower_coef.shape[0]
    filler = jnp.zeros((16 - rows_here,), jnp.float32)
    column = jnp.concatenate([lower_coef, filler, upper_coef, filler, diagonal, filler])
    table = jnp.broadcast_to(column.reshape(48, 1), (48, 128))
    element = pl.pallas_call(
        functools.partial(matrix_kernel, rows_here),
        out_shape=jax.ShapeDtypeStruct((8, 128), jnp.float32),
        in_specs=[pl.BlockSpec(memory_space=pltpu.VMEM)],
        out_specs=pl.BlockSpec(memory_space=pltpu.VMEM),
    )(table)
    return table, pl.pallas_call(
        functools.partial(prefix_kernel, count, team_size(count), rows_here),
        out_shape=jax.ShapeDtypeStruct((48, 128), jnp.float32),
        in_specs=[pl.BlockSpec(memory_space=pltpu.VMEM)] * 2,
        out_specs=pl.BlockSpec(memory_space=pltpu.VMEM),
        scratch_shapes=[
            pltpu.VMEM((count, 8, 128), jnp.float32),
            pltpu.SemaphoreType.DMA((team_size(count) + count // team_size(count),)),
            pltpu.SemaphoreType.DMA((team_size(count) + count // team_size(count),)),
            pltpu.SemaphoreType.DMA((1,)),
        ],
        compiler_params=pltpu.CompilerParams(collective_id=1, has_side_effects=True),
    )(element, table)


def stream_slope(padded, planes):
    summed = STENCIL[0] * (padded[..., 5 : 5 + planes] - padded[..., 3 : 3 + planes])
    for offset in range(2, 5):
        summed = summed + STENCIL[offset - 1] * (
            padded[..., 4 + offset : 4 + offset + planes]
            - padded[..., 4 - offset : 4 - offset + planes]
        )
    return summed


def roll_slope(values, along_axis):
    summed = STENCIL[0] * (jnp.roll(values, -1, along_axis) - jnp.roll(values, 1, along_axis))
    for offset in range(2, 5):
        summed = summed + STENCIL[offset - 1] * (
            jnp.roll(values, -offset, along_axis) - jnp.roll(values, offset, along_axis)
        )
    return summed


def compose(earlier, latter):
    return (latter[0] * earlier[0], latter[1] + latter[0] * earlier[1])


def chain_ratio(earlier, latter):
    product = jnp.dot(latter, earlier, precision=lax.Precision.HIGHEST)
    return product / jnp.max(jnp.abs(product))


def ratio_matrix(cross_term, top_right, bottom_left):
    unit_entry = jnp.ones((), jnp.float32)
    return jnp.stack([jnp.stack([cross_term, top_right]), jnp.stack([bottom_left, unit_entry])])


def radix_plan(count):
    plan = [list(range(1, min(4, count - 1) + 1))]
    span = len(plan[0])
    while span < count - 1:
        offsets = [span * j for j in range(1, 4) if span * j < count]
        plan.append(offsets)
        span = span * (1 + len(offsets))
    return plan


def radix_scan(me, row, count, backward, element, parts, recv, send_sem, recv_sem, base, copies):
    sign = -1 if backward else 1
    plan = radix_plan(count)
    slot = base
    for level, offsets in enumerate(plan):
        source = element if level == 0 else parts.at[level - 1]
        started = []
        for offset in offsets:
            target = (me + count + sign * offset) % count
            copy = pltpu.make_async_remote_copy(
                src_ref=source,
                dst_ref=recv.at[slot],
                send_sem=send_sem.at[slot],
                recv_sem=recv_sem.at[slot],
                device_id=(row, target),
                device_id_type=MESH,
            )
            copy.start()
            started.append((offset, slot, copy))
            slot += 1
        acc = line_neutral() if level == 0 else parts[level - 1]
        for offset, index, copy in started:
            copy.wait_recv()
            copies.append(copy)
            valid = (me + offset <= count - 1) if backward else (me >= offset)
            acc = jnp.where(valid, line_join(recv[index], acc), acc)
        parts[level] = acc
    return parts[len(plan) - 1]


def carry_kernel(count, rows_here, rows_ref, given_ref, coef_ref, out_ref, down_element, parts_down, up_element,
                 parts_up, recv, send_sem, recv_sem):
    me = lax.axis_index("gy")
    row = lax.axis_index("gx")
    plan = radix_plan(count)
    residues = set()
    for offsets in plan:
        for offset in offsets:
            residues.add(offset % count)
            residues.add((count - offset) % count)
    residues.discard(0)
    barrier = pltpu.get_barrier_semaphore()
    for residue in sorted(residues):
        pl.semaphore_signal(barrier, inc=1, device_id=(row, (me + residue) % count), device_id_type=MESH)
    pl.semaphore_wait(barrier, len(residues))
    copies = []
    slots = sum(len(offsets) for offsets in plan)

    coef = coef_ref[...]
    given = given_ref[...]
    carried = None
    for i in range(rows_here):
        lower = given[i : i + 1]
        pivot = coef[i : i + 1]
        carried = rows_ref[i] / pivot if carried is None else (rows_ref[i] - lower * carried) / pivot
        out_ref[i] = carried
    down_element[...] = jnp.concatenate(
        [carried, jnp.broadcast_to(coef[32 + rows_here - 1 : 32 + rows_here], (8, 128))], axis=0
    )
    below_carry = radix_scan(
        me, row, count, False, down_element, parts_down, recv, send_sem, recv_sem, 0, copies
    )[:LINES]
    carried = None
    weight = None
    for i in reversed(range(rows_here)):
        sensitivity = coef[32 + i : 33 + i]
        modified = coef[16 + i : 17 + i]
        reduced = out_ref[i] + sensitivity * below_carry
        if carried is None:
            carried = reduced
            weight = -modified
        else:
            carried = reduced - modified * carried
            weight = -modified * weight
        out_ref[i] = carried
    up_element[...] = jnp.concatenate([carried, jnp.broadcast_to(weight, (8, 128))], axis=0)
    above_carry = radix_scan(
        me, row, count, True, up_element, parts_up, recv, send_sem, recv_sem, slots, copies
    )[:LINES]
    weight = None
    for i in reversed(range(rows_here)):
        modified = coef[16 + i : 17 + i]
        weight = -modified if weight is None else -modified * weight
        out_ref[i] = out_ref[i] + weight * above_carry
    for copy in copies:
        copy.wait_send()


def carry_solve(stacked, given, coef):
    count = lax.axis_size("gy")
    rows_here = stacked.shape[0]
    plan = radix_plan(count)
    slots = 2 * sum(len(offsets) for offsets in plan)
    big = (LINES + 8, 128)
    return pl.pallas_call(
        functools.partial(carry_kernel, count, rows_here),
        out_shape=jax.ShapeDtypeStruct((rows_here, LINES, 128), jnp.float32),
        in_specs=[pl.BlockSpec(memory_space=pltpu.VMEM)] * 3,
        out_specs=pl.BlockSpec(memory_space=pltpu.VMEM),
        scratch_shapes=[
            pltpu.VMEM(big, jnp.float32),
            pltpu.VMEM((len(plan),) + big, jnp.float32),
            pltpu.VMEM(big, jnp.float32),
            pltpu.VMEM((len(plan),) + big, jnp.float32),
            pltpu.VMEM((slots,) + big, jnp.float32),
            pltpu.SemaphoreType.DMA((slots,)),
            pltpu.SemaphoreType.DMA((slots,)),
        ],
        compiler_params=pltpu.CompilerParams(collective_id=0, has_side_effects=True),
    )(stacked, given, coef)


def shards(velocity, old_advection, lower_gap, upper_gap):
    planes = velocity.shape[3]
    padded = extended(velocity, (("gx", 3),), 4, True)
    stream = stream_slope(padded, planes)
    spanwise = roll_slope(velocity, 2)
    rimmed = extended(velocity, (("gy", 1),), 1, False)
    gap_sum = lower_gap + upper_gap
    normal_slope = (rimmed[:, 2:] - rimmed[:, :-2]) / gap_sum[None, :, None, None]
    advection = -(
        velocity[0][None] * stream + velocity[1][None] * normal_slope + velocity[2][None] * spanwise
    )
    forcing = velocity + GAMMA * advection + ZETA * old_advection
    lower_coef = -2.0 * STIFF / (gap_sum * lower_gap)
    upper_coef = -2.0 * STIFF / (gap_sum * upper_gap)
    diagonal = 1.0 - lower_coef - upper_coef
    rows_here = velocity.shape[1]

    given, table = coefficient_table(lower_coef, upper_coef, diagonal)
    stacked = jnp.transpose(forcing, (1, 0, 2, 3)).reshape(rows_here, LINES, 128)
    solved = carry_solve(stacked, given, table)
    finished = jnp.transpose(solved.reshape(rows_here, 3, 32, -1), (1, 0, 2, 3))
    return (finished.reshape(velocity.shape), advection)


def solution(mesh):
    return jax.shard_map(
        shards,
        mesh=mesh,
        in_specs=(P(None, "gy", None, "gx"), P(None, "gy", None, "gx"), P("gy"), P("gy")),
        out_specs=(P(None, "gy", None, "gx"), P(None, "gy", None, "gx")),
        check_vma=False,
    )
```

```python
import functools

import jax
import jax.numpy as jnp
from jax import lax
from jax.sharding import PartitionSpec as P
from jax.experimental import pallas as pl
from jax.experimental.pallas import tpu as pltpu

MESH = pl.DeviceIdType.MESH
LINES = 96

STIFF = 1024


STENCIL = (0.8, -0.2, 4.0 / 105.0, -1.0 / 280.0)
GAMMA = 5.0 / 12.0
ZETA = -17.0 / 60.0


def extended(array, sides, width, wrap):
    for axis, dim in sides:
        size, length = (lax.axis_size(axis), array.shape[dim])
        up = [(i, (i + 1) % size) for i in range(size if wrap else size - 1)]
        down = [(j, i) for i, j in up]
        last = lax.slice_in_dim(array, length - width, length, axis=dim)
        first = lax.slice_in_dim(array, 0, width, axis=dim)
        before = lax.ppermute(last, axis, up)
        after = lax.ppermute(first, axis, down)
        array = jnp.concatenate([before, array, after], axis=dim)
    return array


def prefix(value, axis, join, neutral, backward):
    count, mine = (lax.axis_size(axis), lax.axis_index(axis))
    step = -1 if backward else 1
    order = [(i, i + step) for i in range(count) if 0 <= i + step < count]
    total = jax.tree.map(lambda part: lax.ppermute(part, axis, order), value)
    inside = (mine >= 1) if not backward else (mine <= count - 2)
    total = jax.tree.map(
        lambda part, zero: jnp.where(inside, part, jnp.full_like(part, 0) + jnp.asarray(zero, part.dtype)),
        total,
        neutral,
    )
    offset = 1
    while offset < count:
        pairs = [(i, i + step * offset) for i in range(count) if 0 <= i + step * offset < count]
        earlier = jax.tree.map(lambda part: lax.ppermute(part, axis, pairs), total)
        longer = join(earlier, total)
        reach = (mine >= offset) if not backward else (mine <= count - 1 - offset)
        total = jax.tree.map(lambda new, old: jnp.where(reach, new, old), longer, total)
        offset *= 2
    return total


def ratio_join(earlier, latter):
    def entry(i, j):
        return latter[2 * i : 2 * i + 1] * earlier[j : j + 1] + latter[2 * i + 1 : 2 * i + 2] * earlier[2 + j : 3 + j]

    entries = [entry(0, 0), entry(0, 1), entry(1, 0), entry(1, 1)]
    big = jnp.maximum(
        jnp.maximum(jnp.abs(entries[0]), jnp.abs(entries[1])),
        jnp.maximum(jnp.abs(entries[2]), jnp.abs(entries[3])),
    )
    rows = [part / big for part in entries]
    return jnp.concatenate(rows + [jnp.zeros((4, 128), jnp.float32)], axis=0)


def line_join(earlier, latter):
    factor = latter[LINES : LINES + 1, :]
    joined_lines = latter[:LINES] + factor * earlier[:LINES]
    joined_scale = latter[LINES:] * earlier[LINES:]
    return jnp.concatenate([joined_lines, joined_scale], axis=0)


def ratio_neutral():
    unit = jnp.ones((1, 128), jnp.float32)
    blank = jnp.zeros((1, 128), jnp.float32)
    return jnp.concatenate([unit, blank, blank, unit, blank, blank, blank, blank], axis=0)


def line_neutral():
    return jnp.concatenate([jnp.zeros((LINES, 128), jnp.float32), jnp.ones((8, 128), jnp.float32)], axis=0)


def scan_kernel(count, backward, join, neutral, x_ref, out_ref, totals, recv, send_sem, recv_sem):
    me = lax.axis_index("gy")
    row = lax.axis_index("gx")
    sign = -1 if backward else 1
    offsets = [1]
    while offsets[-1] * 2 < count:
        offsets.append(offsets[-1] * 2)
    partners = []
    for offset in offsets:
        partners.append((me + offset) % count)
        if 2 * offset != count:
            partners.append((me + count - offset) % count)
    barrier = pltpu.get_barrier_semaphore()
    for partner in partners:
        pl.semaphore_signal(barrier, inc=1, device_id=(row, partner), device_id_type=MESH)
    pl.semaphore_wait(barrier, len(partners))
    rounds = [1] + offsets
    copies = []
    for step, offset in enumerate(rounds):
        source = x_ref if step == 0 else totals.at[step - 1]
        target = (me + count + sign * offset) % count
        copy = pltpu.make_async_remote_copy(
            src_ref=source,
            dst_ref=recv.at[step],
            send_sem=send_sem.at[step],
            recv_sem=recv_sem.at[step],
            device_id=(row, target),
            device_id_type=MESH,
        )
        copy.start()
        copy.wait_recv()
        copies.append(copy)
        valid = (me + offset <= count - 1) if backward else (me >= offset)
        earlier = recv[step]
        if step == 0:
            totals[step] = jnp.where(valid, earlier, neutral())
        else:
            latter = totals[step - 1]
            totals[step] = jnp.where(valid, join(earlier, latter), latter)
    out_ref[...] = totals[len(rounds) - 1]
    for copy in copies:
        copy.wait_send()


def line_scan(step_value, backward):
    count = lax.axis_size("gy")
    factor, lines = step_value
    shape = lines.shape
    packed = jnp.concatenate(
        [lines.reshape(LINES, 128), jnp.broadcast_to(factor.reshape(1, 1), (8, 128))], axis=0
    )
    rounds = 1
    while (1 << (rounds - 1)) * 2 < count:
        rounds += 1
    rounds += 1
    result = pl.pallas_call(
        functools.partial(scan_kernel, count, backward, line_join, line_neutral),
        out_shape=jax.ShapeDtypeStruct(packed.shape, jnp.float32),
        in_specs=[pl.BlockSpec(memory_space=pltpu.VMEM)],
        out_specs=pl.BlockSpec(memory_space=pltpu.VMEM),
        scratch_shapes=[
            pltpu.VMEM((rounds,) + packed.shape, jnp.float32),
            pltpu.VMEM((rounds,) + packed.shape, jnp.float32),
            pltpu.SemaphoreType.DMA((rounds,)),
            pltpu.SemaphoreType.DMA((rounds,)),
        ],
        compiler_params=pltpu.CompilerParams(collective_id=1 if backward else 0, has_side_effects=True),
    )(packed)
    return result[:LINES].reshape(shape)


def ratio_scan(matrix):
    count = lax.axis_size("gy")
    packed = jnp.concatenate(
        [jnp.broadcast_to(matrix.reshape(4, 1), (4, 128)), jnp.zeros((4, 128), jnp.float32)], axis=0
    )
    rounds = 1
    while (1 << (rounds - 1)) * 2 < count:
        rounds += 1
    rounds += 1
    result = pl.pallas_call(
        functools.partial(scan_kernel, count, False, ratio_join, ratio_neutral),
        out_shape=jax.ShapeDtypeStruct(packed.shape, jnp.float32),
        in_specs=[pl.BlockSpec(memory_space=pltpu.VMEM)],
        out_specs=pl.BlockSpec(memory_space=pltpu.VMEM),
        scratch_shapes=[
            pltpu.VMEM((rounds,) + packed.shape, jnp.float32),
            pltpu.VMEM((rounds,) + packed.shape, jnp.float32),
            pltpu.SemaphoreType.DMA((rounds,)),
            pltpu.SemaphoreType.DMA((rounds,)),
        ],
        compiler_params=pltpu.CompilerParams(collective_id=2, has_side_effects=True),
    )(packed)
    return result[:4, 0].reshape(2, 2)


def prefix_kernel(count, group, rows_here, element_ref, table_ref, out_ref, pieces, send_sem, recv_sem, local_sem):
    mine = lax.axis_index("gy")
    row = lax.axis_index("gx")
    teams = count // group
    team = mine // group
    seat = mine % group
    barrier = pltpu.get_barrier_semaphore()
    partners = [team * group + (seat + step) % group for step in range(1, group)]
    partners += [((team + step) % teams) * group + seat for step in range(1, teams)]
    for partner in partners:
        pl.semaphore_signal(barrier, inc=1, device_id=(row, partner), device_id_type=MESH)
    pl.semaphore_wait(barrier, len(partners))

    own = pltpu.make_async_copy(element_ref, pieces.at[mine], local_sem.at[0])
    own.start()

    def mate_copy(step, source_seat, target_seat):
        return pltpu.make_async_remote_copy(
            src_ref=element_ref,
            dst_ref=pieces.at[team * group + source_seat],
            send_sem=send_sem.at[step],
            recv_sem=recv_sem.at[source_seat],
            device_id=(row, team * group + target_seat),
            device_id_type=MESH,
        )

    def team_copy(step, source_team, target_team):
        block = pieces.at[pl.ds(source_team * group, group)]
        return pltpu.make_async_remote_copy(
            src_ref=block,
            dst_ref=block,
            send_sem=send_sem.at[group + step],
            recv_sem=recv_sem.at[group + source_team],
            device_id=(row, target_team * group + seat),
            device_id_type=MESH,
        )

    for step in range(1, group):
        mate_copy(step, seat, (seat + step) % group).start()
    for step in range(1, group):
        mate_copy(step, (seat + group - step) % group, seat).wait_recv()
    own.wait()
    for step in range(1, teams):
        team_copy(step, team, (team + step) % teams).start()
    for step in range(1, teams):
        team_copy(step, (team + teams - step) % teams, team).wait_recv()

    def turn(position, total):
        piece = pieces[position]
        entries = [
            piece[2 * i : 2 * i + 1] * total[j] + piece[2 * i + 1 : 2 * i + 2] * total[2 + j]
            for i in range(2)
            for j in range(2)
        ]
        big = jnp.maximum(
            jnp.maximum(jnp.abs(entries[0]), jnp.abs(entries[1])),
            jnp.maximum(jnp.abs(entries[2]), jnp.abs(entries[3])),
        )
        inside = position < mine
        shrink = 1.0 / big
        return tuple(jnp.where(inside, value * shrink, old) for value, old in zip(entries, total))

    unit = jnp.ones((1, 128), jnp.float32)
    blank = jnp.zeros((1, 128), jnp.float32)
    total = lax.fori_loop(0, count - 1, turn, (unit, blank, blank, unit))
    modified_prev = total[1] / total[3]
    weight = unit
    for i in range(rows_here):
        lower = table_ref[i : i + 1]
        upper = table_ref[16 + i : 17 + i]
        diagonal = table_ref[32 + i : 33 + i]
        pivot = diagonal - lower * modified_prev
        modified_prev = upper / pivot
        weight = -lower / pivot * weight
        out_ref[i : i + 1] = pivot
        out_ref[16 + i : 17 + i] = modified_prev
        out_ref[32 + i : 33 + i] = weight
    for step in range(1, group):
        mate_copy(step, seat, (seat + step) % group).wait_send()
    for step in range(1, teams):
        team_copy(step, team, (team + step) % teams).wait_send()


def team_size(count):
    if count > 16 and count % 16 == 0:
        return 16
    return max(1, count // 2)


def matrix_kernel(rows_here, table_ref, out_ref):
    unit = jnp.ones((1, 128), jnp.float32)
    blank = jnp.zeros((1, 128), jnp.float32)
    top = (unit, blank)
    bottom = (blank, unit)
    for i in range(rows_here):
        scale = 1.0 / table_ref[32 + i : 33 + i]
        up = table_ref[16 + i : 17 + i] * scale
        low = -table_ref[i : i + 1] * scale
        top, bottom = (
            (up * bottom[0], up * bottom[1]),
            (low * top[0] + bottom[0], low * top[1] + bottom[1]),
        )
    big = jnp.maximum(
        jnp.maximum(jnp.abs(top[0]), jnp.abs(top[1])), jnp.maximum(jnp.abs(bottom[0]), jnp.abs(bottom[1]))
    )
    out_ref[...] = jnp.concatenate(
        [top[0] / big, top[1] / big, bottom[0] / big, bottom[1] / big, blank, blank, blank, blank], axis=0
    )


def coefficient_table(lower_coef, upper_coef, diagonal):
    count = lax.axis_size("gy")
    rows_here = lower_coef.shape[0]
    filler = jnp.zeros((16 - rows_here,), jnp.float32)
    column = jnp.concatenate([lower_coef, filler, upper_coef, filler, diagonal, filler])
    table = jnp.broadcast_to(column.reshape(48, 1), (48, 128))
    element = pl.pallas_call(
        functools.partial(matrix_kernel, rows_here),
        out_shape=jax.ShapeDtypeStruct((8, 128), jnp.float32),
        in_specs=[pl.BlockSpec(memory_space=pltpu.VMEM)],
        out_specs=pl.BlockSpec(memory_space=pltpu.VMEM),
    )(table)
    return table, pl.pallas_call(
        functools.partial(prefix_kernel, count, team_size(count), rows_here),
        out_shape=jax.ShapeDtypeStruct((48, 128), jnp.float32),
        in_specs=[pl.BlockSpec(memory_space=pltpu.VMEM)] * 2,
        out_specs=pl.BlockSpec(memory_space=pltpu.VMEM),
        scratch_shapes=[
            pltpu.VMEM((count, 8, 128), jnp.float32),
            pltpu.SemaphoreType.DMA((team_size(count) + count // team_size(count),)),
            pltpu.SemaphoreType.DMA((team_size(count) + count // team_size(count),)),
            pltpu.SemaphoreType.DMA((1,)),
        ],
        compiler_params=pltpu.CompilerParams(collective_id=1, has_side_effects=True),
    )(element, table)


def stream_slope(padded, planes):
    summed = STENCIL[0] * (padded[..., 5 : 5 + planes] - padded[..., 3 : 3 + planes])
    for offset in range(2, 5):
        summed = summed + STENCIL[offset - 1] * (
            padded[..., 4 + offset : 4 + offset + planes]
            - padded[..., 4 - offset : 4 - offset + planes]
        )
    return summed


def roll_slope(values, along_axis):
    summed = STENCIL[0] * (jnp.roll(values, -1, along_axis) - jnp.roll(values, 1, along_axis))
    for offset in range(2, 5):
        summed = summed + STENCIL[offset - 1] * (
            jnp.roll(values, -offset, along_axis) - jnp.roll(values, offset, along_axis)
        )
    return summed


def compose(earlier, latter):
    return (latter[0] * earlier[0], latter[1] + latter[0] * earlier[1])


def chain_ratio(earlier, latter):
    product = jnp.dot(latter, earlier, precision=lax.Precision.HIGHEST)
    return product / jnp.max(jnp.abs(product))


def ratio_matrix(cross_term, top_right, bottom_left):
    unit_entry = jnp.ones((), jnp.float32)
    return jnp.stack([jnp.stack([cross_term, top_right]), jnp.stack([bottom_left, unit_entry])])


def radix_plan(count):
    plan = [list(range(1, min(4, count - 1) + 1))]
    span = len(plan[0])
    while span < count - 1:
        offsets = [span * j for j in range(1, 4) if span * j < count]
        plan.append(offsets)
        span = span * (1 + len(offsets))
    return plan


def radix_scan(me, row, count, backward, element, parts, recv, send_sem, recv_sem, base, copies):
    sign = -1 if backward else 1
    plan = radix_plan(count)
    slot = base
    for level, offsets in enumerate(plan):
        source = element if level == 0 else parts.at[level - 1]
        started = []
        for offset in offsets:
            target = (me + count + sign * offset) % count
            copy = pltpu.make_async_remote_copy(
                src_ref=source,
                dst_ref=recv.at[slot],
                send_sem=send_sem.at[slot],
                recv_sem=recv_sem.at[slot],
                device_id=(row, target),
                device_id_type=MESH,
            )
            copy.start()
            started.append((offset, slot, copy))
            slot += 1
        acc = line_neutral() if level == 0 else parts[level - 1]
        for offset, index, copy in started:
            copy.wait_recv()
            copies.append(copy)
            valid = (me + offset <= count - 1) if backward else (me >= offset)
            acc = jnp.where(valid, line_join(recv[index], acc), acc)
        parts[level] = acc
    return parts[len(plan) - 1]


def carry_kernel(count, rows_here, rows_ref, given_ref, coef_ref, out_ref, down_element, parts_down, up_element,
                 parts_up, recv, send_sem, recv_sem):
    me = lax.axis_index("gy")
    row = lax.axis_index("gx")
    plan = radix_plan(count)
    residues = set()
    for offsets in plan:
        for offset in offsets:
            residues.add(offset % count)
            residues.add((count - offset) % count)
    residues.discard(0)
    barrier = pltpu.get_barrier_semaphore()
    for residue in sorted(residues):
        pl.semaphore_signal(barrier, inc=1, device_id=(row, (me + residue) % count), device_id_type=MESH)
    pl.semaphore_wait(barrier, len(residues))
    copies = []
    slots = sum(len(offsets) for offsets in plan)

    coef = coef_ref[...]
    given = given_ref[...]
    carried = None
    for i in range(rows_here):
        lower = given[i : i + 1]
        pivot = coef[i : i + 1]
        carried = rows_ref[i] / pivot if carried is None else (rows_ref[i] - lower * carried) / pivot
        out_ref[i] = carried
    down_element[...] = jnp.concatenate(
        [carried, jnp.broadcast_to(coef[32 + rows_here - 1 : 32 + rows_here], (8, 128))], axis=0
    )
    below_carry = radix_scan(
        me, row, count, False, down_element, parts_down, recv, send_sem, recv_sem, 0, copies
    )[:LINES]
    carried = None
    weight = None
    for i in reversed(range(rows_here)):
        sensitivity = coef[32 + i : 33 + i]
        modified = coef[16 + i : 17 + i]
        reduced = out_ref[i] + sensitivity * below_carry
        if carried is None:
            carried = reduced
            weight = -modified
        else:
            carried = reduced - modified * carried
            weight = -modified * weight
        out_ref[i] = carried
    up_element[...] = jnp.concatenate([carried, jnp.broadcast_to(weight, (8, 128))], axis=0)
    above_carry = radix_scan(
        me, row, count, True, up_element, parts_up, recv, send_sem, recv_sem, slots, copies
    )[:LINES]
    weight = None
    for i in reversed(range(rows_here)):
        modified = coef[16 + i : 17 + i]
        weight = -modified if weight is None else -modified * weight
        out_ref[i] = out_ref[i] + weight * above_carry
    for copy in copies:
        copy.wait_send()


def carry_solve(stacked, given, coef):
    count = lax.axis_size("gy")
    rows_here = stacked.shape[0]
    plan = radix_plan(count)
    slots = 2 * sum(len(offsets) for offsets in plan)
    big = (LINES + 8, 128)
    return pl.pallas_call(
        functools.partial(carry_kernel, count, rows_here),
        out_shape=jax.ShapeDtypeStruct((rows_here, LINES, 128), jnp.float32),
        in_specs=[pl.BlockSpec(memory_space=pltpu.VMEM)] * 3,
        out_specs=pl.BlockSpec(memory_space=pltpu.VMEM),
        scratch_shapes=[
            pltpu.VMEM(big, jnp.float32),
            pltpu.VMEM((len(plan),) + big, jnp.float32),
            pltpu.VMEM(big, jnp.float32),
            pltpu.VMEM((len(plan),) + big, jnp.float32),
            pltpu.VMEM((slots,) + big, jnp.float32),
            pltpu.SemaphoreType.DMA((slots,)),
            pltpu.SemaphoreType.DMA((slots,)),
        ],
        compiler_params=pltpu.CompilerParams(collective_id=0, has_side_effects=True),
    )(stacked, given, coef)


def shards(velocity, old_advection, lower_gap, upper_gap):
    planes = velocity.shape[3]
    padded = extended(velocity, (("gx", 3),), 4, True)
    stream = stream_slope(padded, planes)
    spanwise = roll_slope(velocity, 2)
    rimmed = extended(velocity, (("gy", 1),), 1, False)
    gap_sum = lower_gap + upper_gap
    normal_slope = (rimmed[:, 2:] - rimmed[:, :-2]) / gap_sum[None, :, None, None]
    advection = -(
        velocity[0][None] * stream + velocity[1][None] * normal_slope + velocity[2][None] * spanwise
    )
    forcing = velocity + GAMMA * advection + ZETA * old_advection
    lower_coef = -2.0 * STIFF / (gap_sum * lower_gap)
    upper_coef = -2.0 * STIFF / (gap_sum * upper_gap)
    diagonal = 1.0 - lower_coef - upper_coef
    rows_here = velocity.shape[1]

    given, table = coefficient_table(lower_coef, upper_coef, diagonal)
    stacked = jnp.transpose(forcing, (1, 0, 2, 3)).reshape(rows_here, LINES, 128)
    solved = carry_solve(stacked, given, table)
    finished = jnp.transpose(solved.reshape(rows_here, 3, 32, -1), (1, 0, 2, 3))
    return (finished.reshape(velocity.shape), advection)


def solution(mesh):
    return jax.shard_map(
        shards,
        mesh=mesh,
        in_specs=(P(None, "gy", None, "gx"), P(None, "gy", None, "gx"), P("gy"), P("gy")),
        out_specs=(P(None, "gy", None, "gx"), P(None, "gy", None, "gx")),
        check_vma=False,
    )
```

```python
import functools

import jax
import jax.numpy as jnp
from jax import lax
from jax.sharding import PartitionSpec as P
from jax.experimental import pallas as pl
from jax.experimental.pallas import tpu as pltpu

MESH = pl.DeviceIdType.MESH
LINES = 96

STIFF = 1024


STENCIL = (0.8, -0.2, 4.0 / 105.0, -1.0 / 280.0)
GAMMA = 5.0 / 12.0
ZETA = -17.0 / 60.0


def extended(array, sides, width, wrap):
    for axis, dim in sides:
        size, length = (lax.axis_size(axis), array.shape[dim])
        up = [(i, (i + 1) % size) for i in range(size if wrap else size - 1)]
        down = [(j, i) for i, j in up]
        last = lax.slice_in_dim(array, length - width, length, axis=dim)
        first = lax.slice_in_dim(array, 0, width, axis=dim)
        before = lax.ppermute(last, axis, up)
        after = lax.ppermute(first, axis, down)
        array = jnp.concatenate([before, array, after], axis=dim)
    return array


def prefix(value, axis, join, neutral, backward):
    count, mine = (lax.axis_size(axis), lax.axis_index(axis))
    step = -1 if backward else 1
    order = [(i, i + step) for i in range(count) if 0 <= i + step < count]
    total = jax.tree.map(lambda part: lax.ppermute(part, axis, order), value)
    inside = (mine >= 1) if not backward else (mine <= count - 2)
    total = jax.tree.map(
        lambda part, zero: jnp.where(inside, part, jnp.full_like(part, 0) + jnp.asarray(zero, part.dtype)),
        total,
        neutral,
    )
    offset = 1
    while offset < count:
        pairs = [(i, i + step * offset) for i in range(count) if 0 <= i + step * offset < count]
        earlier = jax.tree.map(lambda part: lax.ppermute(part, axis, pairs), total)
        longer = join(earlier, total)
        reach = (mine >= offset) if not backward else (mine <= count - 1 - offset)
        total = jax.tree.map(lambda new, old: jnp.where(reach, new, old), longer, total)
        offset *= 2
    return total


def ratio_join(earlier, latter):
    def entry(i, j):
        return latter[2 * i : 2 * i + 1] * earlier[j : j + 1] + latter[2 * i + 1 : 2 * i + 2] * earlier[2 + j : 3 + j]

    entries = [entry(0, 0), entry(0, 1), entry(1, 0), entry(1, 1)]
    big = jnp.maximum(
        jnp.maximum(jnp.abs(entries[0]), jnp.abs(entries[1])),
        jnp.maximum(jnp.abs(entries[2]), jnp.abs(entries[3])),
    )
    rows = [part / big for part in entries]
    return jnp.concatenate(rows + [jnp.zeros((4, 128), jnp.float32)], axis=0)


def line_join(earlier, latter):
    factor = latter[LINES : LINES + 1, :]
    joined_lines = latter[:LINES] + factor * earlier[:LINES]
    joined_scale = latter[LINES:] * earlier[LINES:]
    return jnp.concatenate([joined_lines, joined_scale], axis=0)


def ratio_neutral():
    unit = jnp.ones((1, 128), jnp.float32)
    blank = jnp.zeros((1, 128), jnp.float32)
    return jnp.concatenate([unit, blank, blank, unit, blank, blank, blank, blank], axis=0)


def line_neutral():
    return jnp.concatenate([jnp.zeros((LINES, 128), jnp.float32), jnp.ones((8, 128), jnp.float32)], axis=0)


def scan_kernel(count, backward, join, neutral, x_ref, out_ref, totals, recv, send_sem, recv_sem):
    me = lax.axis_index("gy")
    row = lax.axis_index("gx")
    sign = -1 if backward else 1
    offsets = [1]
    while offsets[-1] * 2 < count:
        offsets.append(offsets[-1] * 2)
    partners = []
    for offset in offsets:
        partners.append((me + offset) % count)
        if 2 * offset != count:
            partners.append((me + count - offset) % count)
    barrier = pltpu.get_barrier_semaphore()
    for partner in partners:
        pl.semaphore_signal(barrier, inc=1, device_id=(row, partner), device_id_type=MESH)
    pl.semaphore_wait(barrier, len(partners))
    rounds = [1] + offsets
    copies = []
    for step, offset in enumerate(rounds):
        source = x_ref if step == 0 else totals.at[step - 1]
        target = (me + count + sign * offset) % count
        copy = pltpu.make_async_remote_copy(
            src_ref=source,
            dst_ref=recv.at[step],
            send_sem=send_sem.at[step],
            recv_sem=recv_sem.at[step],
            device_id=(row, target),
            device_id_type=MESH,
        )
        copy.start()
        copy.wait_recv()
        copies.append(copy)
        valid = (me + offset <= count - 1) if backward else (me >= offset)
        earlier = recv[step]
        if step == 0:
            totals[step] = jnp.where(valid, earlier, neutral())
        else:
            latter = totals[step - 1]
            totals[step] = jnp.where(valid, join(earlier, latter), latter)
    out_ref[...] = totals[len(rounds) - 1]
    for copy in copies:
        copy.wait_send()


def line_scan(step_value, backward):
    count = lax.axis_size("gy")
    factor, lines = step_value
    shape = lines.shape
    packed = jnp.concatenate(
        [lines.reshape(LINES, 128), jnp.broadcast_to(factor.reshape(1, 1), (8, 128))], axis=0
    )
    rounds = 1
    while (1 << (rounds - 1)) * 2 < count:
        rounds += 1
    rounds += 1
    result = pl.pallas_call(
        functools.partial(scan_kernel, count, backward, line_join, line_neutral),
        out_shape=jax.ShapeDtypeStruct(packed.shape, jnp.float32),
        in_specs=[pl.BlockSpec(memory_space=pltpu.VMEM)],
        out_specs=pl.BlockSpec(memory_space=pltpu.VMEM),
        scratch_shapes=[
            pltpu.VMEM((rounds,) + packed.shape, jnp.float32),
            pltpu.VMEM((rounds,) + packed.shape, jnp.float32),
            pltpu.SemaphoreType.DMA((rounds,)),
            pltpu.SemaphoreType.DMA((rounds,)),
        ],
        compiler_params=pltpu.CompilerParams(collective_id=1 if backward else 0, has_side_effects=True),
    )(packed)
    return result[:LINES].reshape(shape)


def ratio_scan(matrix):
    count = lax.axis_size("gy")
    packed = jnp.concatenate(
        [jnp.broadcast_to(matrix.reshape(4, 1), (4, 128)), jnp.zeros((4, 128), jnp.float32)], axis=0
    )
    rounds = 1
    while (1 << (rounds - 1)) * 2 < count:
        rounds += 1
    rounds += 1
    result = pl.pallas_call(
        functools.partial(scan_kernel, count, False, ratio_join, ratio_neutral),
        out_shape=jax.ShapeDtypeStruct(packed.shape, jnp.float32),
        in_specs=[pl.BlockSpec(memory_space=pltpu.VMEM)],
        out_specs=pl.BlockSpec(memory_space=pltpu.VMEM),
        scratch_shapes=[
            pltpu.VMEM((rounds,) + packed.shape, jnp.float32),
            pltpu.VMEM((rounds,) + packed.shape, jnp.float32),
            pltpu.SemaphoreType.DMA((rounds,)),
            pltpu.SemaphoreType.DMA((rounds,)),
        ],
        compiler_params=pltpu.CompilerParams(collective_id=2, has_side_effects=True),
    )(packed)
    return result[:4, 0].reshape(2, 2)


def prefix_kernel(count, group, rows_here, element_ref, table_ref, out_ref, pieces, send_sem, recv_sem, local_sem):
    mine = lax.axis_index("gy")
    row = lax.axis_index("gx")
    teams = count // group
    team = mine // group
    seat = mine % group
    barrier = pltpu.get_barrier_semaphore()
    partners = [team * group + (seat + step) % group for step in range(1, group)]
    partners += [((team + step) % teams) * group + seat for step in range(1, teams)]
    for partner in partners:
        pl.semaphore_signal(barrier, inc=1, device_id=(row, partner), device_id_type=MESH)
    pl.semaphore_wait(barrier, len(partners))

    own = pltpu.make_async_copy(element_ref, pieces.at[mine], local_sem.at[0])
    own.start()

    def mate_copy(step, source_seat, target_seat):
        return pltpu.make_async_remote_copy(
            src_ref=element_ref,
            dst_ref=pieces.at[team * group + source_seat],
            send_sem=send_sem.at[step],
            recv_sem=recv_sem.at[source_seat],
            device_id=(row, team * group + target_seat),
            device_id_type=MESH,
        )

    def team_copy(step, source_team, target_team):
        block = pieces.at[pl.ds(source_team * group, group)]
        return pltpu.make_async_remote_copy(
            src_ref=block,
            dst_ref=block,
            send_sem=send_sem.at[group + step],
            recv_sem=recv_sem.at[group + source_team],
            device_id=(row, target_team * group + seat),
            device_id_type=MESH,
        )

    for step in range(1, group):
        mate_copy(step, seat, (seat + step) % group).start()
    for step in range(1, group):
        mate_copy(step, (seat + group - step) % group, seat).wait_recv()
    own.wait()
    for step in range(1, teams):
        team_copy(step, team, (team + step) % teams).start()
    for step in range(1, teams):
        team_copy(step, (team + teams - step) % teams, team).wait_recv()

    def turn(position, total):
        piece = pieces[position]
        entries = [
            piece[2 * i : 2 * i + 1] * total[j] + piece[2 * i + 1 : 2 * i + 2] * total[2 + j]
            for i in range(2)
            for j in range(2)
        ]
        big = jnp.maximum(
            jnp.maximum(jnp.abs(entries[0]), jnp.abs(entries[1])),
            jnp.maximum(jnp.abs(entries[2]), jnp.abs(entries[3])),
        )
        inside = position < mine
        return tuple(jnp.where(inside, value / big, old) for value, old in zip(entries, total))

    unit = jnp.ones((1, 128), jnp.float32)
    blank = jnp.zeros((1, 128), jnp.float32)
    total = lax.fori_loop(0, count - 1, turn, (unit, blank, blank, unit))
    modified_prev = total[1] / total[3]
    weight = unit
    for i in range(rows_here):
        lower = table_ref[i : i + 1]
        upper = table_ref[16 + i : 17 + i]
        diagonal = table_ref[32 + i : 33 + i]
        pivot = diagonal - lower * modified_prev
        modified_prev = upper / pivot
        weight = -lower / pivot * weight
        out_ref[i : i + 1] = pivot
        out_ref[16 + i : 17 + i] = modified_prev
        out_ref[32 + i : 33 + i] = weight
    for step in range(1, group):
        mate_copy(step, seat, (seat + step) % group).wait_send()
    for step in range(1, teams):
        team_copy(step, team, (team + step) % teams).wait_send()


def team_size(count):
    if count > 16 and count % 16 == 0:
        return 16
    return max(1, count // 2)


def matrix_kernel(rows_here, table_ref, out_ref):
    unit = jnp.ones((1, 128), jnp.float32)
    blank = jnp.zeros((1, 128), jnp.float32)
    top = (unit, blank)
    bottom = (blank, unit)
    for i in range(rows_here):
        scale = 1.0 / table_ref[32 + i : 33 + i]
        up = table_ref[16 + i : 17 + i] * scale
        low = -table_ref[i : i + 1] * scale
        top, bottom = (
            (up * bottom[0], up * bottom[1]),
            (low * top[0] + bottom[0], low * top[1] + bottom[1]),
        )
    big = jnp.maximum(
        jnp.maximum(jnp.abs(top[0]), jnp.abs(top[1])), jnp.maximum(jnp.abs(bottom[0]), jnp.abs(bottom[1]))
    )
    out_ref[...] = jnp.concatenate(
        [top[0] / big, top[1] / big, bottom[0] / big, bottom[1] / big, blank, blank, blank, blank], axis=0
    )


def coefficient_table(lower_coef, upper_coef, diagonal):
    count = lax.axis_size("gy")
    rows_here = lower_coef.shape[0]
    filler = jnp.zeros((16 - rows_here,), jnp.float32)
    column = jnp.concatenate([lower_coef, filler, upper_coef, filler, diagonal, filler])
    table = jnp.broadcast_to(column.reshape(48, 1), (48, 128))
    element = pl.pallas_call(
        functools.partial(matrix_kernel, rows_here),
        out_shape=jax.ShapeDtypeStruct((8, 128), jnp.float32),
        in_specs=[pl.BlockSpec(memory_space=pltpu.VMEM)],
        out_specs=pl.BlockSpec(memory_space=pltpu.VMEM),
    )(table)
    return table, pl.pallas_call(
        functools.partial(prefix_kernel, count, team_size(count), rows_here),
        out_shape=jax.ShapeDtypeStruct((48, 128), jnp.float32),
        in_specs=[pl.BlockSpec(memory_space=pltpu.VMEM)] * 2,
        out_specs=pl.BlockSpec(memory_space=pltpu.VMEM),
        scratch_shapes=[
            pltpu.VMEM((count, 8, 128), jnp.float32),
            pltpu.SemaphoreType.DMA((team_size(count) + count // team_size(count),)),
            pltpu.SemaphoreType.DMA((team_size(count) + count // team_size(count),)),
            pltpu.SemaphoreType.DMA((1,)),
        ],
        compiler_params=pltpu.CompilerParams(collective_id=1, has_side_effects=True),
    )(element, table)


def stream_slope(padded, planes):
    summed = STENCIL[0] * (padded[..., 5 : 5 + planes] - padded[..., 3 : 3 + planes])
    for offset in range(2, 5):
        summed = summed + STENCIL[offset - 1] * (
            padded[..., 4 + offset : 4 + offset + planes]
            - padded[..., 4 - offset : 4 - offset + planes]
        )
    return summed


def roll_slope(values, along_axis):
    summed = STENCIL[0] * (jnp.roll(values, -1, along_axis) - jnp.roll(values, 1, along_axis))
    for offset in range(2, 5):
        summed = summed + STENCIL[offset - 1] * (
            jnp.roll(values, -offset, along_axis) - jnp.roll(values, offset, along_axis)
        )
    return summed


def compose(earlier, latter):
    return (latter[0] * earlier[0], latter[1] + latter[0] * earlier[1])


def chain_ratio(earlier, latter):
    product = jnp.dot(latter, earlier, precision=lax.Precision.HIGHEST)
    return product / jnp.max(jnp.abs(product))


def ratio_matrix(cross_term, top_right, bottom_left):
    unit_entry = jnp.ones((), jnp.float32)
    return jnp.stack([jnp.stack([cross_term, top_right]), jnp.stack([bottom_left, unit_entry])])


def radix_plan(count):
    plan = [list(range(1, min(8, count - 1) + 1))]
    span = len(plan[0])
    while span < count - 1:
        offsets = [span * j for j in range(1, 8) if span * j < count]
        plan.append(offsets)
        span = span * (1 + len(offsets))
    return plan


def radix_scan(me, row, count, backward, element, parts, recv, send_sem, recv_sem, base, copies):
    sign = -1 if backward else 1
    plan = radix_plan(count)
    slot = base
    for level, offsets in enumerate(plan):
        source = element if level == 0 else parts.at[level - 1]
        started = []
        for offset in offsets:
            target = (me + count + sign * offset) % count
            copy = pltpu.make_async_remote_copy(
                src_ref=source,
                dst_ref=recv.at[slot],
                send_sem=send_sem.at[slot],
                recv_sem=recv_sem.at[slot],
                device_id=(row, target),
                device_id_type=MESH,
            )
            copy.start()
            started.append((offset, slot, copy))
            slot += 1
        acc = line_neutral() if level == 0 else parts[level - 1]
        for offset, index, copy in started:
            copy.wait_recv()
            copies.append(copy)
            valid = (me + offset <= count - 1) if backward else (me >= offset)
            acc = jnp.where(valid, line_join(recv[index], acc), acc)
        parts[level] = acc
    return parts[len(plan) - 1]


def carry_kernel(count, rows_here, rows_ref, given_ref, coef_ref, out_ref, down_element, parts_down, up_element,
                 parts_up, recv, send_sem, recv_sem):
    me = lax.axis_index("gy")
    row = lax.axis_index("gx")
    plan = radix_plan(count)
    residues = set()
    for offsets in plan:
        for offset in offsets:
            residues.add(offset % count)
            residues.add((count - offset) % count)
    residues.discard(0)
    barrier = pltpu.get_barrier_semaphore()
    for residue in sorted(residues):
        pl.semaphore_signal(barrier, inc=1, device_id=(row, (me + residue) % count), device_id_type=MESH)
    pl.semaphore_wait(barrier, len(residues))
    copies = []
    slots = sum(len(offsets) for offsets in plan)

    coef = coef_ref[...]
    given = given_ref[...]
    carried = None
    for i in range(rows_here):
        lower = given[i : i + 1]
        pivot = coef[i : i + 1]
        carried = rows_ref[i] / pivot if carried is None else (rows_ref[i] - lower * carried) / pivot
        out_ref[i] = carried
    down_element[...] = jnp.concatenate(
        [carried, jnp.broadcast_to(coef[32 + rows_here - 1 : 32 + rows_here], (8, 128))], axis=0
    )
    below_carry = radix_scan(
        me, row, count, False, down_element, parts_down, recv, send_sem, recv_sem, 0, copies
    )[:LINES]
    carried = None
    weight = None
    for i in reversed(range(rows_here)):
        sensitivity = coef[32 + i : 33 + i]
        modified = coef[16 + i : 17 + i]
        reduced = out_ref[i] + sensitivity * below_carry
        if carried is None:
            carried = reduced
            weight = -modified
        else:
            carried = reduced - modified * carried
            weight = -modified * weight
        out_ref[i] = carried
    up_element[...] = jnp.concatenate([carried, jnp.broadcast_to(weight, (8, 128))], axis=0)
    above_carry = radix_scan(
        me, row, count, True, up_element, parts_up, recv, send_sem, recv_sem, slots, copies
    )[:LINES]
    weight = None
    for i in reversed(range(rows_here)):
        modified = coef[16 + i : 17 + i]
        weight = -modified if weight is None else -modified * weight
        out_ref[i] = out_ref[i] + weight * above_carry
    for copy in copies:
        copy.wait_send()


def carry_solve(stacked, given, coef):
    count = lax.axis_size("gy")
    rows_here = stacked.shape[0]
    plan = radix_plan(count)
    slots = 2 * sum(len(offsets) for offsets in plan)
    big = (LINES + 8, 128)
    return pl.pallas_call(
        functools.partial(carry_kernel, count, rows_here),
        out_shape=jax.ShapeDtypeStruct((rows_here, LINES, 128), jnp.float32),
        in_specs=[pl.BlockSpec(memory_space=pltpu.VMEM)] * 3,
        out_specs=pl.BlockSpec(memory_space=pltpu.VMEM),
        scratch_shapes=[
            pltpu.VMEM(big, jnp.float32),
            pltpu.VMEM((len(plan),) + big, jnp.float32),
            pltpu.VMEM(big, jnp.float32),
            pltpu.VMEM((len(plan),) + big, jnp.float32),
            pltpu.VMEM((slots,) + big, jnp.float32),
            pltpu.SemaphoreType.DMA((slots,)),
            pltpu.SemaphoreType.DMA((slots,)),
        ],
        compiler_params=pltpu.CompilerParams(collective_id=0, has_side_effects=True),
    )(stacked, given, coef)


def shards(velocity, old_advection, lower_gap, upper_gap):
    planes = velocity.shape[3]
    padded = extended(velocity, (("gx", 3),), 4, True)
    stream = stream_slope(padded, planes)
    spanwise = roll_slope(velocity, 2)
    rimmed = extended(velocity, (("gy", 1),), 1, False)
    gap_sum = lower_gap + upper_gap
    normal_slope = (rimmed[:, 2:] - rimmed[:, :-2]) / gap_sum[None, :, None, None]
    advection = -(
        velocity[0][None] * stream + velocity[1][None] * normal_slope + velocity[2][None] * spanwise
    )
    forcing = velocity + GAMMA * advection + ZETA * old_advection
    lower_coef = -2.0 * STIFF / (gap_sum * lower_gap)
    upper_coef = -2.0 * STIFF / (gap_sum * upper_gap)
    diagonal = 1.0 - lower_coef - upper_coef
    rows_here = velocity.shape[1]

    given, table = coefficient_table(lower_coef, upper_coef, diagonal)
    stacked = jnp.transpose(forcing, (1, 0, 2, 3)).reshape(rows_here, LINES, 128)
    solved = carry_solve(stacked, given, table)
    finished = jnp.transpose(solved.reshape(rows_here, 3, 32, -1), (1, 0, 2, 3))
    return (finished.reshape(velocity.shape), advection)


def solution(mesh):
    return jax.shard_map(
        shards,
        mesh=mesh,
        in_specs=(P(None, "gy", None, "gx"), P(None, "gy", None, "gx"), P("gy"), P("gy")),
        out_specs=(P(None, "gy", None, "gx"), P(None, "gy", None, "gx")),
        check_vma=False,
    )
```

```python
import functools

import jax
import jax.numpy as jnp
from jax import lax
from jax.sharding import PartitionSpec as P
from jax.experimental import pallas as pl
from jax.experimental.pallas import tpu as pltpu

MESH = pl.DeviceIdType.MESH
LINES = 96

STIFF = 1024


STENCIL = (0.8, -0.2, 4.0 / 105.0, -1.0 / 280.0)
GAMMA = 5.0 / 12.0
ZETA = -17.0 / 60.0


def extended(array, sides, width, wrap):
    for axis, dim in sides:
        size, length = (lax.axis_size(axis), array.shape[dim])
        up = [(i, (i + 1) % size) for i in range(size if wrap else size - 1)]
        down = [(j, i) for i, j in up]
        last = lax.slice_in_dim(array, length - width, length, axis=dim)
        first = lax.slice_in_dim(array, 0, width, axis=dim)
        before = lax.ppermute(last, axis, up)
        after = lax.ppermute(first, axis, down)
        array = jnp.concatenate([before, array, after], axis=dim)
    return array


def prefix(value, axis, join, neutral, backward):
    count, mine = (lax.axis_size(axis), lax.axis_index(axis))
    step = -1 if backward else 1
    order = [(i, i + step) for i in range(count) if 0 <= i + step < count]
    total = jax.tree.map(lambda part: lax.ppermute(part, axis, order), value)
    inside = (mine >= 1) if not backward else (mine <= count - 2)
    total = jax.tree.map(
        lambda part, zero: jnp.where(inside, part, jnp.full_like(part, 0) + jnp.asarray(zero, part.dtype)),
        total,
        neutral,
    )
    offset = 1
    while offset < count:
        pairs = [(i, i + step * offset) for i in range(count) if 0 <= i + step * offset < count]
        earlier = jax.tree.map(lambda part: lax.ppermute(part, axis, pairs), total)
        longer = join(earlier, total)
        reach = (mine >= offset) if not backward else (mine <= count - 1 - offset)
        total = jax.tree.map(lambda new, old: jnp.where(reach, new, old), longer, total)
        offset *= 2
    return total


def ratio_join(earlier, latter):
    def entry(i, j):
        return latter[2 * i : 2 * i + 1] * earlier[j : j + 1] + latter[2 * i + 1 : 2 * i + 2] * earlier[2 + j : 3 + j]

    entries = [entry(0, 0), entry(0, 1), entry(1, 0), entry(1, 1)]
    big = jnp.maximum(
        jnp.maximum(jnp.abs(entries[0]), jnp.abs(entries[1])),
        jnp.maximum(jnp.abs(entries[2]), jnp.abs(entries[3])),
    )
    rows = [part / big for part in entries]
    return jnp.concatenate(rows + [jnp.zeros((4, 128), jnp.float32)], axis=0)


def line_join(earlier, latter):
    factor = latter[LINES : LINES + 1, :]
    joined_lines = latter[:LINES] + factor * earlier[:LINES]
    joined_scale = latter[LINES:] * earlier[LINES:]
    return jnp.concatenate([joined_lines, joined_scale], axis=0)


def ratio_neutral():
    unit = jnp.ones((1, 128), jnp.float32)
    blank = jnp.zeros((1, 128), jnp.float32)
    return jnp.concatenate([unit, blank, blank, unit, blank, blank, blank, blank], axis=0)


def line_neutral():
    return jnp.concatenate([jnp.zeros((LINES, 128), jnp.float32), jnp.ones((8, 128), jnp.float32)], axis=0)


def scan_kernel(count, backward, join, neutral, x_ref, out_ref, totals, recv, send_sem, recv_sem):
    me = lax.axis_index("gy")
    row = lax.axis_index("gx")
    sign = -1 if backward else 1
    offsets = [1]
    while offsets[-1] * 2 < count:
        offsets.append(offsets[-1] * 2)
    partners = []
    for offset in offsets:
        partners.append((me + offset) % count)
        if 2 * offset != count:
            partners.append((me + count - offset) % count)
    barrier = pltpu.get_barrier_semaphore()
    for partner in partners:
        pl.semaphore_signal(barrier, inc=1, device_id=(row, partner), device_id_type=MESH)
    pl.semaphore_wait(barrier, len(partners))
    rounds = [1] + offsets
    copies = []
    for step, offset in enumerate(rounds):
        source = x_ref if step == 0 else totals.at[step - 1]
        target = (me + count + sign * offset) % count
        copy = pltpu.make_async_remote_copy(
            src_ref=source,
            dst_ref=recv.at[step],
            send_sem=send_sem.at[step],
            recv_sem=recv_sem.at[step],
            device_id=(row, target),
            device_id_type=MESH,
        )
        copy.start()
        copy.wait_recv()
        copies.append(copy)
        valid = (me + offset <= count - 1) if backward else (me >= offset)
        earlier = recv[step]
        if step == 0:
            totals[step] = jnp.where(valid, earlier, neutral())
        else:
            latter = totals[step - 1]
            totals[step] = jnp.where(valid, join(earlier, latter), latter)
    out_ref[...] = totals[len(rounds) - 1]
    for copy in copies:
        copy.wait_send()


def line_scan(step_value, backward):
    count = lax.axis_size("gy")
    factor, lines = step_value
    shape = lines.shape
    packed = jnp.concatenate(
        [lines.reshape(LINES, 128), jnp.broadcast_to(factor.reshape(1, 1), (8, 128))], axis=0
    )
    rounds = 1
    while (1 << (rounds - 1)) * 2 < count:
        rounds += 1
    rounds += 1
    result = pl.pallas_call(
        functools.partial(scan_kernel, count, backward, line_join, line_neutral),
        out_shape=jax.ShapeDtypeStruct(packed.shape, jnp.float32),
        in_specs=[pl.BlockSpec(memory_space=pltpu.VMEM)],
        out_specs=pl.BlockSpec(memory_space=pltpu.VMEM),
        scratch_shapes=[
            pltpu.VMEM((rounds,) + packed.shape, jnp.float32),
            pltpu.VMEM((rounds,) + packed.shape, jnp.float32),
            pltpu.SemaphoreType.DMA((rounds,)),
            pltpu.SemaphoreType.DMA((rounds,)),
        ],
        compiler_params=pltpu.CompilerParams(collective_id=1 if backward else 0, has_side_effects=True),
    )(packed)
    return result[:LINES].reshape(shape)


def ratio_scan(matrix):
    count = lax.axis_size("gy")
    packed = jnp.concatenate(
        [jnp.broadcast_to(matrix.reshape(4, 1), (4, 128)), jnp.zeros((4, 128), jnp.float32)], axis=0
    )
    rounds = 1
    while (1 << (rounds - 1)) * 2 < count:
        rounds += 1
    rounds += 1
    result = pl.pallas_call(
        functools.partial(scan_kernel, count, False, ratio_join, ratio_neutral),
        out_shape=jax.ShapeDtypeStruct(packed.shape, jnp.float32),
        in_specs=[pl.BlockSpec(memory_space=pltpu.VMEM)],
        out_specs=pl.BlockSpec(memory_space=pltpu.VMEM),
        scratch_shapes=[
            pltpu.VMEM((rounds,) + packed.shape, jnp.float32),
            pltpu.VMEM((rounds,) + packed.shape, jnp.float32),
            pltpu.SemaphoreType.DMA((rounds,)),
            pltpu.SemaphoreType.DMA((rounds,)),
        ],
        compiler_params=pltpu.CompilerParams(collective_id=2, has_side_effects=True),
    )(packed)
    return result[:4, 0].reshape(2, 2)


def prefix_kernel(count, group, rows_here, element_ref, table_ref, out_ref, pieces, send_sem, recv_sem, local_sem):
    mine = lax.axis_index("gy")
    row = lax.axis_index("gx")
    teams = count // group
    team = mine // group
    seat = mine % group
    barrier = pltpu.get_barrier_semaphore()
    partners = [team * group + (seat + step) % group for step in range(1, group)]
    partners += [((team + step) % teams) * group + seat for step in range(1, teams)]
    for partner in partners:
        pl.semaphore_signal(barrier, inc=1, device_id=(row, partner), device_id_type=MESH)
    pl.semaphore_wait(barrier, len(partners))

    own = pltpu.make_async_copy(element_ref, pieces.at[mine], local_sem.at[0])
    own.start()

    def mate_copy(step, source_seat, target_seat):
        return pltpu.make_async_remote_copy(
            src_ref=element_ref,
            dst_ref=pieces.at[team * group + source_seat],
            send_sem=send_sem.at[step],
            recv_sem=recv_sem.at[source_seat],
            device_id=(row, team * group + target_seat),
            device_id_type=MESH,
        )

    def team_copy(step, source_team, target_team):
        block = pieces.at[pl.ds(source_team * group, group)]
        return pltpu.make_async_remote_copy(
            src_ref=block,
            dst_ref=block,
            send_sem=send_sem.at[group + step],
            recv_sem=recv_sem.at[group + source_team],
            device_id=(row, target_team * group + seat),
            device_id_type=MESH,
        )

    for step in range(1, group):
        mate_copy(step, seat, (seat + step) % group).start()
    for step in range(1, group):
        mate_copy(step, (seat + group - step) % group, seat).wait_recv()
    own.wait()
    for step in range(1, teams):
        team_copy(step, team, (team + step) % teams).start()
    for step in range(1, teams):
        team_copy(step, (team + teams - step) % teams, team).wait_recv()

    def turn(position, total):
        piece = pieces[position]
        entries = [
            piece[2 * i : 2 * i + 1] * total[j] + piece[2 * i + 1 : 2 * i + 2] * total[2 + j]
            for i in range(2)
            for j in range(2)
        ]
        big = jnp.maximum(
            jnp.maximum(jnp.abs(entries[0]), jnp.abs(entries[1])),
            jnp.maximum(jnp.abs(entries[2]), jnp.abs(entries[3])),
        )
        inside = position < mine
        return tuple(jnp.where(inside, value / big, old) for value, old in zip(entries, total))

    unit = jnp.ones((1, 128), jnp.float32)
    blank = jnp.zeros((1, 128), jnp.float32)
    total = lax.fori_loop(0, count - 1, turn, (unit, blank, blank, unit))
    modified_prev = total[1] / total[3]
    weight = unit
    for i in range(rows_here):
        lower = table_ref[i : i + 1]
        upper = table_ref[16 + i : 17 + i]
        diagonal = table_ref[32 + i : 33 + i]
        pivot = diagonal - lower * modified_prev
        modified_prev = upper / pivot
        weight = -lower / pivot * weight
        out_ref[i : i + 1] = pivot
        out_ref[16 + i : 17 + i] = modified_prev
        out_ref[32 + i : 33 + i] = weight
    for step in range(1, group):
        mate_copy(step, seat, (seat + step) % group).wait_send()
    for step in range(1, teams):
        team_copy(step, team, (team + step) % teams).wait_send()


def team_size(count):
    if count > 16 and count % 16 == 0:
        return 16
    return max(1, count // 2)


def matrix_kernel(rows_here, table_ref, out_ref):
    unit = jnp.ones((1, 128), jnp.float32)
    blank = jnp.zeros((1, 128), jnp.float32)
    top = (unit, blank)
    bottom = (blank, unit)
    for i in range(rows_here):
        scale = 1.0 / table_ref[32 + i : 33 + i]
        up = table_ref[16 + i : 17 + i] * scale
        low = -table_ref[i : i + 1] * scale
        top, bottom = (
            (up * bottom[0], up * bottom[1]),
            (low * top[0] + bottom[0], low * top[1] + bottom[1]),
        )
    big = jnp.maximum(
        jnp.maximum(jnp.abs(top[0]), jnp.abs(top[1])), jnp.maximum(jnp.abs(bottom[0]), jnp.abs(bottom[1]))
    )
    out_ref[...] = jnp.concatenate(
        [top[0] / big, top[1] / big, bottom[0] / big, bottom[1] / big, blank, blank, blank, blank], axis=0
    )


def coefficient_table(lower_coef, upper_coef, diagonal):
    count = lax.axis_size("gy")
    rows_here = lower_coef.shape[0]
    filler = jnp.zeros((16 - rows_here,), jnp.float32)
    column = jnp.concatenate([lower_coef, filler, upper_coef, filler, diagonal, filler])
    table = jnp.broadcast_to(column.reshape(48, 1), (48, 128))
    element = pl.pallas_call(
        functools.partial(matrix_kernel, rows_here),
        out_shape=jax.ShapeDtypeStruct((8, 128), jnp.float32),
        in_specs=[pl.BlockSpec(memory_space=pltpu.VMEM)],
        out_specs=pl.BlockSpec(memory_space=pltpu.VMEM),
    )(table)
    return table, pl.pallas_call(
        functools.partial(prefix_kernel, count, team_size(count), rows_here),
        out_shape=jax.ShapeDtypeStruct((48, 128), jnp.float32),
        in_specs=[pl.BlockSpec(memory_space=pltpu.VMEM)] * 2,
        out_specs=pl.BlockSpec(memory_space=pltpu.VMEM),
        scratch_shapes=[
            pltpu.VMEM((count, 8, 128), jnp.float32),
            pltpu.SemaphoreType.DMA((team_size(count) + count // team_size(count),)),
            pltpu.SemaphoreType.DMA((team_size(count) + count // team_size(count),)),
            pltpu.SemaphoreType.DMA((1,)),
        ],
        compiler_params=pltpu.CompilerParams(collective_id=1, has_side_effects=True),
    )(element, table)


def stream_slope(padded, planes):
    summed = STENCIL[0] * (padded[..., 5 : 5 + planes] - padded[..., 3 : 3 + planes])
    for offset in range(2, 5):
        summed = summed + STENCIL[offset - 1] * (
            padded[..., 4 + offset : 4 + offset + planes]
            - padded[..., 4 - offset : 4 - offset + planes]
        )
    return summed


def roll_slope(values, along_axis):
    summed = STENCIL[0] * (jnp.roll(values, -1, along_axis) - jnp.roll(values, 1, along_axis))
    for offset in range(2, 5):
        summed = summed + STENCIL[offset - 1] * (
            jnp.roll(values, -offset, along_axis) - jnp.roll(values, offset, along_axis)
        )
    return summed


def compose(earlier, latter):
    return (latter[0] * earlier[0], latter[1] + latter[0] * earlier[1])


def chain_ratio(earlier, latter):
    product = jnp.dot(latter, earlier, precision=lax.Precision.HIGHEST)
    return product / jnp.max(jnp.abs(product))


def ratio_matrix(cross_term, top_right, bottom_left):
    unit_entry = jnp.ones((), jnp.float32)
    return jnp.stack([jnp.stack([cross_term, top_right]), jnp.stack([bottom_left, unit_entry])])


def radix_plan(count):
    plan = [list(range(1, min(4, count - 1) + 1))]
    span = len(plan[0])
    while span < count - 1:
        offsets = [span * j for j in range(1, 4) if span * j < count]
        plan.append(offsets)
        span = span * (1 + len(offsets))
    return plan


def radix_scan(me, row, count, backward, element, parts, recv, send_sem, recv_sem, base, copies):
    sign = -1 if backward else 1
    plan = radix_plan(count)
    slot = base
    for level, offsets in enumerate(plan):
        source = element if level == 0 else parts.at[level - 1]
        started = []
        for offset in offsets:
            target = (me + count + sign * offset) % count
            copy = pltpu.make_async_remote_copy(
                src_ref=source,
                dst_ref=recv.at[slot],
                send_sem=send_sem.at[slot],
                recv_sem=recv_sem.at[slot],
                device_id=(row, target),
                device_id_type=MESH,
            )
            copy.start()
            started.append((offset, slot, copy))
            slot += 1
        acc = line_neutral() if level == 0 else parts[level - 1]
        for offset, index, copy in started:
            copy.wait_recv()
            copies.append(copy)
            valid = (me + offset <= count - 1) if backward else (me >= offset)
            acc = jnp.where(valid, line_join(recv[index], acc), acc)
        parts[level] = acc
    return parts[len(plan) - 1]


def carry_kernel(count, rows_here, rows_ref, given_ref, coef_ref, out_ref, down_element, parts_down, up_element,
                 parts_up, recv, send_sem, recv_sem):
    me = lax.axis_index("gy")
    row = lax.axis_index("gx")
    plan = radix_plan(count)
    residues = set()
    for offsets in plan:
        for offset in offsets:
            residues.add(offset % count)
            residues.add((count - offset) % count)
    residues.discard(0)
    barrier = pltpu.get_barrier_semaphore()
    for residue in sorted(residues):
        pl.semaphore_signal(barrier, inc=1, device_id=(row, (me + residue) % count), device_id_type=MESH)
    pl.semaphore_wait(barrier, len(residues))
    copies = []
    slots = sum(len(offsets) for offsets in plan)

    coef = coef_ref[...]
    given = given_ref[...]
    carried = None
    for i in range(rows_here):
        lower = given[i : i + 1]
        pivot = coef[i : i + 1]
        line = rows_ref[:, i].reshape(LINES, 128)
        carried = line / pivot if carried is None else (line - lower * carried) / pivot
        out_ref[:, i] = carried.reshape(out_ref.shape[0], out_ref.shape[2], 128)
    down_element[...] = jnp.concatenate(
        [carried, jnp.broadcast_to(coef[32 + rows_here - 1 : 32 + rows_here], (8, 128))], axis=0
    )
    below_carry = radix_scan(
        me, row, count, False, down_element, parts_down, recv, send_sem, recv_sem, 0, copies
    )[:LINES]
    carried = None
    weight = None
    for i in reversed(range(rows_here)):
        sensitivity = coef[32 + i : 33 + i]
        modified = coef[16 + i : 17 + i]
        reduced = out_ref[:, i].reshape(LINES, 128) + sensitivity * below_carry
        if carried is None:
            carried = reduced
            weight = -modified
        else:
            carried = reduced - modified * carried
            weight = -modified * weight
        out_ref[:, i] = carried.reshape(out_ref.shape[0], out_ref.shape[2], 128)
    up_element[...] = jnp.concatenate([carried, jnp.broadcast_to(weight, (8, 128))], axis=0)
    above_carry = radix_scan(
        me, row, count, True, up_element, parts_up, recv, send_sem, recv_sem, slots, copies
    )[:LINES]
    weight = None
    for i in reversed(range(rows_here)):
        modified = coef[16 + i : 17 + i]
        weight = -modified if weight is None else -modified * weight
        value = out_ref[:, i].reshape(LINES, 128) + weight * above_carry
        out_ref[:, i] = value.reshape(out_ref.shape[0], out_ref.shape[2], 128)
    for copy in copies:
        copy.wait_send()


def carry_solve(stacked, given, coef):
    count = lax.axis_size("gy")
    rows_here = stacked.shape[1]
    plan = radix_plan(count)
    slots = 2 * sum(len(offsets) for offsets in plan)
    big = (LINES + 8, 128)
    return pl.pallas_call(
        functools.partial(carry_kernel, count, rows_here),
        out_shape=jax.ShapeDtypeStruct(stacked.shape, jnp.float32),
        in_specs=[pl.BlockSpec(memory_space=pltpu.VMEM)] * 3,
        out_specs=pl.BlockSpec(memory_space=pltpu.VMEM),
        scratch_shapes=[
            pltpu.VMEM(big, jnp.float32),
            pltpu.VMEM((len(plan),) + big, jnp.float32),
            pltpu.VMEM(big, jnp.float32),
            pltpu.VMEM((len(plan),) + big, jnp.float32),
            pltpu.VMEM((slots,) + big, jnp.float32),
            pltpu.SemaphoreType.DMA((slots,)),
            pltpu.SemaphoreType.DMA((slots,)),
        ],
        compiler_params=pltpu.CompilerParams(collective_id=0, has_side_effects=True),
    )(stacked, given, coef)


def shards(velocity, old_advection, lower_gap, upper_gap):
    planes = velocity.shape[3]
    padded = extended(velocity, (("gx", 3),), 4, True)
    stream = stream_slope(padded, planes)
    spanwise = roll_slope(velocity, 2)
    rimmed = extended(velocity, (("gy", 1),), 1, False)
    gap_sum = lower_gap + upper_gap
    normal_slope = (rimmed[:, 2:] - rimmed[:, :-2]) / gap_sum[None, :, None, None]
    advection = -(
        velocity[0][None] * stream + velocity[1][None] * normal_slope + velocity[2][None] * spanwise
    )
    forcing = velocity + GAMMA * advection + ZETA * old_advection
    lower_coef = -2.0 * STIFF / (gap_sum * lower_gap)
    upper_coef = -2.0 * STIFF / (gap_sum * upper_gap)
    diagonal = 1.0 - lower_coef - upper_coef
    rows_here = velocity.shape[1]

    given, table = coefficient_table(lower_coef, upper_coef, diagonal)
    finished = carry_solve(forcing, given, table)
    return (finished.reshape(velocity.shape), advection)


def solution(mesh):
    return jax.shard_map(
        shards,
        mesh=mesh,
        in_specs=(P(None, "gy", None, "gx"), P(None, "gy", None, "gx"), P("gy"), P("gy")),
        out_specs=(P(None, "gy", None, "gx"), P(None, "gy", None, "gx")),
        check_vma=False,
    )
```

```python
import functools

import jax
import jax.numpy as jnp
from jax import lax
from jax.sharding import PartitionSpec as P
from jax.experimental import pallas as pl
from jax.experimental.pallas import tpu as pltpu

MESH = pl.DeviceIdType.MESH
LINES = 96

STIFF = 1024


STENCIL = (0.8, -0.2, 4.0 / 105.0, -1.0 / 280.0)
GAMMA = 5.0 / 12.0
ZETA = -17.0 / 60.0


def extended(array, sides, width, wrap):
    for axis, dim in sides:
        size, length = (lax.axis_size(axis), array.shape[dim])
        up = [(i, (i + 1) % size) for i in range(size if wrap else size - 1)]
        down = [(j, i) for i, j in up]
        last = lax.slice_in_dim(array, length - width, length, axis=dim)
        first = lax.slice_in_dim(array, 0, width, axis=dim)
        before = lax.ppermute(last, axis, up)
        after = lax.ppermute(first, axis, down)
        array = jnp.concatenate([before, array, after], axis=dim)
    return array


def prefix(value, axis, join, neutral, backward):
    count, mine = (lax.axis_size(axis), lax.axis_index(axis))
    step = -1 if backward else 1
    order = [(i, i + step) for i in range(count) if 0 <= i + step < count]
    total = jax.tree.map(lambda part: lax.ppermute(part, axis, order), value)
    inside = (mine >= 1) if not backward else (mine <= count - 2)
    total = jax.tree.map(
        lambda part, zero: jnp.where(inside, part, jnp.full_like(part, 0) + jnp.asarray(zero, part.dtype)),
        total,
        neutral,
    )
    offset = 1
    while offset < count:
        pairs = [(i, i + step * offset) for i in range(count) if 0 <= i + step * offset < count]
        earlier = jax.tree.map(lambda part: lax.ppermute(part, axis, pairs), total)
        longer = join(earlier, total)
        reach = (mine >= offset) if not backward else (mine <= count - 1 - offset)
        total = jax.tree.map(lambda new, old: jnp.where(reach, new, old), longer, total)
        offset *= 2
    return total


def ratio_join(earlier, latter):
    def entry(i, j):
        return latter[2 * i : 2 * i + 1] * earlier[j : j + 1] + latter[2 * i + 1 : 2 * i + 2] * earlier[2 + j : 3 + j]

    entries = [entry(0, 0), entry(0, 1), entry(1, 0), entry(1, 1)]
    big = jnp.maximum(
        jnp.maximum(jnp.abs(entries[0]), jnp.abs(entries[1])),
        jnp.maximum(jnp.abs(entries[2]), jnp.abs(entries[3])),
    )
    rows = [part / big for part in entries]
    return jnp.concatenate(rows + [jnp.zeros((4, 128), jnp.float32)], axis=0)


def line_join(earlier, latter):
    factor = latter[LINES : LINES + 1, :]
    joined_lines = latter[:LINES] + factor * earlier[:LINES]
    joined_scale = latter[LINES:] * earlier[LINES:]
    return jnp.concatenate([joined_lines, joined_scale], axis=0)


def ratio_neutral():
    unit = jnp.ones((1, 128), jnp.float32)
    blank = jnp.zeros((1, 128), jnp.float32)
    return jnp.concatenate([unit, blank, blank, unit, blank, blank, blank, blank], axis=0)


def line_neutral():
    return jnp.concatenate([jnp.zeros((LINES, 128), jnp.float32), jnp.ones((8, 128), jnp.float32)], axis=0)


def scan_kernel(count, backward, join, neutral, x_ref, out_ref, totals, recv, send_sem, recv_sem):
    me = lax.axis_index("gy")
    row = lax.axis_index("gx")
    sign = -1 if backward else 1
    offsets = [1]
    while offsets[-1] * 2 < count:
        offsets.append(offsets[-1] * 2)
    partners = []
    for offset in offsets:
        partners.append((me + offset) % count)
        if 2 * offset != count:
            partners.append((me + count - offset) % count)
    barrier = pltpu.get_barrier_semaphore()
    for partner in partners:
        pl.semaphore_signal(barrier, inc=1, device_id=(row, partner), device_id_type=MESH)
    pl.semaphore_wait(barrier, len(partners))
    rounds = [1] + offsets
    copies = []
    for step, offset in enumerate(rounds):
        source = x_ref if step == 0 else totals.at[step - 1]
        target = (me + count + sign * offset) % count
        copy = pltpu.make_async_remote_copy(
            src_ref=source,
            dst_ref=recv.at[step],
            send_sem=send_sem.at[step],
            recv_sem=recv_sem.at[step],
            device_id=(row, target),
            device_id_type=MESH,
        )
        copy.start()
        copy.wait_recv()
        copies.append(copy)
        valid = (me + offset <= count - 1) if backward else (me >= offset)
        earlier = recv[step]
        if step == 0:
            totals[step] = jnp.where(valid, earlier, neutral())
        else:
            latter = totals[step - 1]
            totals[step] = jnp.where(valid, join(earlier, latter), latter)
    out_ref[...] = totals[len(rounds) - 1]
    for copy in copies:
        copy.wait_send()


def line_scan(step_value, backward):
    count = lax.axis_size("gy")
    factor, lines = step_value
    shape = lines.shape
    packed = jnp.concatenate(
        [lines.reshape(LINES, 128), jnp.broadcast_to(factor.reshape(1, 1), (8, 128))], axis=0
    )
    rounds = 1
    while (1 << (rounds - 1)) * 2 < count:
        rounds += 1
    rounds += 1
    result = pl.pallas_call(
        functools.partial(scan_kernel, count, backward, line_join, line_neutral),
        out_shape=jax.ShapeDtypeStruct(packed.shape, jnp.float32),
        in_specs=[pl.BlockSpec(memory_space=pltpu.VMEM)],
        out_specs=pl.BlockSpec(memory_space=pltpu.VMEM),
        scratch_shapes=[
            pltpu.VMEM((rounds,) + packed.shape, jnp.float32),
            pltpu.VMEM((rounds,) + packed.shape, jnp.float32),
            pltpu.SemaphoreType.DMA((rounds,)),
            pltpu.SemaphoreType.DMA((rounds,)),
        ],
        compiler_params=pltpu.CompilerParams(collective_id=1 if backward else 0, has_side_effects=True),
    )(packed)
    return result[:LINES].reshape(shape)


def ratio_scan(matrix):
    count = lax.axis_size("gy")
    packed = jnp.concatenate(
        [jnp.broadcast_to(matrix.reshape(4, 1), (4, 128)), jnp.zeros((4, 128), jnp.float32)], axis=0
    )
    rounds = 1
    while (1 << (rounds - 1)) * 2 < count:
        rounds += 1
    rounds += 1
    result = pl.pallas_call(
        functools.partial(scan_kernel, count, False, ratio_join, ratio_neutral),
        out_shape=jax.ShapeDtypeStruct(packed.shape, jnp.float32),
        in_specs=[pl.BlockSpec(memory_space=pltpu.VMEM)],
        out_specs=pl.BlockSpec(memory_space=pltpu.VMEM),
        scratch_shapes=[
            pltpu.VMEM((rounds,) + packed.shape, jnp.float32),
            pltpu.VMEM((rounds,) + packed.shape, jnp.float32),
            pltpu.SemaphoreType.DMA((rounds,)),
            pltpu.SemaphoreType.DMA((rounds,)),
        ],
        compiler_params=pltpu.CompilerParams(collective_id=2, has_side_effects=True),
    )(packed)
    return result[:4, 0].reshape(2, 2)


def prefix_kernel(count, group, rows_here, element_ref, table_ref, out_ref, pieces, send_sem, recv_sem, local_sem):
    mine = lax.axis_index("gy")
    row = lax.axis_index("gx")
    teams = count // group
    team = mine // group
    seat = mine % group
    barrier = pltpu.get_barrier_semaphore()
    partners = [team * group + (seat + step) % group for step in range(1, group)]
    partners += [((team + step) % teams) * group + seat for step in range(1, teams)]
    for partner in partners:
        pl.semaphore_signal(barrier, inc=1, device_id=(row, partner), device_id_type=MESH)
    pl.semaphore_wait(barrier, len(partners))

    own = pltpu.make_async_copy(element_ref, pieces.at[mine], local_sem.at[0])
    own.start()

    def mate_copy(step, source_seat, target_seat):
        return pltpu.make_async_remote_copy(
            src_ref=element_ref,
            dst_ref=pieces.at[team * group + source_seat],
            send_sem=send_sem.at[step],
            recv_sem=recv_sem.at[source_seat],
            device_id=(row, team * group + target_seat),
            device_id_type=MESH,
        )

    def team_copy(step, source_team, target_team):
        block = pieces.at[pl.ds(source_team * group, group)]
        return pltpu.make_async_remote_copy(
            src_ref=block,
            dst_ref=block,
            send_sem=send_sem.at[group + step],
            recv_sem=recv_sem.at[group + source_team],
            device_id=(row, target_team * group + seat),
            device_id_type=MESH,
        )

    for step in range(1, group):
        mate_copy(step, seat, (seat + step) % group).start()
    for step in range(1, group):
        mate_copy(step, (seat + group - step) % group, seat).wait_recv()
    own.wait()
    for step in range(1, teams):
        team_copy(step, team, (team + step) % teams).start()
    for step in range(1, teams):
        team_copy(step, (team + teams - step) % teams, team).wait_recv()

    def turn(position, total):
        piece = pieces[position]
        entries = [
            piece[2 * i : 2 * i + 1] * total[j] + piece[2 * i + 1 : 2 * i + 2] * total[2 + j]
            for i in range(2)
            for j in range(2)
        ]
        big = jnp.maximum(
            jnp.maximum(jnp.abs(entries[0]), jnp.abs(entries[1])),
            jnp.maximum(jnp.abs(entries[2]), jnp.abs(entries[3])),
        )
        inside = position < mine
        return tuple(jnp.where(inside, value / big, old) for value, old in zip(entries, total))

    unit = jnp.ones((1, 128), jnp.float32)
    blank = jnp.zeros((1, 128), jnp.float32)
    total = lax.fori_loop(0, count - 1, turn, (unit, blank, blank, unit))
    modified_prev = total[1] / total[3]
    weight = unit
    for i in range(rows_here):
        lower = table_ref[i : i + 1]
        upper = table_ref[16 + i : 17 + i]
        diagonal = table_ref[32 + i : 33 + i]
        pivot = diagonal - lower * modified_prev
        modified_prev = upper / pivot
        weight = -lower / pivot * weight
        out_ref[i : i + 1] = pivot
        out_ref[16 + i : 17 + i] = modified_prev
        out_ref[32 + i : 33 + i] = weight
    for step in range(1, group):
        mate_copy(step, seat, (seat + step) % group).wait_send()
    for step in range(1, teams):
        team_copy(step, team, (team + step) % teams).wait_send()


def team_size(count):
    if count > 16 and count % 16 == 0:
        return 16
    return max(1, count // 2)


def matrix_kernel(rows_here, table_ref, out_ref):
    unit = jnp.ones((1, 128), jnp.float32)
    blank = jnp.zeros((1, 128), jnp.float32)
    top = (unit, blank)
    bottom = (blank, unit)
    for i in range(rows_here):
        scale = 1.0 / table_ref[32 + i : 33 + i]
        up = table_ref[16 + i : 17 + i] * scale
        low = -table_ref[i : i + 1] * scale
        top, bottom = (
            (up * bottom[0], up * bottom[1]),
            (low * top[0] + bottom[0], low * top[1] + bottom[1]),
        )
    big = jnp.maximum(
        jnp.maximum(jnp.abs(top[0]), jnp.abs(top[1])), jnp.maximum(jnp.abs(bottom[0]), jnp.abs(bottom[1]))
    )
    out_ref[...] = jnp.concatenate(
        [top[0] / big, top[1] / big, bottom[0] / big, bottom[1] / big, blank, blank, blank, blank], axis=0
    )


def coefficient_table(lower_coef, upper_coef, diagonal):
    count = lax.axis_size("gy")
    rows_here = lower_coef.shape[0]
    filler = jnp.zeros((16 - rows_here,), jnp.float32)
    column = jnp.concatenate([lower_coef, filler, upper_coef, filler, diagonal, filler])
    table = jnp.broadcast_to(column.reshape(48, 1), (48, 128))
    element = pl.pallas_call(
        functools.partial(matrix_kernel, rows_here),
        out_shape=jax.ShapeDtypeStruct((8, 128), jnp.float32),
        in_specs=[pl.BlockSpec(memory_space=pltpu.VMEM)],
        out_specs=pl.BlockSpec(memory_space=pltpu.VMEM),
    )(table)
    return table, pl.pallas_call(
        functools.partial(prefix_kernel, count, team_size(count), rows_here),
        out_shape=jax.ShapeDtypeStruct((48, 128), jnp.float32),
        in_specs=[pl.BlockSpec(memory_space=pltpu.VMEM)] * 2,
        out_specs=pl.BlockSpec(memory_space=pltpu.VMEM),
        scratch_shapes=[
            pltpu.VMEM((count, 8, 128), jnp.float32),
            pltpu.SemaphoreType.DMA((team_size(count) + count // team_size(count),)),
            pltpu.SemaphoreType.DMA((team_size(count) + count // team_size(count),)),
            pltpu.SemaphoreType.DMA((1,)),
        ],
        compiler_params=pltpu.CompilerParams(collective_id=1, has_side_effects=True),
    )(element, table)


def stream_slope(padded, planes):
    summed = STENCIL[0] * (padded[..., 5 : 5 + planes] - padded[..., 3 : 3 + planes])
    for offset in range(2, 5):
        summed = summed + STENCIL[offset - 1] * (
            padded[..., 4 + offset : 4 + offset + planes]
            - padded[..., 4 - offset : 4 - offset + planes]
        )
    return summed


def roll_slope(values, along_axis):
    summed = STENCIL[0] * (jnp.roll(values, -1, along_axis) - jnp.roll(values, 1, along_axis))
    for offset in range(2, 5):
        summed = summed + STENCIL[offset - 1] * (
            jnp.roll(values, -offset, along_axis) - jnp.roll(values, offset, along_axis)
        )
    return summed


def compose(earlier, latter):
    return (latter[0] * earlier[0], latter[1] + latter[0] * earlier[1])


def chain_ratio(earlier, latter):
    product = jnp.dot(latter, earlier, precision=lax.Precision.HIGHEST)
    return product / jnp.max(jnp.abs(product))


def ratio_matrix(cross_term, top_right, bottom_left):
    unit_entry = jnp.ones((), jnp.float32)
    return jnp.stack([jnp.stack([cross_term, top_right]), jnp.stack([bottom_left, unit_entry])])


def radix_plan(count):
    plan = [list(range(1, min(2, count - 1) + 1))]
    span = len(plan[0])
    while span < count - 1:
        offsets = [span * j for j in range(1, 2) if span * j < count]
        plan.append(offsets)
        span = span * (1 + len(offsets))
    return plan


def radix_scan(me, row, count, backward, element, parts, recv, send_sem, recv_sem, base, copies):
    sign = -1 if backward else 1
    plan = radix_plan(count)
    slot = base
    for level, offsets in enumerate(plan):
        source = element if level == 0 else parts.at[level - 1]
        started = []
        for offset in offsets:
            target = (me + count + sign * offset) % count
            copy = pltpu.make_async_remote_copy(
                src_ref=source,
                dst_ref=recv.at[slot],
                send_sem=send_sem.at[slot],
                recv_sem=recv_sem.at[slot],
                device_id=(row, target),
                device_id_type=MESH,
            )
            copy.start()
            started.append((offset, slot, copy))
            slot += 1
        acc = line_neutral() if level == 0 else parts[level - 1]
        for offset, index, copy in started:
            copy.wait_recv()
            copies.append(copy)
            valid = (me + offset <= count - 1) if backward else (me >= offset)
            acc = jnp.where(valid, line_join(recv[index], acc), acc)
        parts[level] = acc
    return parts[len(plan) - 1]


def carry_kernel(count, rows_here, rows_ref, given_ref, coef_ref, out_ref, down_element, parts_down, up_element,
                 parts_up, recv, send_sem, recv_sem):
    me = lax.axis_index("gy")
    row = lax.axis_index("gx")
    plan = radix_plan(count)
    residues = set()
    for offsets in plan:
        for offset in offsets:
            residues.add(offset % count)
            residues.add((count - offset) % count)
    residues.discard(0)
    barrier = pltpu.get_barrier_semaphore()
    for residue in sorted(residues):
        pl.semaphore_signal(barrier, inc=1, device_id=(row, (me + residue) % count), device_id_type=MESH)
    pl.semaphore_wait(barrier, len(residues))
    copies = []
    slots = sum(len(offsets) for offsets in plan)

    coef = coef_ref[...]
    given = given_ref[...]
    carried = None
    for i in range(rows_here):
        lower = given[i : i + 1]
        pivot = coef[i : i + 1]
        line = rows_ref[:, i].reshape(LINES, 128)
        carried = line / pivot if carried is None else (line - lower * carried) / pivot
        out_ref[:, i] = carried.reshape(out_ref.shape[0], out_ref.shape[2], 128)
    down_element[...] = jnp.concatenate(
        [carried, jnp.broadcast_to(coef[32 + rows_here - 1 : 32 + rows_here], (8, 128))], axis=0
    )
    below_carry = radix_scan(
        me, row, count, False, down_element, parts_down, recv, send_sem, recv_sem, 0, copies
    )[:LINES]
    carried = None
    weight = None
    for i in reversed(range(rows_here)):
        sensitivity = coef[32 + i : 33 + i]
        modified = coef[16 + i : 17 + i]
        reduced = out_ref[:, i].reshape(LINES, 128) + sensitivity * below_carry
        if carried is None:
            carried = reduced
            weight = -modified
        else:
            carried = reduced - modified * carried
            weight = -modified * weight
        out_ref[:, i] = carried.reshape(out_ref.shape[0], out_ref.shape[2], 128)
    up_element[...] = jnp.concatenate([carried, jnp.broadcast_to(weight, (8, 128))], axis=0)
    above_carry = radix_scan(
        me, row, count, True, up_element, parts_up, recv, send_sem, recv_sem, slots, copies
    )[:LINES]
    weight = None
    for i in reversed(range(rows_here)):
        modified = coef[16 + i : 17 + i]
        weight = -modified if weight is None else -modified * weight
        value = out_ref[:, i].reshape(LINES, 128) + weight * above_carry
        out_ref[:, i] = value.reshape(out_ref.shape[0], out_ref.shape[2], 128)
    for copy in copies:
        copy.wait_send()


def carry_solve(stacked, given, coef):
    count = lax.axis_size("gy")
    rows_here = stacked.shape[1]
    plan = radix_plan(count)
    slots = 2 * sum(len(offsets) for offsets in plan)
    big = (LINES + 8, 128)
    return pl.pallas_call(
        functools.partial(carry_kernel, count, rows_here),
        out_shape=jax.ShapeDtypeStruct(stacked.shape, jnp.float32),
        in_specs=[pl.BlockSpec(memory_space=pltpu.VMEM)] * 3,
        out_specs=pl.BlockSpec(memory_space=pltpu.VMEM),
        scratch_shapes=[
            pltpu.VMEM(big, jnp.float32),
            pltpu.VMEM((len(plan),) + big, jnp.float32),
            pltpu.VMEM(big, jnp.float32),
            pltpu.VMEM((len(plan),) + big, jnp.float32),
            pltpu.VMEM((slots,) + big, jnp.float32),
            pltpu.SemaphoreType.DMA((slots,)),
            pltpu.SemaphoreType.DMA((slots,)),
        ],
        compiler_params=pltpu.CompilerParams(collective_id=0, has_side_effects=True),
    )(stacked, given, coef)


def shards(velocity, old_advection, lower_gap, upper_gap):
    planes = velocity.shape[3]
    padded = extended(velocity, (("gx", 3),), 4, True)
    stream = stream_slope(padded, planes)
    spanwise = roll_slope(velocity, 2)
    rimmed = extended(velocity, (("gy", 1),), 1, False)
    gap_sum = lower_gap + upper_gap
    normal_slope = (rimmed[:, 2:] - rimmed[:, :-2]) / gap_sum[None, :, None, None]
    advection = -(
        velocity[0][None] * stream + velocity[1][None] * normal_slope + velocity[2][None] * spanwise
    )
    forcing = velocity + GAMMA * advection + ZETA * old_advection
    lower_coef = -2.0 * STIFF / (gap_sum * lower_gap)
    upper_coef = -2.0 * STIFF / (gap_sum * upper_gap)
    diagonal = 1.0 - lower_coef - upper_coef
    rows_here = velocity.shape[1]

    given, table = coefficient_table(lower_coef, upper_coef, diagonal)
    finished = carry_solve(forcing, given, table)
    return (finished.reshape(velocity.shape), advection)


def solution(mesh):
    return jax.shard_map(
        shards,
        mesh=mesh,
        in_specs=(P(None, "gy", None, "gx"), P(None, "gy", None, "gx"), P("gy"), P("gy")),
        out_specs=(P(None, "gy", None, "gx"), P(None, "gy", None, "gx")),
        check_vma=False,
    )
```

```python
import functools

import jax
import jax.numpy as jnp
from jax import lax
from jax.sharding import PartitionSpec as P
from jax.experimental import pallas as pl
from jax.experimental.pallas import tpu as pltpu

MESH = pl.DeviceIdType.MESH
LINES = 96

STIFF = 1024


STENCIL = (0.8, -0.2, 4.0 / 105.0, -1.0 / 280.0)
GAMMA = 5.0 / 12.0
ZETA = -17.0 / 60.0


def extended(array, sides, width, wrap):
    for axis, dim in sides:
        size, length = (lax.axis_size(axis), array.shape[dim])
        up = [(i, (i + 1) % size) for i in range(size if wrap else size - 1)]
        down = [(j, i) for i, j in up]
        last = lax.slice_in_dim(array, length - width, length, axis=dim)
        first = lax.slice_in_dim(array, 0, width, axis=dim)
        before = lax.ppermute(last, axis, up)
        after = lax.ppermute(first, axis, down)
        array = jnp.concatenate([before, array, after], axis=dim)
    return array


def prefix(value, axis, join, neutral, backward):
    count, mine = (lax.axis_size(axis), lax.axis_index(axis))
    step = -1 if backward else 1
    order = [(i, i + step) for i in range(count) if 0 <= i + step < count]
    total = jax.tree.map(lambda part: lax.ppermute(part, axis, order), value)
    inside = (mine >= 1) if not backward else (mine <= count - 2)
    total = jax.tree.map(
        lambda part, zero: jnp.where(inside, part, jnp.full_like(part, 0) + jnp.asarray(zero, part.dtype)),
        total,
        neutral,
    )
    offset = 1
    while offset < count:
        pairs = [(i, i + step * offset) for i in range(count) if 0 <= i + step * offset < count]
        earlier = jax.tree.map(lambda part: lax.ppermute(part, axis, pairs), total)
        longer = join(earlier, total)
        reach = (mine >= offset) if not backward else (mine <= count - 1 - offset)
        total = jax.tree.map(lambda new, old: jnp.where(reach, new, old), longer, total)
        offset *= 2
    return total


def ratio_join(earlier, latter):
    def entry(i, j):
        return latter[2 * i : 2 * i + 1] * earlier[j : j + 1] + latter[2 * i + 1 : 2 * i + 2] * earlier[2 + j : 3 + j]

    entries = [entry(0, 0), entry(0, 1), entry(1, 0), entry(1, 1)]
    big = jnp.maximum(
        jnp.maximum(jnp.abs(entries[0]), jnp.abs(entries[1])),
        jnp.maximum(jnp.abs(entries[2]), jnp.abs(entries[3])),
    )
    rows = [part / big for part in entries]
    return jnp.concatenate(rows + [jnp.zeros((4, 128), jnp.float32)], axis=0)


def line_join(earlier, latter):
    factor = latter[LINES : LINES + 1, :]
    joined_lines = latter[:LINES] + factor * earlier[:LINES]
    joined_scale = latter[LINES:] * earlier[LINES:]
    return jnp.concatenate([joined_lines, joined_scale], axis=0)


def ratio_neutral():
    unit = jnp.ones((1, 128), jnp.float32)
    blank = jnp.zeros((1, 128), jnp.float32)
    return jnp.concatenate([unit, blank, blank, unit, blank, blank, blank, blank], axis=0)


def line_neutral():
    return jnp.concatenate([jnp.zeros((LINES, 128), jnp.float32), jnp.ones((8, 128), jnp.float32)], axis=0)


def scan_kernel(count, backward, join, neutral, x_ref, out_ref, totals, recv, send_sem, recv_sem):
    me = lax.axis_index("gy")
    row = lax.axis_index("gx")
    sign = -1 if backward else 1
    offsets = [1]
    while offsets[-1] * 2 < count:
        offsets.append(offsets[-1] * 2)
    partners = []
    for offset in offsets:
        partners.append((me + offset) % count)
        if 2 * offset != count:
            partners.append((me + count - offset) % count)
    barrier = pltpu.get_barrier_semaphore()
    for partner in partners:
        pl.semaphore_signal(barrier, inc=1, device_id=(row, partner), device_id_type=MESH)
    pl.semaphore_wait(barrier, len(partners))
    rounds = [1] + offsets
    copies = []
    for step, offset in enumerate(rounds):
        source = x_ref if step == 0 else totals.at[step - 1]
        target = (me + count + sign * offset) % count
        copy = pltpu.make_async_remote_copy(
            src_ref=source,
            dst_ref=recv.at[step],
            send_sem=send_sem.at[step],
            recv_sem=recv_sem.at[step],
            device_id=(row, target),
            device_id_type=MESH,
        )
        copy.start()
        copy.wait_recv()
        copies.append(copy)
        valid = (me + offset <= count - 1) if backward else (me >= offset)
        earlier = recv[step]
        if step == 0:
            totals[step] = jnp.where(valid, earlier, neutral())
        else:
            latter = totals[step - 1]
            totals[step] = jnp.where(valid, join(earlier, latter), latter)
    out_ref[...] = totals[len(rounds) - 1]
    for copy in copies:
        copy.wait_send()


def line_scan(step_value, backward):
    count = lax.axis_size("gy")
    factor, lines = step_value
    shape = lines.shape
    packed = jnp.concatenate(
        [lines.reshape(LINES, 128), jnp.broadcast_to(factor.reshape(1, 1), (8, 128))], axis=0
    )
    rounds = 1
    while (1 << (rounds - 1)) * 2 < count:
        rounds += 1
    rounds += 1
    result = pl.pallas_call(
        functools.partial(scan_kernel, count, backward, line_join, line_neutral),
        out_shape=jax.ShapeDtypeStruct(packed.shape, jnp.float32),
        in_specs=[pl.BlockSpec(memory_space=pltpu.VMEM)],
        out_specs=pl.BlockSpec(memory_space=pltpu.VMEM),
        scratch_shapes=[
            pltpu.VMEM((rounds,) + packed.shape, jnp.float32),
            pltpu.VMEM((rounds,) + packed.shape, jnp.float32),
            pltpu.SemaphoreType.DMA((rounds,)),
            pltpu.SemaphoreType.DMA((rounds,)),
        ],
        compiler_params=pltpu.CompilerParams(collective_id=1 if backward else 0, has_side_effects=True),
    )(packed)
    return result[:LINES].reshape(shape)


def ratio_scan(matrix):
    count = lax.axis_size("gy")
    packed = jnp.concatenate(
        [jnp.broadcast_to(matrix.reshape(4, 1), (4, 128)), jnp.zeros((4, 128), jnp.float32)], axis=0
    )
    rounds = 1
    while (1 << (rounds - 1)) * 2 < count:
        rounds += 1
    rounds += 1
    result = pl.pallas_call(
        functools.partial(scan_kernel, count, False, ratio_join, ratio_neutral),
        out_shape=jax.ShapeDtypeStruct(packed.shape, jnp.float32),
        in_specs=[pl.BlockSpec(memory_space=pltpu.VMEM)],
        out_specs=pl.BlockSpec(memory_space=pltpu.VMEM),
        scratch_shapes=[
            pltpu.VMEM((rounds,) + packed.shape, jnp.float32),
            pltpu.VMEM((rounds,) + packed.shape, jnp.float32),
            pltpu.SemaphoreType.DMA((rounds,)),
            pltpu.SemaphoreType.DMA((rounds,)),
        ],
        compiler_params=pltpu.CompilerParams(collective_id=2, has_side_effects=True),
    )(packed)
    return result[:4, 0].reshape(2, 2)


def prefix_kernel(count, group, rows_here, element_ref, table_ref, out_ref, pieces, send_sem, recv_sem, local_sem):
    mine = lax.axis_index("gy")
    row = lax.axis_index("gx")
    teams = count // group
    team = mine // group
    seat = mine % group
    barrier = pltpu.get_barrier_semaphore()
    partners = [team * group + (seat + step) % group for step in range(1, group)]
    partners += [((team + step) % teams) * group + seat for step in range(1, teams)]
    for partner in partners:
        pl.semaphore_signal(barrier, inc=1, device_id=(row, partner), device_id_type=MESH)
    pl.semaphore_wait(barrier, len(partners))

    own = pltpu.make_async_copy(element_ref, pieces.at[mine], local_sem.at[0])
    own.start()

    def mate_copy(step, source_seat, target_seat):
        return pltpu.make_async_remote_copy(
            src_ref=element_ref,
            dst_ref=pieces.at[team * group + source_seat],
            send_sem=send_sem.at[step],
            recv_sem=recv_sem.at[source_seat],
            device_id=(row, team * group + target_seat),
            device_id_type=MESH,
        )

    def team_copy(step, source_team, target_team):
        block = pieces.at[pl.ds(source_team * group, group)]
        return pltpu.make_async_remote_copy(
            src_ref=block,
            dst_ref=block,
            send_sem=send_sem.at[group + step],
            recv_sem=recv_sem.at[group + source_team],
            device_id=(row, target_team * group + seat),
            device_id_type=MESH,
        )

    for step in range(1, group):
        mate_copy(step, seat, (seat + step) % group).start()
    for step in range(1, group):
        mate_copy(step, (seat + group - step) % group, seat).wait_recv()
    own.wait()
    for step in range(1, teams):
        team_copy(step, team, (team + step) % teams).start()
    for step in range(1, teams):
        team_copy(step, (team + teams - step) % teams, team).wait_recv()

    def turn(position, total):
        piece = pieces[position]
        entries = [
            piece[2 * i : 2 * i + 1] * total[j] + piece[2 * i + 1 : 2 * i + 2] * total[2 + j]
            for i in range(2)
            for j in range(2)
        ]
        big = jnp.maximum(
            jnp.maximum(jnp.abs(entries[0]), jnp.abs(entries[1])),
            jnp.maximum(jnp.abs(entries[2]), jnp.abs(entries[3])),
        )
        inside = position < mine
        return tuple(jnp.where(inside, value / big, old) for value, old in zip(entries, total))

    unit = jnp.ones((1, 128), jnp.float32)
    blank = jnp.zeros((1, 128), jnp.float32)
    total = lax.fori_loop(0, count - 1, turn, (unit, blank, blank, unit))
    modified_prev = total[1] / total[3]
    weight = unit
    for i in range(rows_here):
        lower = table_ref[i : i + 1]
        upper = table_ref[16 + i : 17 + i]
        diagonal = table_ref[32 + i : 33 + i]
        pivot = diagonal - lower * modified_prev
        modified_prev = upper / pivot
        weight = -lower / pivot * weight
        out_ref[i : i + 1] = pivot
        out_ref[16 + i : 17 + i] = modified_prev
        out_ref[32 + i : 33 + i] = weight
    for step in range(1, group):
        mate_copy(step, seat, (seat + step) % group).wait_send()
    for step in range(1, teams):
        team_copy(step, team, (team + step) % teams).wait_send()


def team_size(count):
    if count > 32 and count % 32 == 0:
        return 32
    return max(1, count // 2)


def matrix_kernel(rows_here, table_ref, out_ref):
    unit = jnp.ones((1, 128), jnp.float32)
    blank = jnp.zeros((1, 128), jnp.float32)
    top = (unit, blank)
    bottom = (blank, unit)
    for i in range(rows_here):
        scale = 1.0 / table_ref[32 + i : 33 + i]
        up = table_ref[16 + i : 17 + i] * scale
        low = -table_ref[i : i + 1] * scale
        top, bottom = (
            (up * bottom[0], up * bottom[1]),
            (low * top[0] + bottom[0], low * top[1] + bottom[1]),
        )
    big = jnp.maximum(
        jnp.maximum(jnp.abs(top[0]), jnp.abs(top[1])), jnp.maximum(jnp.abs(bottom[0]), jnp.abs(bottom[1]))
    )
    out_ref[...] = jnp.concatenate(
        [top[0] / big, top[1] / big, bottom[0] / big, bottom[1] / big, blank, blank, blank, blank], axis=0
    )


def coefficient_table(lower_coef, upper_coef, diagonal):
    count = lax.axis_size("gy")
    rows_here = lower_coef.shape[0]
    filler = jnp.zeros((16 - rows_here,), jnp.float32)
    column = jnp.concatenate([lower_coef, filler, upper_coef, filler, diagonal, filler])
    table = jnp.broadcast_to(column.reshape(48, 1), (48, 128))
    element = pl.pallas_call(
        functools.partial(matrix_kernel, rows_here),
        out_shape=jax.ShapeDtypeStruct((8, 128), jnp.float32),
        in_specs=[pl.BlockSpec(memory_space=pltpu.VMEM)],
        out_specs=pl.BlockSpec(memory_space=pltpu.VMEM),
    )(table)
    return table, pl.pallas_call(
        functools.partial(prefix_kernel, count, team_size(count), rows_here),
        out_shape=jax.ShapeDtypeStruct((48, 128), jnp.float32),
        in_specs=[pl.BlockSpec(memory_space=pltpu.VMEM)] * 2,
        out_specs=pl.BlockSpec(memory_space=pltpu.VMEM),
        scratch_shapes=[
            pltpu.VMEM((count, 8, 128), jnp.float32),
            pltpu.SemaphoreType.DMA((team_size(count) + count // team_size(count),)),
            pltpu.SemaphoreType.DMA((team_size(count) + count // team_size(count),)),
            pltpu.SemaphoreType.DMA((1,)),
        ],
        compiler_params=pltpu.CompilerParams(collective_id=1, has_side_effects=True),
    )(element, table)


def stream_slope(padded, planes):
    summed = STENCIL[0] * (padded[..., 5 : 5 + planes] - padded[..., 3 : 3 + planes])
    for offset in range(2, 5):
        summed = summed + STENCIL[offset - 1] * (
            padded[..., 4 + offset : 4 + offset + planes]
            - padded[..., 4 - offset : 4 - offset + planes]
        )
    return summed


def roll_slope(values, along_axis):
    summed = STENCIL[0] * (jnp.roll(values, -1, along_axis) - jnp.roll(values, 1, along_axis))
    for offset in range(2, 5):
        summed = summed + STENCIL[offset - 1] * (
            jnp.roll(values, -offset, along_axis) - jnp.roll(values, offset, along_axis)
        )
    return summed


def compose(earlier, latter):
    return (latter[0] * earlier[0], latter[1] + latter[0] * earlier[1])


def chain_ratio(earlier, latter):
    product = jnp.dot(latter, earlier, precision=lax.Precision.HIGHEST)
    return product / jnp.max(jnp.abs(product))


def ratio_matrix(cross_term, top_right, bottom_left):
    unit_entry = jnp.ones((), jnp.float32)
    return jnp.stack([jnp.stack([cross_term, top_right]), jnp.stack([bottom_left, unit_entry])])


def radix_plan(count):
    plan = [list(range(1, min(4, count - 1) + 1))]
    span = len(plan[0])
    while span < count - 1:
        offsets = [span * j for j in range(1, 4) if span * j < count]
        plan.append(offsets)
        span = span * (1 + len(offsets))
    return plan


def radix_scan(me, row, count, backward, element, parts, recv, send_sem, recv_sem, base, copies):
    sign = -1 if backward else 1
    plan = radix_plan(count)
    slot = base
    for level, offsets in enumerate(plan):
        source = element if level == 0 else parts.at[level - 1]
        started = []
        for offset in offsets:
            target = (me + count + sign * offset) % count
            copy = pltpu.make_async_remote_copy(
                src_ref=source,
                dst_ref=recv.at[slot],
                send_sem=send_sem.at[slot],
                recv_sem=recv_sem.at[slot],
                device_id=(row, target),
                device_id_type=MESH,
            )
            copy.start()
            started.append((offset, slot, copy))
            slot += 1
        acc = line_neutral() if level == 0 else parts[level - 1]
        for offset, index, copy in started:
            copy.wait_recv()
            copies.append(copy)
            valid = (me + offset <= count - 1) if backward else (me >= offset)
            acc = jnp.where(valid, line_join(recv[index], acc), acc)
        parts[level] = acc
    return parts[len(plan) - 1]


def carry_kernel(count, rows_here, rows_ref, given_ref, coef_ref, out_ref, down_element, parts_down, up_element,
                 parts_up, recv, send_sem, recv_sem):
    me = lax.axis_index("gy")
    row = lax.axis_index("gx")
    plan = radix_plan(count)
    residues = set()
    for offsets in plan:
        for offset in offsets:
            residues.add(offset % count)
            residues.add((count - offset) % count)
    residues.discard(0)
    barrier = pltpu.get_barrier_semaphore()
    for residue in sorted(residues):
        pl.semaphore_signal(barrier, inc=1, device_id=(row, (me + residue) % count), device_id_type=MESH)
    pl.semaphore_wait(barrier, len(residues))
    copies = []
    slots = sum(len(offsets) for offsets in plan)

    coef = coef_ref[...]
    given = given_ref[...]
    carried = None
    for i in range(rows_here):
        lower = given[i : i + 1]
        pivot = coef[i : i + 1]
        line = rows_ref[:, i].reshape(LINES, 128)
        carried = line / pivot if carried is None else (line - lower * carried) / pivot
        out_ref[:, i] = carried.reshape(out_ref.shape[0], out_ref.shape[2], 128)
    down_element[...] = jnp.concatenate(
        [carried, jnp.broadcast_to(coef[32 + rows_here - 1 : 32 + rows_here], (8, 128))], axis=0
    )
    below_carry = radix_scan(
        me, row, count, False, down_element, parts_down, recv, send_sem, recv_sem, 0, copies
    )[:LINES]
    carried = None
    weight = None
    for i in reversed(range(rows_here)):
        sensitivity = coef[32 + i : 33 + i]
        modified = coef[16 + i : 17 + i]
        reduced = out_ref[:, i].reshape(LINES, 128) + sensitivity * below_carry
        if carried is None:
            carried = reduced
            weight = -modified
        else:
            carried = reduced - modified * carried
            weight = -modified * weight
        out_ref[:, i] = carried.reshape(out_ref.shape[0], out_ref.shape[2], 128)
    up_element[...] = jnp.concatenate([carried, jnp.broadcast_to(weight, (8, 128))], axis=0)
    above_carry = radix_scan(
        me, row, count, True, up_element, parts_up, recv, send_sem, recv_sem, slots, copies
    )[:LINES]
    weight = None
    for i in reversed(range(rows_here)):
        modified = coef[16 + i : 17 + i]
        weight = -modified if weight is None else -modified * weight
        value = out_ref[:, i].reshape(LINES, 128) + weight * above_carry
        out_ref[:, i] = value.reshape(out_ref.shape[0], out_ref.shape[2], 128)
    for copy in copies:
        copy.wait_send()


def carry_solve(stacked, given, coef):
    count = lax.axis_size("gy")
    rows_here = stacked.shape[1]
    plan = radix_plan(count)
    slots = 2 * sum(len(offsets) for offsets in plan)
    big = (LINES + 8, 128)
    return pl.pallas_call(
        functools.partial(carry_kernel, count, rows_here),
        out_shape=jax.ShapeDtypeStruct(stacked.shape, jnp.float32),
        in_specs=[pl.BlockSpec(memory_space=pltpu.VMEM)] * 3,
        out_specs=pl.BlockSpec(memory_space=pltpu.VMEM),
        scratch_shapes=[
            pltpu.VMEM(big, jnp.float32),
            pltpu.VMEM((len(plan),) + big, jnp.float32),
            pltpu.VMEM(big, jnp.float32),
            pltpu.VMEM((len(plan),) + big, jnp.float32),
            pltpu.VMEM((slots,) + big, jnp.float32),
            pltpu.SemaphoreType.DMA((slots,)),
            pltpu.SemaphoreType.DMA((slots,)),
        ],
        compiler_params=pltpu.CompilerParams(collective_id=0, has_side_effects=True),
    )(stacked, given, coef)


def shards(velocity, old_advection, lower_gap, upper_gap):
    planes = velocity.shape[3]
    padded = extended(velocity, (("gx", 3),), 4, True)
    stream = stream_slope(padded, planes)
    spanwise = roll_slope(velocity, 2)
    rimmed = extended(velocity, (("gy", 1),), 1, False)
    gap_sum = lower_gap + upper_gap
    normal_slope = (rimmed[:, 2:] - rimmed[:, :-2]) / gap_sum[None, :, None, None]
    advection = -(
        velocity[0][None] * stream + velocity[1][None] * normal_slope + velocity[2][None] * spanwise
    )
    forcing = velocity + GAMMA * advection + ZETA * old_advection
    lower_coef = -2.0 * STIFF / (gap_sum * lower_gap)
    upper_coef = -2.0 * STIFF / (gap_sum * upper_gap)
    diagonal = 1.0 - lower_coef - upper_coef
    rows_here = velocity.shape[1]

    given, table = coefficient_table(lower_coef, upper_coef, diagonal)
    finished = carry_solve(forcing, given, table)
    return (finished.reshape(velocity.shape), advection)


def solution(mesh):
    return jax.shard_map(
        shards,
        mesh=mesh,
        in_specs=(P(None, "gy", None, "gx"), P(None, "gy", None, "gx"), P("gy"), P("gy")),
        out_specs=(P(None, "gy", None, "gx"), P(None, "gy", None, "gx")),
        check_vma=False,
    )
```

```python
import functools

import jax
import jax.numpy as jnp
from jax import lax
from jax.sharding import PartitionSpec as P
from jax.experimental import pallas as pl
from jax.experimental.pallas import tpu as pltpu

MESH = pl.DeviceIdType.MESH
LINES = 96

STIFF = 1024


STENCIL = (0.8, -0.2, 4.0 / 105.0, -1.0 / 280.0)
GAMMA = 5.0 / 12.0
ZETA = -17.0 / 60.0


def extended(array, sides, width, wrap):
    for axis, dim in sides:
        size, length = (lax.axis_size(axis), array.shape[dim])
        up = [(i, (i + 1) % size) for i in range(size if wrap else size - 1)]
        down = [(j, i) for i, j in up]
        last = lax.slice_in_dim(array, length - width, length, axis=dim)
        first = lax.slice_in_dim(array, 0, width, axis=dim)
        before = lax.ppermute(last, axis, up)
        after = lax.ppermute(first, axis, down)
        array = jnp.concatenate([before, array, after], axis=dim)
    return array


def prefix(value, axis, join, neutral, backward):
    count, mine = (lax.axis_size(axis), lax.axis_index(axis))
    step = -1 if backward else 1
    order = [(i, i + step) for i in range(count) if 0 <= i + step < count]
    total = jax.tree.map(lambda part: lax.ppermute(part, axis, order), value)
    inside = (mine >= 1) if not backward else (mine <= count - 2)
    total = jax.tree.map(
        lambda part, zero: jnp.where(inside, part, jnp.full_like(part, 0) + jnp.asarray(zero, part.dtype)),
        total,
        neutral,
    )
    offset = 1
    while offset < count:
        pairs = [(i, i + step * offset) for i in range(count) if 0 <= i + step * offset < count]
        earlier = jax.tree.map(lambda part: lax.ppermute(part, axis, pairs), total)
        longer = join(earlier, total)
        reach = (mine >= offset) if not backward else (mine <= count - 1 - offset)
        total = jax.tree.map(lambda new, old: jnp.where(reach, new, old), longer, total)
        offset *= 2
    return total


def ratio_join(earlier, latter):
    def entry(i, j):
        return latter[2 * i : 2 * i + 1] * earlier[j : j + 1] + latter[2 * i + 1 : 2 * i + 2] * earlier[2 + j : 3 + j]

    entries = [entry(0, 0), entry(0, 1), entry(1, 0), entry(1, 1)]
    big = jnp.maximum(
        jnp.maximum(jnp.abs(entries[0]), jnp.abs(entries[1])),
        jnp.maximum(jnp.abs(entries[2]), jnp.abs(entries[3])),
    )
    rows = [part / big for part in entries]
    return jnp.concatenate(rows + [jnp.zeros((4, 128), jnp.float32)], axis=0)


def line_join(earlier, latter):
    factor = latter[LINES : LINES + 1, :]
    joined_lines = latter[:LINES] + factor * earlier[:LINES]
    joined_scale = latter[LINES:] * earlier[LINES:]
    return jnp.concatenate([joined_lines, joined_scale], axis=0)


def ratio_neutral():
    unit = jnp.ones((1, 128), jnp.float32)
    blank = jnp.zeros((1, 128), jnp.float32)
    return jnp.concatenate([unit, blank, blank, unit, blank, blank, blank, blank], axis=0)


def line_neutral():
    return jnp.concatenate([jnp.zeros((LINES, 128), jnp.float32), jnp.ones((8, 128), jnp.float32)], axis=0)


def scan_kernel(count, backward, join, neutral, x_ref, out_ref, totals, recv, send_sem, recv_sem):
    me = lax.axis_index("gy")
    row = lax.axis_index("gx")
    sign = -1 if backward else 1
    offsets = [1]
    while offsets[-1] * 2 < count:
        offsets.append(offsets[-1] * 2)
    partners = []
    for offset in offsets:
        partners.append((me + offset) % count)
        if 2 * offset != count:
            partners.append((me + count - offset) % count)
    barrier = pltpu.get_barrier_semaphore()
    for partner in partners:
        pl.semaphore_signal(barrier, inc=1, device_id=(row, partner), device_id_type=MESH)
    pl.semaphore_wait(barrier, len(partners))
    rounds = [1] + offsets
    copies = []
    for step, offset in enumerate(rounds):
        source = x_ref if step == 0 else totals.at[step - 1]
        target = (me + count + sign * offset) % count
        copy = pltpu.make_async_remote_copy(
            src_ref=source,
            dst_ref=recv.at[step],
            send_sem=send_sem.at[step],
            recv_sem=recv_sem.at[step],
            device_id=(row, target),
            device_id_type=MESH,
        )
        copy.start()
        copy.wait_recv()
        copies.append(copy)
        valid = (me + offset <= count - 1) if backward else (me >= offset)
        earlier = recv[step]
        if step == 0:
            totals[step] = jnp.where(valid, earlier, neutral())
        else:
            latter = totals[step - 1]
            totals[step] = jnp.where(valid, join(earlier, latter), latter)
    out_ref[...] = totals[len(rounds) - 1]
    for copy in copies:
        copy.wait_send()


def line_scan(step_value, backward):
    count = lax.axis_size("gy")
    factor, lines = step_value
    shape = lines.shape
    packed = jnp.concatenate(
        [lines.reshape(LINES, 128), jnp.broadcast_to(factor.reshape(1, 1), (8, 128))], axis=0
    )
    rounds = 1
    while (1 << (rounds - 1)) * 2 < count:
        rounds += 1
    rounds += 1
    result = pl.pallas_call(
        functools.partial(scan_kernel, count, backward, line_join, line_neutral),
        out_shape=jax.ShapeDtypeStruct(packed.shape, jnp.float32),
        in_specs=[pl.BlockSpec(memory_space=pltpu.VMEM)],
        out_specs=pl.BlockSpec(memory_space=pltpu.VMEM),
        scratch_shapes=[
            pltpu.VMEM((rounds,) + packed.shape, jnp.float32),
            pltpu.VMEM((rounds,) + packed.shape, jnp.float32),
            pltpu.SemaphoreType.DMA((rounds,)),
            pltpu.SemaphoreType.DMA((rounds,)),
        ],
        compiler_params=pltpu.CompilerParams(collective_id=1 if backward else 0, has_side_effects=True),
    )(packed)
    return result[:LINES].reshape(shape)


def ratio_scan(matrix):
    count = lax.axis_size("gy")
    packed = jnp.concatenate(
        [jnp.broadcast_to(matrix.reshape(4, 1), (4, 128)), jnp.zeros((4, 128), jnp.float32)], axis=0
    )
    rounds = 1
    while (1 << (rounds - 1)) * 2 < count:
        rounds += 1
    rounds += 1
    result = pl.pallas_call(
        functools.partial(scan_kernel, count, False, ratio_join, ratio_neutral),
        out_shape=jax.ShapeDtypeStruct(packed.shape, jnp.float32),
        in_specs=[pl.BlockSpec(memory_space=pltpu.VMEM)],
        out_specs=pl.BlockSpec(memory_space=pltpu.VMEM),
        scratch_shapes=[
            pltpu.VMEM((rounds,) + packed.shape, jnp.float32),
            pltpu.VMEM((rounds,) + packed.shape, jnp.float32),
            pltpu.SemaphoreType.DMA((rounds,)),
            pltpu.SemaphoreType.DMA((rounds,)),
        ],
        compiler_params=pltpu.CompilerParams(collective_id=2, has_side_effects=True),
    )(packed)
    return result[:4, 0].reshape(2, 2)


def prefix_kernel(count, group, rows_here, element_ref, table_ref, out_ref, pieces, send_sem, recv_sem, local_sem):
    mine = lax.axis_index("gy")
    row = lax.axis_index("gx")
    teams = count // group
    team = mine // group
    seat = mine % group
    barrier = pltpu.get_barrier_semaphore()
    partners = [team * group + (seat + step) % group for step in range(1, group)]
    partners += [((team + step) % teams) * group + seat for step in range(1, teams)]
    for partner in partners:
        pl.semaphore_signal(barrier, inc=1, device_id=(row, partner), device_id_type=MESH)
    pl.semaphore_wait(barrier, len(partners))

    own = pltpu.make_async_copy(element_ref, pieces.at[mine], local_sem.at[0])
    own.start()

    def mate_copy(step, source_seat, target_seat):
        return pltpu.make_async_remote_copy(
            src_ref=element_ref,
            dst_ref=pieces.at[team * group + source_seat],
            send_sem=send_sem.at[step],
            recv_sem=recv_sem.at[source_seat],
            device_id=(row, team * group + target_seat),
            device_id_type=MESH,
        )

    def team_copy(step, source_team, target_team):
        block = pieces.at[pl.ds(source_team * group, group)]
        return pltpu.make_async_remote_copy(
            src_ref=block,
            dst_ref=block,
            send_sem=send_sem.at[group + step],
            recv_sem=recv_sem.at[group + source_team],
            device_id=(row, target_team * group + seat),
            device_id_type=MESH,
        )

    for step in range(1, group):
        mate_copy(step, seat, (seat + step) % group).start()
    for step in range(1, group):
        mate_copy(step, (seat + group - step) % group, seat).wait_recv()
    own.wait()
    for step in range(1, teams):
        team_copy(step, team, (team + step) % teams).start()
    for step in range(1, teams):
        team_copy(step, (team + teams - step) % teams, team).wait_recv()

    def turn(position, total):
        piece = pieces[position]
        entries = [
            piece[2 * i : 2 * i + 1] * total[j] + piece[2 * i + 1 : 2 * i + 2] * total[2 + j]
            for i in range(2)
            for j in range(2)
        ]
        big = jnp.maximum(
            jnp.maximum(jnp.abs(entries[0]), jnp.abs(entries[1])),
            jnp.maximum(jnp.abs(entries[2]), jnp.abs(entries[3])),
        )
        inside = position < mine
        return tuple(jnp.where(inside, value / big, old) for value, old in zip(entries, total))

    unit = jnp.ones((1, 128), jnp.float32)
    blank = jnp.zeros((1, 128), jnp.float32)
    total = lax.fori_loop(0, count - 1, turn, (unit, blank, blank, unit))
    modified_prev = total[1] / total[3]
    weight = unit
    for i in range(rows_here):
        lower = table_ref[i : i + 1]
        upper = table_ref[16 + i : 17 + i]
        diagonal = table_ref[32 + i : 33 + i]
        pivot = diagonal - lower * modified_prev
        modified_prev = upper / pivot
        weight = -lower / pivot * weight
        out_ref[i : i + 1] = pivot
        out_ref[16 + i : 17 + i] = modified_prev
        out_ref[32 + i : 33 + i] = weight
    for step in range(1, group):
        mate_copy(step, seat, (seat + step) % group).wait_send()
    for step in range(1, teams):
        team_copy(step, team, (team + step) % teams).wait_send()


def team_size(count):
    if count > 8 and count % 8 == 0:
        return 8
    return max(1, count // 2)


def matrix_kernel(rows_here, table_ref, out_ref):
    unit = jnp.ones((1, 128), jnp.float32)
    blank = jnp.zeros((1, 128), jnp.float32)
    top = (unit, blank)
    bottom = (blank, unit)
    for i in range(rows_here):
        scale = 1.0 / table_ref[32 + i : 33 + i]
        up = table_ref[16 + i : 17 + i] * scale
        low = -table_ref[i : i + 1] * scale
        top, bottom = (
            (up * bottom[0], up * bottom[1]),
            (low * top[0] + bottom[0], low * top[1] + bottom[1]),
        )
    big = jnp.maximum(
        jnp.maximum(jnp.abs(top[0]), jnp.abs(top[1])), jnp.maximum(jnp.abs(bottom[0]), jnp.abs(bottom[1]))
    )
    out_ref[...] = jnp.concatenate(
        [top[0] / big, top[1] / big, bottom[0] / big, bottom[1] / big, blank, blank, blank, blank], axis=0
    )


def coefficient_table(lower_coef, upper_coef, diagonal):
    count = lax.axis_size("gy")
    rows_here = lower_coef.shape[0]
    filler = jnp.zeros((16 - rows_here,), jnp.float32)
    column = jnp.concatenate([lower_coef, filler, upper_coef, filler, diagonal, filler])
    table = jnp.broadcast_to(column.reshape(48, 1), (48, 128))
    element = pl.pallas_call(
        functools.partial(matrix_kernel, rows_here),
        out_shape=jax.ShapeDtypeStruct((8, 128), jnp.float32),
        in_specs=[pl.BlockSpec(memory_space=pltpu.VMEM)],
        out_specs=pl.BlockSpec(memory_space=pltpu.VMEM),
    )(table)
    return table, pl.pallas_call(
        functools.partial(prefix_kernel, count, team_size(count), rows_here),
        out_shape=jax.ShapeDtypeStruct((48, 128), jnp.float32),
        in_specs=[pl.BlockSpec(memory_space=pltpu.VMEM)] * 2,
        out_specs=pl.BlockSpec(memory_space=pltpu.VMEM),
        scratch_shapes=[
            pltpu.VMEM((count, 8, 128), jnp.float32),
            pltpu.SemaphoreType.DMA((team_size(count) + count // team_size(count),)),
            pltpu.SemaphoreType.DMA((team_size(count) + count // team_size(count),)),
            pltpu.SemaphoreType.DMA((1,)),
        ],
        compiler_params=pltpu.CompilerParams(collective_id=1, has_side_effects=True),
    )(element, table)


def stream_slope(padded, planes):
    summed = STENCIL[0] * (padded[..., 5 : 5 + planes] - padded[..., 3 : 3 + planes])
    for offset in range(2, 5):
        summed = summed + STENCIL[offset - 1] * (
            padded[..., 4 + offset : 4 + offset + planes]
            - padded[..., 4 - offset : 4 - offset + planes]
        )
    return summed


def roll_slope(values, along_axis):
    summed = STENCIL[0] * (jnp.roll(values, -1, along_axis) - jnp.roll(values, 1, along_axis))
    for offset in range(2, 5):
        summed = summed + STENCIL[offset - 1] * (
            jnp.roll(values, -offset, along_axis) - jnp.roll(values, offset, along_axis)
        )
    return summed


def compose(earlier, latter):
    return (latter[0] * earlier[0], latter[1] + latter[0] * earlier[1])


def chain_ratio(earlier, latter):
    product = jnp.dot(latter, earlier, precision=lax.Precision.HIGHEST)
    return product / jnp.max(jnp.abs(product))


def ratio_matrix(cross_term, top_right, bottom_left):
    unit_entry = jnp.ones((), jnp.float32)
    return jnp.stack([jnp.stack([cross_term, top_right]), jnp.stack([bottom_left, unit_entry])])


def radix_plan(count):
    plan = [list(range(1, min(4, count - 1) + 1))]
    span = len(plan[0])
    while span < count - 1:
        offsets = [span * j for j in range(1, 4) if span * j < count]
        plan.append(offsets)
        span = span * (1 + len(offsets))
    return plan


def radix_scan(me, row, count, backward, element, parts, recv, send_sem, recv_sem, base, copies):
    sign = -1 if backward else 1
    plan = radix_plan(count)
    slot = base
    for level, offsets in enumerate(plan):
        source = element if level == 0 else parts.at[level - 1]
        started = []
        for offset in offsets:
            target = (me + count + sign * offset) % count
            copy = pltpu.make_async_remote_copy(
                src_ref=source,
                dst_ref=recv.at[slot],
                send_sem=send_sem.at[slot],
                recv_sem=recv_sem.at[slot],
                device_id=(row, target),
                device_id_type=MESH,
            )
            copy.start()
            started.append((offset, slot, copy))
            slot += 1
        acc = line_neutral() if level == 0 else parts[level - 1]
        for offset, index, copy in started:
            copy.wait_recv()
            copies.append(copy)
            valid = (me + offset <= count - 1) if backward else (me >= offset)
            acc = jnp.where(valid, line_join(recv[index], acc), acc)
        parts[level] = acc
    return parts[len(plan) - 1]


def carry_kernel(count, rows_here, rows_ref, given_ref, coef_ref, out_ref, down_element, parts_down, up_element,
                 parts_up, recv, send_sem, recv_sem):
    me = lax.axis_index("gy")
    row = lax.axis_index("gx")
    plan = radix_plan(count)
    residues = set()
    for offsets in plan:
        for offset in offsets:
            residues.add(offset % count)
            residues.add((count - offset) % count)
    residues.discard(0)
    barrier = pltpu.get_barrier_semaphore()
    for residue in sorted(residues):
        pl.semaphore_signal(barrier, inc=1, device_id=(row, (me + residue) % count), device_id_type=MESH)
    pl.semaphore_wait(barrier, len(residues))
    copies = []
    slots = sum(len(offsets) for offsets in plan)

    coef = coef_ref[...]
    given = given_ref[...]
    carried = None
    for i in range(rows_here):
        lower = given[i : i + 1]
        pivot = coef[i : i + 1]
        line = rows_ref[:, i].reshape(LINES, 128)
        carried = line / pivot if carried is None else (line - lower * carried) / pivot
        out_ref[:, i] = carried.reshape(out_ref.shape[0], out_ref.shape[2], 128)
    down_element[...] = jnp.concatenate(
        [carried, jnp.broadcast_to(coef[32 + rows_here - 1 : 32 + rows_here], (8, 128))], axis=0
    )
    below_carry = radix_scan(
        me, row, count, False, down_element, parts_down, recv, send_sem, recv_sem, 0, copies
    )[:LINES]
    carried = None
    weight = None
    for i in reversed(range(rows_here)):
        sensitivity = coef[32 + i : 33 + i]
        modified = coef[16 + i : 17 + i]
        reduced = out_ref[:, i].reshape(LINES, 128) + sensitivity * below_carry
        if carried is None:
            carried = reduced
            weight = -modified
        else:
            carried = reduced - modified * carried
            weight = -modified * weight
        out_ref[:, i] = carried.reshape(out_ref.shape[0], out_ref.shape[2], 128)
    up_element[...] = jnp.concatenate([carried, jnp.broadcast_to(weight, (8, 128))], axis=0)
    above_carry = radix_scan(
        me, row, count, True, up_element, parts_up, recv, send_sem, recv_sem, slots, copies
    )[:LINES]
    weight = None
    for i in reversed(range(rows_here)):
        modified = coef[16 + i : 17 + i]
        weight = -modified if weight is None else -modified * weight
        value = out_ref[:, i].reshape(LINES, 128) + weight * above_carry
        out_ref[:, i] = value.reshape(out_ref.shape[0], out_ref.shape[2], 128)
    for copy in copies:
        copy.wait_send()


def carry_solve(stacked, given, coef):
    count = lax.axis_size("gy")
    rows_here = stacked.shape[1]
    plan = radix_plan(count)
    slots = 2 * sum(len(offsets) for offsets in plan)
    big = (LINES + 8, 128)
    return pl.pallas_call(
        functools.partial(carry_kernel, count, rows_here),
        out_shape=jax.ShapeDtypeStruct(stacked.shape, jnp.float32),
        in_specs=[pl.BlockSpec(memory_space=pltpu.VMEM)] * 3,
        out_specs=pl.BlockSpec(memory_space=pltpu.VMEM),
        scratch_shapes=[
            pltpu.VMEM(big, jnp.float32),
            pltpu.VMEM((len(plan),) + big, jnp.float32),
            pltpu.VMEM(big, jnp.float32),
            pltpu.VMEM((len(plan),) + big, jnp.float32),
            pltpu.VMEM((slots,) + big, jnp.float32),
            pltpu.SemaphoreType.DMA((slots,)),
            pltpu.SemaphoreType.DMA((slots,)),
        ],
        compiler_params=pltpu.CompilerParams(collective_id=0, has_side_effects=True),
    )(stacked, given, coef)


def shards(velocity, old_advection, lower_gap, upper_gap):
    planes = velocity.shape[3]
    padded = extended(velocity, (("gx", 3),), 4, True)
    stream = stream_slope(padded, planes)
    spanwise = roll_slope(velocity, 2)
    rimmed = extended(velocity, (("gy", 1),), 1, False)
    gap_sum = lower_gap + upper_gap
    normal_slope = (rimmed[:, 2:] - rimmed[:, :-2]) / gap_sum[None, :, None, None]
    advection = -(
        velocity[0][None] * stream + velocity[1][None] * normal_slope + velocity[2][None] * spanwise
    )
    forcing = velocity + GAMMA * advection + ZETA * old_advection
    lower_coef = -2.0 * STIFF / (gap_sum * lower_gap)
    upper_coef = -2.0 * STIFF / (gap_sum * upper_gap)
    diagonal = 1.0 - lower_coef - upper_coef
    rows_here = velocity.shape[1]

    given, table = coefficient_table(lower_coef, upper_coef, diagonal)
    finished = carry_solve(forcing, given, table)
    return (finished.reshape(velocity.shape), advection)


def solution(mesh):
    return jax.shard_map(
        shards,
        mesh=mesh,
        in_specs=(P(None, "gy", None, "gx"), P(None, "gy", None, "gx"), P("gy"), P("gy")),
        out_specs=(P(None, "gy", None, "gx"), P(None, "gy", None, "gx")),
        check_vma=False,
    )
```

```python
import functools

import jax
import jax.numpy as jnp
from jax import lax
from jax.sharding import PartitionSpec as P
from jax.experimental import pallas as pl
from jax.experimental.pallas import tpu as pltpu

MESH = pl.DeviceIdType.MESH
LINES = 96

STIFF = 1024


STENCIL = (0.8, -0.2, 4.0 / 105.0, -1.0 / 280.0)
GAMMA = 5.0 / 12.0
ZETA = -17.0 / 60.0


def extended(array, sides, width, wrap):
    for axis, dim in sides:
        size, length = (lax.axis_size(axis), array.shape[dim])
        up = [(i, (i + 1) % size) for i in range(size if wrap else size - 1)]
        down = [(j, i) for i, j in up]
        last = lax.slice_in_dim(array, length - width, length, axis=dim)
        first = lax.slice_in_dim(array, 0, width, axis=dim)
        before = lax.ppermute(last, axis, up)
        after = lax.ppermute(first, axis, down)
        array = jnp.concatenate([before, array, after], axis=dim)
    return array


def prefix(value, axis, join, neutral, backward):
    count, mine = (lax.axis_size(axis), lax.axis_index(axis))
    step = -1 if backward else 1
    order = [(i, i + step) for i in range(count) if 0 <= i + step < count]
    total = jax.tree.map(lambda part: lax.ppermute(part, axis, order), value)
    inside = (mine >= 1) if not backward else (mine <= count - 2)
    total = jax.tree.map(
        lambda part, zero: jnp.where(inside, part, jnp.full_like(part, 0) + jnp.asarray(zero, part.dtype)),
        total,
        neutral,
    )
    offset = 1
    while offset < count:
        pairs = [(i, i + step * offset) for i in range(count) if 0 <= i + step * offset < count]
        earlier = jax.tree.map(lambda part: lax.ppermute(part, axis, pairs), total)
        longer = join(earlier, total)
        reach = (mine >= offset) if not backward else (mine <= count - 1 - offset)
        total = jax.tree.map(lambda new, old: jnp.where(reach, new, old), longer, total)
        offset *= 2
    return total


def ratio_join(earlier, latter):
    def entry(i, j):
        return latter[2 * i : 2 * i + 1] * earlier[j : j + 1] + latter[2 * i + 1 : 2 * i + 2] * earlier[2 + j : 3 + j]

    entries = [entry(0, 0), entry(0, 1), entry(1, 0), entry(1, 1)]
    big = jnp.maximum(
        jnp.maximum(jnp.abs(entries[0]), jnp.abs(entries[1])),
        jnp.maximum(jnp.abs(entries[2]), jnp.abs(entries[3])),
    )
    rows = [part / big for part in entries]
    return jnp.concatenate(rows + [jnp.zeros((4, 128), jnp.float32)], axis=0)


def line_join(earlier, latter):
    factor = latter[LINES : LINES + 1, :]
    joined_lines = latter[:LINES] + factor * earlier[:LINES]
    joined_scale = latter[LINES:] * earlier[LINES:]
    return jnp.concatenate([joined_lines, joined_scale], axis=0)


def ratio_neutral():
    unit = jnp.ones((1, 128), jnp.float32)
    blank = jnp.zeros((1, 128), jnp.float32)
    return jnp.concatenate([unit, blank, blank, unit, blank, blank, blank, blank], axis=0)


def line_neutral():
    return jnp.concatenate([jnp.zeros((LINES, 128), jnp.float32), jnp.ones((8, 128), jnp.float32)], axis=0)


def scan_kernel(count, backward, join, neutral, x_ref, out_ref, totals, recv, send_sem, recv_sem):
    me = lax.axis_index("gy")
    row = lax.axis_index("gx")
    sign = -1 if backward else 1
    offsets = [1]
    while offsets[-1] * 2 < count:
        offsets.append(offsets[-1] * 2)
    partners = []
    for offset in offsets:
        partners.append((me + offset) % count)
        if 2 * offset != count:
            partners.append((me + count - offset) % count)
    barrier = pltpu.get_barrier_semaphore()
    for partner in partners:
        pl.semaphore_signal(barrier, inc=1, device_id=(row, partner), device_id_type=MESH)
    pl.semaphore_wait(barrier, len(partners))
    rounds = [1] + offsets
    copies = []
    for step, offset in enumerate(rounds):
        source = x_ref if step == 0 else totals.at[step - 1]
        target = (me + count + sign * offset) % count
        copy = pltpu.make_async_remote_copy(
            src_ref=source,
            dst_ref=recv.at[step],
            send_sem=send_sem.at[step],
            recv_sem=recv_sem.at[step],
            device_id=(row, target),
            device_id_type=MESH,
        )
        copy.start()
        copy.wait_recv()
        copies.append(copy)
        valid = (me + offset <= count - 1) if backward else (me >= offset)
        earlier = recv[step]
        if step == 0:
            totals[step] = jnp.where(valid, earlier, neutral())
        else:
            latter = totals[step - 1]
            totals[step] = jnp.where(valid, join(earlier, latter), latter)
    out_ref[...] = totals[len(rounds) - 1]
    for copy in copies:
        copy.wait_send()


def line_scan(step_value, backward):
    count = lax.axis_size("gy")
    factor, lines = step_value
    shape = lines.shape
    packed = jnp.concatenate(
        [lines.reshape(LINES, 128), jnp.broadcast_to(factor.reshape(1, 1), (8, 128))], axis=0
    )
    rounds = 1
    while (1 << (rounds - 1)) * 2 < count:
        rounds += 1
    rounds += 1
    result = pl.pallas_call(
        functools.partial(scan_kernel, count, backward, line_join, line_neutral),
        out_shape=jax.ShapeDtypeStruct(packed.shape, jnp.float32),
        in_specs=[pl.BlockSpec(memory_space=pltpu.VMEM)],
        out_specs=pl.BlockSpec(memory_space=pltpu.VMEM),
        scratch_shapes=[
            pltpu.VMEM((rounds,) + packed.shape, jnp.float32),
            pltpu.VMEM((rounds,) + packed.shape, jnp.float32),
            pltpu.SemaphoreType.DMA((rounds,)),
            pltpu.SemaphoreType.DMA((rounds,)),
        ],
        compiler_params=pltpu.CompilerParams(collective_id=1 if backward else 0, has_side_effects=True),
    )(packed)
    return result[:LINES].reshape(shape)


def ratio_scan(matrix):
    count = lax.axis_size("gy")
    packed = jnp.concatenate(
        [jnp.broadcast_to(matrix.reshape(4, 1), (4, 128)), jnp.zeros((4, 128), jnp.float32)], axis=0
    )
    rounds = 1
    while (1 << (rounds - 1)) * 2 < count:
        rounds += 1
    rounds += 1
    result = pl.pallas_call(
        functools.partial(scan_kernel, count, False, ratio_join, ratio_neutral),
        out_shape=jax.ShapeDtypeStruct(packed.shape, jnp.float32),
        in_specs=[pl.BlockSpec(memory_space=pltpu.VMEM)],
        out_specs=pl.BlockSpec(memory_space=pltpu.VMEM),
        scratch_shapes=[
            pltpu.VMEM((rounds,) + packed.shape, jnp.float32),
            pltpu.VMEM((rounds,) + packed.shape, jnp.float32),
            pltpu.SemaphoreType.DMA((rounds,)),
            pltpu.SemaphoreType.DMA((rounds,)),
        ],
        compiler_params=pltpu.CompilerParams(collective_id=2, has_side_effects=True),
    )(packed)
    return result[:4, 0].reshape(2, 2)


def prefix_kernel(count, group, rows_here, element_ref, table_ref, out_ref, pieces, send_sem, recv_sem, local_sem):
    mine = lax.axis_index("gy")
    row = lax.axis_index("gx")
    teams = count // group
    team = mine // group
    seat = mine % group
    barrier = pltpu.get_barrier_semaphore()
    partners = [team * group + (seat + step) % group for step in range(1, group)]
    partners += [((team + step) % teams) * group + seat for step in range(1, teams)]
    for partner in partners:
        pl.semaphore_signal(barrier, inc=1, device_id=(row, partner), device_id_type=MESH)
    pl.semaphore_wait(barrier, len(partners))

    own = pltpu.make_async_copy(element_ref, pieces.at[mine], local_sem.at[0])
    own.start()

    def mate_copy(step, source_seat, target_seat):
        return pltpu.make_async_remote_copy(
            src_ref=element_ref,
            dst_ref=pieces.at[team * group + source_seat],
            send_sem=send_sem.at[step],
            recv_sem=recv_sem.at[source_seat],
            device_id=(row, team * group + target_seat),
            device_id_type=MESH,
        )

    def team_copy(step, source_team, target_team):
        block = pieces.at[pl.ds(source_team * group, group)]
        return pltpu.make_async_remote_copy(
            src_ref=block,
            dst_ref=block,
            send_sem=send_sem.at[group + step],
            recv_sem=recv_sem.at[group + source_team],
            device_id=(row, target_team * group + seat),
            device_id_type=MESH,
        )

    for step in range(1, group):
        mate_copy(step, seat, (seat + step) % group).start()
    for step in range(1, group):
        mate_copy(step, (seat + group - step) % group, seat).wait_recv()
    own.wait()
    for step in range(1, teams):
        team_copy(step, team, (team + step) % teams).start()
    for step in range(1, teams):
        team_copy(step, (team + teams - step) % teams, team).wait_recv()

    def turn(position, total):
        piece = pieces[position]
        entries = [
            piece[2 * i : 2 * i + 1] * total[j] + piece[2 * i + 1 : 2 * i + 2] * total[2 + j]
            for i in range(2)
            for j in range(2)
        ]
        big = jnp.maximum(
            jnp.maximum(jnp.abs(entries[0]), jnp.abs(entries[1])),
            jnp.maximum(jnp.abs(entries[2]), jnp.abs(entries[3])),
        )
        inside = position < mine
        return tuple(jnp.where(inside, value / big, old) for value, old in zip(entries, total))

    unit = jnp.ones((1, 128), jnp.float32)
    blank = jnp.zeros((1, 128), jnp.float32)
    total = lax.fori_loop(0, count - 1, turn, (unit, blank, blank, unit))
    modified_prev = total[1] / total[3]
    weight = unit
    for i in range(rows_here):
        lower = table_ref[i : i + 1]
        upper = table_ref[16 + i : 17 + i]
        diagonal = table_ref[32 + i : 33 + i]
        pivot = diagonal - lower * modified_prev
        modified_prev = upper / pivot
        weight = -lower / pivot * weight
        out_ref[i : i + 1] = pivot
        out_ref[16 + i : 17 + i] = modified_prev
        out_ref[32 + i : 33 + i] = weight
    for step in range(1, group):
        mate_copy(step, seat, (seat + step) % group).wait_send()
    for step in range(1, teams):
        team_copy(step, team, (team + step) % teams).wait_send()


def team_size(count):
    if count > 16 and count % 16 == 0:
        return 16
    return max(1, count // 2)


def matrix_kernel(rows_here, table_ref, out_ref):
    unit = jnp.ones((1, 128), jnp.float32)
    blank = jnp.zeros((1, 128), jnp.float32)
    top = (unit, blank)
    bottom = (blank, unit)
    for i in range(rows_here):
        scale = 1.0 / table_ref[32 + i : 33 + i]
        up = table_ref[16 + i : 17 + i] * scale
        low = -table_ref[i : i + 1] * scale
        top, bottom = (
            (up * bottom[0], up * bottom[1]),
            (low * top[0] + bottom[0], low * top[1] + bottom[1]),
        )
    big = jnp.maximum(
        jnp.maximum(jnp.abs(top[0]), jnp.abs(top[1])), jnp.maximum(jnp.abs(bottom[0]), jnp.abs(bottom[1]))
    )
    out_ref[...] = jnp.concatenate(
        [top[0] / big, top[1] / big, bottom[0] / big, bottom[1] / big, blank, blank, blank, blank], axis=0
    )


def coefficient_table(lower_coef, upper_coef, diagonal):
    count = lax.axis_size("gy")
    rows_here = lower_coef.shape[0]
    filler = jnp.zeros((16 - rows_here,), jnp.float32)
    column = jnp.concatenate([lower_coef, filler, upper_coef, filler, diagonal, filler])
    table = jnp.broadcast_to(column.reshape(48, 1), (48, 128))
    element = pl.pallas_call(
        functools.partial(matrix_kernel, rows_here),
        out_shape=jax.ShapeDtypeStruct((8, 128), jnp.float32),
        in_specs=[pl.BlockSpec(memory_space=pltpu.VMEM)],
        out_specs=pl.BlockSpec(memory_space=pltpu.VMEM),
    )(table)
    return table, pl.pallas_call(
        functools.partial(prefix_kernel, count, team_size(count), rows_here),
        out_shape=jax.ShapeDtypeStruct((48, 128), jnp.float32),
        in_specs=[pl.BlockSpec(memory_space=pltpu.VMEM)] * 2,
        out_specs=pl.BlockSpec(memory_space=pltpu.VMEM),
        scratch_shapes=[
            pltpu.VMEM((count, 8, 128), jnp.float32),
            pltpu.SemaphoreType.DMA((team_size(count) + count // team_size(count),)),
            pltpu.SemaphoreType.DMA((team_size(count) + count // team_size(count),)),
            pltpu.SemaphoreType.DMA((1,)),
        ],
        compiler_params=pltpu.CompilerParams(collective_id=1, has_side_effects=True),
    )(element, table)


def stream_slope(padded, planes):
    summed = STENCIL[0] * (padded[..., 5 : 5 + planes] - padded[..., 3 : 3 + planes])
    for offset in range(2, 5):
        summed = summed + STENCIL[offset - 1] * (
            padded[..., 4 + offset : 4 + offset + planes]
            - padded[..., 4 - offset : 4 - offset + planes]
        )
    return summed


def roll_slope(values, along_axis):
    summed = STENCIL[0] * (jnp.roll(values, -1, along_axis) - jnp.roll(values, 1, along_axis))
    for offset in range(2, 5):
        summed = summed + STENCIL[offset - 1] * (
            jnp.roll(values, -offset, along_axis) - jnp.roll(values, offset, along_axis)
        )
    return summed


def compose(earlier, latter):
    return (latter[0] * earlier[0], latter[1] + latter[0] * earlier[1])


def chain_ratio(earlier, latter):
    product = jnp.dot(latter, earlier, precision=lax.Precision.HIGHEST)
    return product / jnp.max(jnp.abs(product))


def ratio_matrix(cross_term, top_right, bottom_left):
    unit_entry = jnp.ones((), jnp.float32)
    return jnp.stack([jnp.stack([cross_term, top_right]), jnp.stack([bottom_left, unit_entry])])


def radix_plan(count):
    plan = [list(range(1, min(3, count - 1) + 1))]
    span = len(plan[0])
    while span < count - 1:
        offsets = [span * j for j in range(1, 3) if span * j < count]
        plan.append(offsets)
        span = span * (1 + len(offsets))
    return plan


def radix_scan(me, row, count, backward, element, parts, recv, send_sem, recv_sem, base, copies):
    sign = -1 if backward else 1
    plan = radix_plan(count)
    slot = base
    for level, offsets in enumerate(plan):
        source = element if level == 0 else parts.at[level - 1]
        started = []
        for offset in offsets:
            target = (me + count + sign * offset) % count
            copy = pltpu.make_async_remote_copy(
                src_ref=source,
                dst_ref=recv.at[slot],
                send_sem=send_sem.at[slot],
                recv_sem=recv_sem.at[slot],
                device_id=(row, target),
                device_id_type=MESH,
            )
            copy.start()
            started.append((offset, slot, copy))
            slot += 1
        acc = line_neutral() if level == 0 else parts[level - 1]
        for offset, index, copy in started:
            copy.wait_recv()
            copies.append(copy)
            valid = (me + offset <= count - 1) if backward else (me >= offset)
            acc = jnp.where(valid, line_join(recv[index], acc), acc)
        parts[level] = acc
    return parts[len(plan) - 1]


def carry_kernel(count, rows_here, rows_ref, given_ref, coef_ref, out_ref, down_element, parts_down, up_element,
                 parts_up, recv, send_sem, recv_sem):
    me = lax.axis_index("gy")
    row = lax.axis_index("gx")
    plan = radix_plan(count)
    residues = set()
    for offsets in plan:
        for offset in offsets:
            residues.add(offset % count)
            residues.add((count - offset) % count)
    residues.discard(0)
    barrier = pltpu.get_barrier_semaphore()
    for residue in sorted(residues):
        pl.semaphore_signal(barrier, inc=1, device_id=(row, (me + residue) % count), device_id_type=MESH)
    pl.semaphore_wait(barrier, len(residues))
    copies = []
    slots = sum(len(offsets) for offsets in plan)

    coef = coef_ref[...]
    given = given_ref[...]
    carried = None
    for i in range(rows_here):
        lower = given[i : i + 1]
        pivot = coef[i : i + 1]
        line = rows_ref[:, i].reshape(LINES, 128)
        carried = line / pivot if carried is None else (line - lower * carried) / pivot
        out_ref[:, i] = carried.reshape(out_ref.shape[0], out_ref.shape[2], 128)
    down_element[...] = jnp.concatenate(
        [carried, jnp.broadcast_to(coef[32 + rows_here - 1 : 32 + rows_here], (8, 128))], axis=0
    )
    below_carry = radix_scan(
        me, row, count, False, down_element, parts_down, recv, send_sem, recv_sem, 0, copies
    )[:LINES]
    carried = None
    weight = None
    for i in reversed(range(rows_here)):
        sensitivity = coef[32 + i : 33 + i]
        modified = coef[16 + i : 17 + i]
        reduced = out_ref[:, i].reshape(LINES, 128) + sensitivity * below_carry
        if carried is None:
            carried = reduced
            weight = -modified
        else:
            carried = reduced - modified * carried
            weight = -modified * weight
        out_ref[:, i] = carried.reshape(out_ref.shape[0], out_ref.shape[2], 128)
    up_element[...] = jnp.concatenate([carried, jnp.broadcast_to(weight, (8, 128))], axis=0)
    above_carry = radix_scan(
        me, row, count, True, up_element, parts_up, recv, send_sem, recv_sem, slots, copies
    )[:LINES]
    weight = None
    for i in reversed(range(rows_here)):
        modified = coef[16 + i : 17 + i]
        weight = -modified if weight is None else -modified * weight
        value = out_ref[:, i].reshape(LINES, 128) + weight * above_carry
        out_ref[:, i] = value.reshape(out_ref.shape[0], out_ref.shape[2], 128)
    for copy in copies:
        copy.wait_send()


def carry_solve(stacked, given, coef):
    count = lax.axis_size("gy")
    rows_here = stacked.shape[1]
    plan = radix_plan(count)
    slots = 2 * sum(len(offsets) for offsets in plan)
    big = (LINES + 8, 128)
    return pl.pallas_call(
        functools.partial(carry_kernel, count, rows_here),
        out_shape=jax.ShapeDtypeStruct(stacked.shape, jnp.float32),
        in_specs=[pl.BlockSpec(memory_space=pltpu.VMEM)] * 3,
        out_specs=pl.BlockSpec(memory_space=pltpu.VMEM),
        scratch_shapes=[
            pltpu.VMEM(big, jnp.float32),
            pltpu.VMEM((len(plan),) + big, jnp.float32),
            pltpu.VMEM(big, jnp.float32),
            pltpu.VMEM((len(plan),) + big, jnp.float32),
            pltpu.VMEM((slots,) + big, jnp.float32),
            pltpu.SemaphoreType.DMA((slots,)),
            pltpu.SemaphoreType.DMA((slots,)),
        ],
        compiler_params=pltpu.CompilerParams(collective_id=0, has_side_effects=True),
    )(stacked, given, coef)


def shards(velocity, old_advection, lower_gap, upper_gap):
    planes = velocity.shape[3]
    padded = extended(velocity, (("gx", 3),), 4, True)
    stream = stream_slope(padded, planes)
    spanwise = roll_slope(velocity, 2)
    rimmed = extended(velocity, (("gy", 1),), 1, False)
    gap_sum = lower_gap + upper_gap
    normal_slope = (rimmed[:, 2:] - rimmed[:, :-2]) / gap_sum[None, :, None, None]
    advection = -(
        velocity[0][None] * stream + velocity[1][None] * normal_slope + velocity[2][None] * spanwise
    )
    forcing = velocity + GAMMA * advection + ZETA * old_advection
    lower_coef = -2.0 * STIFF / (gap_sum * lower_gap)
    upper_coef = -2.0 * STIFF / (gap_sum * upper_gap)
    diagonal = 1.0 - lower_coef - upper_coef
    rows_here = velocity.shape[1]

    given, table = coefficient_table(lower_coef, upper_coef, diagonal)
    finished = carry_solve(forcing, given, table)
    return (finished.reshape(velocity.shape), advection)


def solution(mesh):
    return jax.shard_map(
        shards,
        mesh=mesh,
        in_specs=(P(None, "gy", None, "gx"), P(None, "gy", None, "gx"), P("gy"), P("gy")),
        out_specs=(P(None, "gy", None, "gx"), P(None, "gy", None, "gx")),
        check_vma=False,
    )
```

```python
import functools

import jax
import jax.numpy as jnp
from jax import lax
from jax.sharding import PartitionSpec as P
from jax.experimental import pallas as pl
from jax.experimental.pallas import tpu as pltpu

MESH = pl.DeviceIdType.MESH
LINES = 96

STIFF = 1024


STENCIL = (0.8, -0.2, 4.0 / 105.0, -1.0 / 280.0)
GAMMA = 5.0 / 12.0
ZETA = -17.0 / 60.0


def extended(array, sides, width, wrap):
    for axis, dim in sides:
        size, length = (lax.axis_size(axis), array.shape[dim])
        up = [(i, (i + 1) % size) for i in range(size if wrap else size - 1)]
        down = [(j, i) for i, j in up]
        last = lax.slice_in_dim(array, length - width, length, axis=dim)
        first = lax.slice_in_dim(array, 0, width, axis=dim)
        before = lax.ppermute(last, axis, up)
        after = lax.ppermute(first, axis, down)
        array = jnp.concatenate([before, array, after], axis=dim)
    return array


def prefix(value, axis, join, neutral, backward):
    count, mine = (lax.axis_size(axis), lax.axis_index(axis))
    step = -1 if backward else 1
    order = [(i, i + step) for i in range(count) if 0 <= i + step < count]
    total = jax.tree.map(lambda part: lax.ppermute(part, axis, order), value)
    inside = (mine >= 1) if not backward else (mine <= count - 2)
    total = jax.tree.map(
        lambda part, zero: jnp.where(inside, part, jnp.full_like(part, 0) + jnp.asarray(zero, part.dtype)),
        total,
        neutral,
    )
    offset = 1
    while offset < count:
        pairs = [(i, i + step * offset) for i in range(count) if 0 <= i + step * offset < count]
        earlier = jax.tree.map(lambda part: lax.ppermute(part, axis, pairs), total)
        longer = join(earlier, total)
        reach = (mine >= offset) if not backward else (mine <= count - 1 - offset)
        total = jax.tree.map(lambda new, old: jnp.where(reach, new, old), longer, total)
        offset *= 2
    return total


def ratio_join(earlier, latter):
    def entry(i, j):
        return latter[2 * i : 2 * i + 1] * earlier[j : j + 1] + latter[2 * i + 1 : 2 * i + 2] * earlier[2 + j : 3 + j]

    entries = [entry(0, 0), entry(0, 1), entry(1, 0), entry(1, 1)]
    big = jnp.maximum(
        jnp.maximum(jnp.abs(entries[0]), jnp.abs(entries[1])),
        jnp.maximum(jnp.abs(entries[2]), jnp.abs(entries[3])),
    )
    rows = [part / big for part in entries]
    return jnp.concatenate(rows + [jnp.zeros((4, 128), jnp.float32)], axis=0)


def line_join(earlier, latter):
    factor = latter[LINES : LINES + 1, :]
    joined_lines = latter[:LINES] + factor * earlier[:LINES]
    joined_scale = latter[LINES:] * earlier[LINES:]
    return jnp.concatenate([joined_lines, joined_scale], axis=0)


def ratio_neutral():
    unit = jnp.ones((1, 128), jnp.float32)
    blank = jnp.zeros((1, 128), jnp.float32)
    return jnp.concatenate([unit, blank, blank, unit, blank, blank, blank, blank], axis=0)


def line_neutral():
    return jnp.concatenate([jnp.zeros((LINES, 128), jnp.float32), jnp.ones((8, 128), jnp.float32)], axis=0)


def scan_kernel(count, backward, join, neutral, x_ref, out_ref, totals, recv, send_sem, recv_sem):
    me = lax.axis_index("gy")
    row = lax.axis_index("gx")
    sign = -1 if backward else 1
    offsets = [1]
    while offsets[-1] * 2 < count:
        offsets.append(offsets[-1] * 2)
    partners = []
    for offset in offsets:
        partners.append((me + offset) % count)
        if 2 * offset != count:
            partners.append((me + count - offset) % count)
    barrier = pltpu.get_barrier_semaphore()
    for partner in partners:
        pl.semaphore_signal(barrier, inc=1, device_id=(row, partner), device_id_type=MESH)
    pl.semaphore_wait(barrier, len(partners))
    rounds = [1] + offsets
    copies = []
    for step, offset in enumerate(rounds):
        source = x_ref if step == 0 else totals.at[step - 1]
        target = (me + count + sign * offset) % count
        copy = pltpu.make_async_remote_copy(
            src_ref=source,
            dst_ref=recv.at[step],
            send_sem=send_sem.at[step],
            recv_sem=recv_sem.at[step],
            device_id=(row, target),
            device_id_type=MESH,
        )
        copy.start()
        copy.wait_recv()
        copies.append(copy)
        valid = (me + offset <= count - 1) if backward else (me >= offset)
        earlier = recv[step]
        if step == 0:
            totals[step] = jnp.where(valid, earlier, neutral())
        else:
            latter = totals[step - 1]
            totals[step] = jnp.where(valid, join(earlier, latter), latter)
    out_ref[...] = totals[len(rounds) - 1]
    for copy in copies:
        copy.wait_send()


def line_scan(step_value, backward):
    count = lax.axis_size("gy")
    factor, lines = step_value
    shape = lines.shape
    packed = jnp.concatenate(
        [lines.reshape(LINES, 128), jnp.broadcast_to(factor.reshape(1, 1), (8, 128))], axis=0
    )
    rounds = 1
    while (1 << (rounds - 1)) * 2 < count:
        rounds += 1
    rounds += 1
    result = pl.pallas_call(
        functools.partial(scan_kernel, count, backward, line_join, line_neutral),
        out_shape=jax.ShapeDtypeStruct(packed.shape, jnp.float32),
        in_specs=[pl.BlockSpec(memory_space=pltpu.VMEM)],
        out_specs=pl.BlockSpec(memory_space=pltpu.VMEM),
        scratch_shapes=[
            pltpu.VMEM((rounds,) + packed.shape, jnp.float32),
            pltpu.VMEM((rounds,) + packed.shape, jnp.float32),
            pltpu.SemaphoreType.DMA((rounds,)),
            pltpu.SemaphoreType.DMA((rounds,)),
        ],
        compiler_params=pltpu.CompilerParams(collective_id=1 if backward else 0, has_side_effects=True),
    )(packed)
    return result[:LINES].reshape(shape)


def ratio_scan(matrix):
    count = lax.axis_size("gy")
    packed = jnp.concatenate(
        [jnp.broadcast_to(matrix.reshape(4, 1), (4, 128)), jnp.zeros((4, 128), jnp.float32)], axis=0
    )
    rounds = 1
    while (1 << (rounds - 1)) * 2 < count:
        rounds += 1
    rounds += 1
    result = pl.pallas_call(
        functools.partial(scan_kernel, count, False, ratio_join, ratio_neutral),
        out_shape=jax.ShapeDtypeStruct(packed.shape, jnp.float32),
        in_specs=[pl.BlockSpec(memory_space=pltpu.VMEM)],
        out_specs=pl.BlockSpec(memory_space=pltpu.VMEM),
        scratch_shapes=[
            pltpu.VMEM((rounds,) + packed.shape, jnp.float32),
            pltpu.VMEM((rounds,) + packed.shape, jnp.float32),
            pltpu.SemaphoreType.DMA((rounds,)),
            pltpu.SemaphoreType.DMA((rounds,)),
        ],
        compiler_params=pltpu.CompilerParams(collective_id=2, has_side_effects=True),
    )(packed)
    return result[:4, 0].reshape(2, 2)


def prefix_kernel(count, group, rows_here, element_ref, table_ref, out_ref, pieces, send_sem, recv_sem, local_sem):
    mine = lax.axis_index("gy")
    row = lax.axis_index("gx")
    teams = count // group
    team = mine // group
    seat = mine % group
    barrier = pltpu.get_barrier_semaphore()
    partners = [team * group + (seat + step) % group for step in range(1, group)]
    partners += [((team + step) % teams) * group + seat for step in range(1, teams)]
    for partner in partners:
        pl.semaphore_signal(barrier, inc=1, device_id=(row, partner), device_id_type=MESH)
    pl.semaphore_wait(barrier, len(partners))

    own = pltpu.make_async_copy(element_ref, pieces.at[mine], local_sem.at[0])
    own.start()

    def mate_copy(step, source_seat, target_seat):
        return pltpu.make_async_remote_copy(
            src_ref=element_ref,
            dst_ref=pieces.at[team * group + source_seat],
            send_sem=send_sem.at[step],
            recv_sem=recv_sem.at[source_seat],
            device_id=(row, team * group + target_seat),
            device_id_type=MESH,
        )

    def team_copy(step, source_team, target_team):
        block = pieces.at[pl.ds(source_team * group, group)]
        return pltpu.make_async_remote_copy(
            src_ref=block,
            dst_ref=block,
            send_sem=send_sem.at[group + step],
            recv_sem=recv_sem.at[group + source_team],
            device_id=(row, target_team * group + seat),
            device_id_type=MESH,
        )

    for step in range(1, group):
        mate_copy(step, seat, (seat + step) % group).start()
    for step in range(1, group):
        mate_copy(step, (seat + group - step) % group, seat).wait_recv()
    own.wait()
    for step in range(1, teams):
        team_copy(step, team, (team + step) % teams).start()
    for step in range(1, teams):
        team_copy(step, (team + teams - step) % teams, team).wait_recv()

    def turn(position, total):
        piece = pieces[position]
        entries = [
            piece[2 * i : 2 * i + 1] * total[j] + piece[2 * i + 1 : 2 * i + 2] * total[2 + j]
            for i in range(2)
            for j in range(2)
        ]
        big = jnp.maximum(
            jnp.maximum(jnp.abs(entries[0]), jnp.abs(entries[1])),
            jnp.maximum(jnp.abs(entries[2]), jnp.abs(entries[3])),
        )
        inside = position < mine
        return tuple(jnp.where(inside, value / big, old) for value, old in zip(entries, total))

    unit = jnp.ones((1, 128), jnp.float32)
    blank = jnp.zeros((1, 128), jnp.float32)
    total = lax.fori_loop(0, count - 1, turn, (unit, blank, blank, unit))
    modified_prev = total[1] / total[3]
    weight = unit
    for i in range(rows_here):
        lower = table_ref[i : i + 1]
        upper = table_ref[16 + i : 17 + i]
        diagonal = table_ref[32 + i : 33 + i]
        pivot = diagonal - lower * modified_prev
        modified_prev = upper / pivot
        weight = -lower / pivot * weight
        out_ref[i : i + 1] = pivot
        out_ref[16 + i : 17 + i] = modified_prev
        out_ref[32 + i : 33 + i] = weight
    for step in range(1, group):
        mate_copy(step, seat, (seat + step) % group).wait_send()
    for step in range(1, teams):
        team_copy(step, team, (team + step) % teams).wait_send()


def team_size(count):
    if count > 16 and count % 16 == 0:
        return 16
    return max(1, count // 2)


def matrix_kernel(rows_here, table_ref, out_ref):
    unit = jnp.ones((1, 128), jnp.float32)
    blank = jnp.zeros((1, 128), jnp.float32)
    top = (unit, blank)
    bottom = (blank, unit)
    for i in range(rows_here):
        scale = 1.0 / table_ref[32 + i : 33 + i]
        up = table_ref[16 + i : 17 + i] * scale
        low = -table_ref[i : i + 1] * scale
        top, bottom = (
            (up * bottom[0], up * bottom[1]),
            (low * top[0] + bottom[0], low * top[1] + bottom[1]),
        )
    big = jnp.maximum(
        jnp.maximum(jnp.abs(top[0]), jnp.abs(top[1])), jnp.maximum(jnp.abs(bottom[0]), jnp.abs(bottom[1]))
    )
    out_ref[...] = jnp.concatenate(
        [top[0] / big, top[1] / big, bottom[0] / big, bottom[1] / big, blank, blank, blank, blank], axis=0
    )


def coefficient_table(lower_coef, upper_coef, diagonal):
    count = lax.axis_size("gy")
    rows_here = lower_coef.shape[0]
    filler = jnp.zeros((16 - rows_here,), jnp.float32)
    column = jnp.concatenate([lower_coef, filler, upper_coef, filler, diagonal, filler])
    table = jnp.broadcast_to(column.reshape(48, 1), (48, 128))
    element = pl.pallas_call(
        functools.partial(matrix_kernel, rows_here),
        out_shape=jax.ShapeDtypeStruct((8, 128), jnp.float32),
        in_specs=[pl.BlockSpec(memory_space=pltpu.VMEM)],
        out_specs=pl.BlockSpec(memory_space=pltpu.VMEM),
    )(table)
    return table, pl.pallas_call(
        functools.partial(prefix_kernel, count, team_size(count), rows_here),
        out_shape=jax.ShapeDtypeStruct((48, 128), jnp.float32),
        in_specs=[pl.BlockSpec(memory_space=pltpu.VMEM)] * 2,
        out_specs=pl.BlockSpec(memory_space=pltpu.VMEM),
        scratch_shapes=[
            pltpu.VMEM((count, 8, 128), jnp.float32),
            pltpu.SemaphoreType.DMA((team_size(count) + count // team_size(count),)),
            pltpu.SemaphoreType.DMA((team_size(count) + count // team_size(count),)),
            pltpu.SemaphoreType.DMA((1,)),
        ],
        compiler_params=pltpu.CompilerParams(collective_id=1, has_side_effects=True),
    )(element, table)


def stream_slope(padded, planes):
    summed = STENCIL[0] * (padded[..., 5 : 5 + planes] - padded[..., 3 : 3 + planes])
    for offset in range(2, 5):
        summed = summed + STENCIL[offset - 1] * (
            padded[..., 4 + offset : 4 + offset + planes]
            - padded[..., 4 - offset : 4 - offset + planes]
        )
    return summed


def roll_slope(values, along_axis):
    summed = STENCIL[0] * (jnp.roll(values, -1, along_axis) - jnp.roll(values, 1, along_axis))
    for offset in range(2, 5):
        summed = summed + STENCIL[offset - 1] * (
            jnp.roll(values, -offset, along_axis) - jnp.roll(values, offset, along_axis)
        )
    return summed


def compose(earlier, latter):
    return (latter[0] * earlier[0], latter[1] + latter[0] * earlier[1])


def chain_ratio(earlier, latter):
    product = jnp.dot(latter, earlier, precision=lax.Precision.HIGHEST)
    return product / jnp.max(jnp.abs(product))


def ratio_matrix(cross_term, top_right, bottom_left):
    unit_entry = jnp.ones((), jnp.float32)
    return jnp.stack([jnp.stack([cross_term, top_right]), jnp.stack([bottom_left, unit_entry])])


def radix_plan(count):
    plan = [list(range(1, min(4, count - 1) + 1))]
    span = len(plan[0])
    while span < count - 1:
        offsets = [span * j for j in range(1, 2) if span * j < count]
        plan.append(offsets)
        span = span * (1 + len(offsets))
    return plan


def radix_scan(me, row, count, backward, element, parts, recv, send_sem, recv_sem, base, copies):
    sign = -1 if backward else 1
    plan = radix_plan(count)
    slot = base
    for level, offsets in enumerate(plan):
        source = element if level == 0 else parts.at[level - 1]
        started = []
        for offset in offsets:
            target = (me + count + sign * offset) % count
            copy = pltpu.make_async_remote_copy(
                src_ref=source,
                dst_ref=recv.at[slot],
                send_sem=send_sem.at[slot],
                recv_sem=recv_sem.at[slot],
                device_id=(row, target),
                device_id_type=MESH,
            )
            copy.start()
            started.append((offset, slot, copy))
            slot += 1
        acc = line_neutral() if level == 0 else parts[level - 1]
        for offset, index, copy in started:
            copy.wait_recv()
            copies.append(copy)
            valid = (me + offset <= count - 1) if backward else (me >= offset)
            acc = jnp.where(valid, line_join(recv[index], acc), acc)
        parts[level] = acc
    return parts[len(plan) - 1]


def carry_kernel(count, rows_here, rows_ref, given_ref, coef_ref, out_ref, down_element, parts_down, up_element,
                 parts_up, recv, send_sem, recv_sem):
    me = lax.axis_index("gy")
    row = lax.axis_index("gx")
    plan = radix_plan(count)
    residues = set()
    for offsets in plan:
        for offset in offsets:
            residues.add(offset % count)
            residues.add((count - offset) % count)
    residues.discard(0)
    barrier = pltpu.get_barrier_semaphore()
    for residue in sorted(residues):
        pl.semaphore_signal(barrier, inc=1, device_id=(row, (me + residue) % count), device_id_type=MESH)
    pl.semaphore_wait(barrier, len(residues))
    copies = []
    slots = sum(len(offsets) for offsets in plan)

    coef = coef_ref[...]
    given = given_ref[...]
    carried = None
    for i in range(rows_here):
        lower = given[i : i + 1]
        pivot = coef[i : i + 1]
        line = rows_ref[:, i].reshape(LINES, 128)
        carried = line / pivot if carried is None else (line - lower * carried) / pivot
        out_ref[:, i] = carried.reshape(out_ref.shape[0], out_ref.shape[2], 128)
    down_element[...] = jnp.concatenate(
        [carried, jnp.broadcast_to(coef[32 + rows_here - 1 : 32 + rows_here], (8, 128))], axis=0
    )
    below_carry = radix_scan(
        me, row, count, False, down_element, parts_down, recv, send_sem, recv_sem, 0, copies
    )[:LINES]
    carried = None
    weight = None
    for i in reversed(range(rows_here)):
        sensitivity = coef[32 + i : 33 + i]
        modified = coef[16 + i : 17 + i]
        reduced = out_ref[:, i].reshape(LINES, 128) + sensitivity * below_carry
        if carried is None:
            carried = reduced
            weight = -modified
        else:
            carried = reduced - modified * carried
            weight = -modified * weight
        out_ref[:, i] = carried.reshape(out_ref.shape[0], out_ref.shape[2], 128)
    up_element[...] = jnp.concatenate([carried, jnp.broadcast_to(weight, (8, 128))], axis=0)
    above_carry = radix_scan(
        me, row, count, True, up_element, parts_up, recv, send_sem, recv_sem, slots, copies
    )[:LINES]
    weight = None
    for i in reversed(range(rows_here)):
        modified = coef[16 + i : 17 + i]
        weight = -modified if weight is None else -modified * weight
        value = out_ref[:, i].reshape(LINES, 128) + weight * above_carry
        out_ref[:, i] = value.reshape(out_ref.shape[0], out_ref.shape[2], 128)
    for copy in copies:
        copy.wait_send()


def carry_solve(stacked, given, coef):
    count = lax.axis_size("gy")
    rows_here = stacked.shape[1]
    plan = radix_plan(count)
    slots = 2 * sum(len(offsets) for offsets in plan)
    big = (LINES + 8, 128)
    return pl.pallas_call(
        functools.partial(carry_kernel, count, rows_here),
        out_shape=jax.ShapeDtypeStruct(stacked.shape, jnp.float32),
        in_specs=[pl.BlockSpec(memory_space=pltpu.VMEM)] * 3,
        out_specs=pl.BlockSpec(memory_space=pltpu.VMEM),
        scratch_shapes=[
            pltpu.VMEM(big, jnp.float32),
            pltpu.VMEM((len(plan),) + big, jnp.float32),
            pltpu.VMEM(big, jnp.float32),
            pltpu.VMEM((len(plan),) + big, jnp.float32),
            pltpu.VMEM((slots,) + big, jnp.float32),
            pltpu.SemaphoreType.DMA((slots,)),
            pltpu.SemaphoreType.DMA((slots,)),
        ],
        compiler_params=pltpu.CompilerParams(collective_id=0, has_side_effects=True),
    )(stacked, given, coef)


def shards(velocity, old_advection, lower_gap, upper_gap):
    planes = velocity.shape[3]
    padded = extended(velocity, (("gx", 3),), 4, True)
    stream = stream_slope(padded, planes)
    spanwise = roll_slope(velocity, 2)
    rimmed = extended(velocity, (("gy", 1),), 1, False)
    gap_sum = lower_gap + upper_gap
    normal_slope = (rimmed[:, 2:] - rimmed[:, :-2]) / gap_sum[None, :, None, None]
    advection = -(
        velocity[0][None] * stream + velocity[1][None] * normal_slope + velocity[2][None] * spanwise
    )
    forcing = velocity + GAMMA * advection + ZETA * old_advection
    lower_coef = -2.0 * STIFF / (gap_sum * lower_gap)
    upper_coef = -2.0 * STIFF / (gap_sum * upper_gap)
    diagonal = 1.0 - lower_coef - upper_coef
    rows_here = velocity.shape[1]

    given, table = coefficient_table(lower_coef, upper_coef, diagonal)
    finished = carry_solve(forcing, given, table)
    return (finished.reshape(velocity.shape), advection)


def solution(mesh):
    return jax.shard_map(
        shards,
        mesh=mesh,
        in_specs=(P(None, "gy", None, "gx"), P(None, "gy", None, "gx"), P("gy"), P("gy")),
        out_specs=(P(None, "gy", None, "gx"), P(None, "gy", None, "gx")),
        check_vma=False,
    )
```
